256 devices in a mesh: gx: 8 (over y, core), gy: 16 (over x_hi, z), pa: 2 (over x_lo).
Axes of the slice: x: 4 (x_hi: 2, x_lo: 2; x = x_hi * 2 + x_lo), y: 4, z: 8, core: 2. Of those that a mesh axis runs over, the one named last changes fastest.
Arguments:
- volume: bfloat16 [4, 4096, 4096], P('pa', 'gx', 'gy'), may hold values from -6 to 6
- view_slopes: int32 [2, 16], replicated, may hold values from -14 to 14, as said below
- measured_x: float32 [16, 4, 4096], P(None, 'pa', 'gy'), may hold values from -6 to 6
- measured_y: float32 [16, 4, 4096], P(None, 'pa', 'gx'), may hold values from -6 to 6
Outputs:
- gradient: float32 [4, 4096, 4096], P('pa', 'gx', 'gy')
- residual_x: float32 [16, 4, 4096], P(None, 'pa', 'gy')
- residual_y: float32 [16, 4, 4096], P(None, 'pa', 'gx')
The draws below stay inside these ranges and needn't reach their ends.
Inputs may be any that keep to these rules, and one draw needn't show every extreme that they name: `view_slopes`: row 0 holds the near-x slopes in units of 1/512, row 1 the near-y slopes in units of 1/256; in each row both 14 and its negative occur.
All inputs are finite; a program needn't handle non-finite values.
Results may differ from the reference program's by a relative error of at most 0.0025.
Values may be sent and summed in bfloat16 or wider, within the bound.
No kernel may reach another device: no remote copies, remote signals or barrier semaphores. Data moves between devices by JAX's collectives and lax.ppermute only.
A program may use at most 128 MiB of HBM per device.

```python
import jax
import jax.numpy as jnp
from jax import lax

CX = 512
CY = 256
VIEWS = 16
SHEAR = 14
HALO = 114
NX = 4096
NY = 4096
PLANES = 4


def draw_view_slopes(key, part):
    slopes = jax.random.randint(jax.random.fold_in(key, 11), (2, VIEWS), -SHEAR, SHEAR + 1, dtype=jnp.int32)
    for family in range(2):
        ranking = jax.random.permutation(jax.random.fold_in(key, 21 + family), VIEWS)
        slopes = slopes.at[family, ranking[0]].set(SHEAR)
        slopes = slopes.at[family, ranking[1]].set(-SHEAR)
    return slopes


def block_scale(rng, extent, pieces, smallest, top_value):
    loudness, own = 1.0, jax.random.fold_in(rng, 6)
    for dim, parts in pieces:
        heights = jnp.exp(jax.random.uniform(jax.random.fold_in(own, dim), (parts,), jnp.float32, smallest / len(pieces), top_value / len(pieces)))
        loudness = loudness * jnp.repeat(heights, extent[dim] // parts).reshape([-1 if axis == dim else 1 for axis in range(len(extent))])
    return loudness


def scatter_about(stream_key, extent, scale, reach, cuts=(), kind=jnp.bfloat16):
    values = scale * jax.random.normal(stream_key, extent, jnp.float32)
    if cuts:
        values = values * block_scale(stream_key, extent, cuts, -0.22, 0.18)
    return jnp.clip(values, -reach, reach).astype(kind)


def setup_inputs(seed: int = 0) -> dict:
    key_list = jax.random.split(jax.random.key(seed), 5)
    return {
        "volume": scatter_about(key_list[0], (PLANES, NX, NY), 1.0, 6.0, ((0, 2), (1, 8), (2, 16))),
        "view_slopes": draw_view_slopes(jax.random.fold_in(key_list[4], 71), 0),
        "measured_x": scatter_about(key_list[2], (VIEWS, PLANES, NY), 1.0, 6.0, ((1, 2), (2, 16)), jnp.float32),
        "measured_y": scatter_about(key_list[3], (VIEWS, PLANES, NX), 1.0, 6.0, ((1, 2), (2, 8)), jnp.float32),
    }


def rounded(values):
    return lax.optimization_barrier(values.astype(jnp.bfloat16)).astype(jnp.float32)


def shear_weights(slopes, cells_all, cells_dev):
    positions = jnp.arange(cells_all, dtype=jnp.int32) - cells_all // 2
    product = slopes[:, None] * positions[None, :]
    shifts = jnp.floor_divide(product, cells_dev)
    fraction = (product - shifts * cells_dev).astype(jnp.float32) / cells_dev
    return shifts, rounded(1.0 - fraction), rounded(fraction)


def project(source, shifts, lower, upper):
    planes_all, sweep_count, bin_count = source.shape
    padded = jnp.pad(source, ((0, 0), (0, 0), (HALO, HALO)))

    def one_view(strip, shift, low_weight, high_weight):
        segment = lax.dynamic_slice_in_dim(strip, (shift + HALO).astype(jnp.int32), bin_count + 1, 1)
        return low_weight * segment[:, :bin_count] + high_weight * segment[:, 1:]

    def advance(totals, position):
        strip = lax.dynamic_index_in_dim(padded, position, 1, False).astype(jnp.float32)
        shift_now = lax.dynamic_index_in_dim(shifts, position, 1, False)
        low_now = lax.dynamic_index_in_dim(lower, position, 1, False)
        high_now = lax.dynamic_index_in_dim(upper, position, 1, False)
        terms = jax.vmap(one_view, in_axes=(None, 0, 0, 0))(strip, shift_now, low_now, high_now)
        return totals + terms, None

    start = jnp.zeros((shifts.shape[0], planes_all, bin_count), jnp.float32)
    totals, unused = lax.scan(advance, start, jnp.arange(sweep_count, dtype=jnp.int32))
    return totals


def backproject(residual, shifts, lower, upper):
    view_count, planes_all, bin_count = residual.shape
    sweep_count = shifts.shape[1]
    padded = jnp.pad(residual, ((0, 0), (0, 0), (HALO, HALO)))

    def one_view(strip, shift, low_weight, high_weight):
        segment = lax.dynamic_slice_in_dim(strip, (HALO - shift - 1).astype(jnp.int32), bin_count + 1, 1)
        return low_weight * segment[:, 1:] + high_weight * segment[:, :bin_count]

    def advance(dummy, position):
        shift_now = lax.dynamic_index_in_dim(shifts, position, 1, False)
        low_now = lax.dynamic_index_in_dim(lower, position, 1, False)
        high_now = lax.dynamic_index_in_dim(upper, position, 1, False)
        terms = jax.vmap(one_view, in_axes=(0, 0, 0, 0))(padded, shift_now, low_now, high_now)
        return dummy, jnp.sum(terms, axis=0)

    dummy, stacked = lax.scan(advance, jnp.zeros((), jnp.float32), jnp.arange(sweep_count, dtype=jnp.int32))
    return jnp.moveaxis(stacked, 0, 1)


def reference(volume, view_slopes, measured_x, measured_y):
    shift_x, lower_x, upper_x = shear_weights(view_slopes[0], NX, CX)
    shift_y, lower_y, upper_y = shear_weights(view_slopes[1], NY, CY)
    scale_x = float(NX) ** -0.5
    scale_y = float(NY) ** -0.5
    forward_x = project(volume, shift_x, lower_x, upper_x) * scale_x
    forward_y = project(jnp.swapaxes(volume, 1, 2), shift_y, lower_y, upper_y) * scale_y
    residual_x = forward_x - measured_x
    residual_y = forward_y - measured_y
    back_x = backproject(rounded(residual_x), shift_x, lower_x, upper_x) * scale_x
    back_y = jnp.swapaxes(backproject(rounded(residual_y), shift_y, lower_y, upper_y), 1, 2) * scale_y
    values = volume.astype(jnp.float32)
    stacked = jnp.pad(values, ((1, 1), (0, 0), (0, 0)))
    coupling = 0.02 * (2.0 * values - stacked[:-2] - stacked[2:])
    gradient = back_x + back_y + coupling
    return gradient, residual_x, residual_y
```

```python
import jax
import jax.numpy as jnp
from jax import lax
from jax.experimental import pallas as pl
from jax.experimental.pallas import tpu as pltpu
from jax.sharding import PartitionSpec as P

LEVELS = 16
F32 = jnp.float32
BF16 = jnp.bfloat16


def interpreted():
    return False


def fill(slopes_ref, family, shape, dim):
    views = slopes_ref.shape[1]
    view = lax.broadcasted_iota(jnp.int32, shape, dim) % views
    slopes = jnp.zeros(shape, jnp.int32)
    for v in range(views):
        slopes = jnp.where(view == v, slopes_ref[family, v], slopes)
    return slopes


def lowest_shift(slopes, block, blocks):
    return slopes * (block - blocks // 2) + jnp.minimum(slopes, 0)


def barrel(value, amounts, bits):
    for bit in range(bits):
        taken = ((amounts >> bit) & 1) == 1
        value = jnp.where(taken, pltpu.roll(value, 1 << bit, 1), value)
    return value


def offsets(slopes_ref, family, block, blocks, cells):
    views = slopes_ref.shape[1]
    slopes = fill(slopes_ref, family, (views, cells), 0)
    cell = lax.broadcasted_iota(jnp.int32, (views, cells), 1) + (block * cells - blocks * cells // 2)
    lowest = lowest_shift(slopes, block, blocks)
    return (slopes * cell - lowest * cells).astype(F32) * (1.0 / cells)


def hat(offset, level):
    return jnp.maximum(1.0 - jnp.abs(offset - level), 0.0)


def forward_kernel(slopes_ref, block_ref, volume_ref, measured_ref, out_ref, table_ref, rows_ref, *, family, blocks, pad, scale):
    views = slopes_ref.shape[1]
    planes = volume_ref.shape[0]
    bins = volume_ref.shape[2 - family]
    cells = volume_ref.shape[1 + family]
    width = out_ref.shape[1]
    block = block_ref[0]
    first = (block == 0).astype(F32)
    offset = offsets(slopes_ref, family, block, blocks, cells)
    for level in range(LEVELS):
        table_ref[level * views : (level + 1) * views, :] = hat(offset, float(LEVELS - 1 - level)).astype(BF16)
    for plane in range(planes):
        for v in range(views):
            rows_ref[plane * views + v : plane * views + v + 1, :] = measured_ref[v, plane : plane + 1, :]
    slopes = fill(slopes_ref, family, (views, width), 0)
    amounts = pad - LEVELS + 1 - lowest_shift(slopes, block, blocks)
    bits = max(1, (2 * pad).bit_length() - 1)
    empty = jnp.zeros((views, width - bins), F32)
    for plane in range(planes):
        dims = (((1,), (family,)), ((), ()))
        summands = lax.dot_general(table_ref[...], volume_ref[plane], dims, preferred_element_type=F32)
        total = None
        for level in reversed(range(LEVELS)):
            piece = jnp.concatenate([summands[level * views : (level + 1) * views, :], empty], axis=1)
            total = piece if total is None else pltpu.roll(total, 1, 1) + piece
        total = barrel(total, amounts, bits) * scale
        known = jnp.concatenate([rows_ref[plane * views : (plane + 1) * views, :], empty], axis=1)
        known = pltpu.roll(known, pad, 1)
        out_ref[plane * views : (plane + 1) * views, :] = total - known * first


def forward(slopes, block, volume, measured, family, blocks, pad, scale):
    views, planes, bins = measured.shape
    width = bins + 2 * pad
    cells = volume.shape[1 + family]

    def body(*refs):
        forward_kernel(*refs, family=family, blocks=blocks, pad=pad, scale=scale)

    smem = pl.BlockSpec(memory_space=pltpu.SMEM)
    vmem = pl.BlockSpec(memory_space=pltpu.VMEM)
    return pl.pallas_call(
        body,
        out_shape=jax.ShapeDtypeStruct((planes * views, width), F32),
        in_specs=[smem, smem, vmem, vmem],
        out_specs=vmem,
        scratch_shapes=[pltpu.VMEM((LEVELS * views, cells), BF16), pltpu.VMEM((planes * views, bins), F32)],
        interpret=interpreted(),
        name="forward_" + "xy"[family],
    )(slopes, block, volume, measured)


def spread_into(residual_ref, plane, slopes_ref, family, block, blocks, other, others, pad, spread_ref):
    views = slopes_ref.shape[1]
    width = residual_ref.shape[1]
    bins = width - 2 * pad
    slopes = fill(slopes_ref, family, (views, width), 0)
    bits = max(1, (2 * pad).bit_length() - 1)
    place = lax.broadcasted_iota(jnp.int32, (views, width), 1)
    inside = (place >= jnp.where(other == 0, pad, 0)) & (place < jnp.where(other == others - 1, pad + bins, width))
    value = residual_ref[plane * views : (plane + 1) * views, :]
    value = jnp.where(inside, value, 0.0).astype(BF16).astype(F32)
    amounts = lowest_shift(slopes, block, blocks) + pad
    value = pltpu.roll(barrel(value, amounts, bits), width - 2 * pad, 1)
    for level in range(LEVELS):
        spread_ref[level * views : (level + 1) * views, :] = value[:, :bins].astype(BF16)
        value = pltpu.roll(value, 1, 1)


def split_rows(residual_ref, out_ref, rows_ref, pad):
    views, planes, bins = out_ref.shape
    width = residual_ref.shape[1]
    for plane in range(planes):
        value = residual_ref[plane * views : (plane + 1) * views, :]
        rows_ref[plane * views : (plane + 1) * views, :] = pltpu.roll(value, width - pad, 1)[:, :bins]
    for plane in range(planes):
        for v in range(views):
            out_ref[v, plane : plane + 1, :] = rows_ref[plane * views + v : plane * views + v + 1, :]


def back_x_kernel(slopes_ref, blocks_ref, volume_ref, beside_ref, residual_ref, out_ref, rest_ref, table_ref, spread_ref, rows_ref, *, blocks, others, pad, scale):
    views = slopes_ref.shape[1]
    planes, cells, bins = volume_ref.shape
    block, other, band = blocks_ref[0], blocks_ref[1], blocks_ref[2]
    shape = (cells, LEVELS * views)
    slopes = fill(slopes_ref, 0, (8, shape[1]), 1)
    level = lax.broadcasted_iota(jnp.int32, (8, shape[1]), 1) // views
    base = ((lowest_shift(slopes, block, blocks) + level) * cells).astype(F32)[:1]
    slopes = slopes.astype(F32)[:1]
    cell = (lax.broadcasted_iota(jnp.int32, shape, 0) + (block * cells - blocks * cells // 2)).astype(F32)
    gap = (cell * slopes - base) * (1.0 / cells)
    table_ref[...] = jnp.maximum(1.0 - jnp.abs(gap), 0.0).astype(BF16)
    beside = beside_ref[0].astype(F32)
    for plane in range(planes):
        spread_into(residual_ref, plane, slopes_ref, 0, block, blocks, other, others, pad, spread_ref)
        value = jnp.dot(table_ref[...], spread_ref[...], preferred_element_type=F32) * scale
        here = volume_ref[plane].astype(F32)
        if plane == 0:
            before = beside * (band == 1).astype(F32)
            after = volume_ref[1].astype(F32)
        else:
            before = volume_ref[0].astype(F32)
            after = beside * (band == 0).astype(F32)
        out_ref[plane] = value + 0.02 * (2.0 * here - before - after)
    split_rows(residual_ref, rest_ref, rows_ref, pad)


def back_y_kernel(slopes_ref, blocks_ref, partial_ref, residual_ref, out_ref, rest_ref, table_ref, spread_ref, rows_ref, *, blocks, others, pad, scale):
    views = slopes_ref.shape[1]
    planes, bins, cells = partial_ref.shape
    block, other = blocks_ref[1], blocks_ref[0]
    offset = offsets(slopes_ref, 1, block, blocks, cells)
    for level in range(LEVELS):
        table_ref[level * views : (level + 1) * views, :] = hat(offset, float(level)).astype(BF16)
    for plane in range(planes):
        spread_into(residual_ref, plane, slopes_ref, 1, block, blocks, other, others, pad, spread_ref)
        dims = (((0,), (0,)), ((), ()))
        value = lax.dot_general(spread_ref[...], table_ref[...], dims, preferred_element_type=F32)
        out_ref[plane] = partial_ref[plane] + value * scale
    split_rows(residual_ref, rest_ref, rows_ref, pad)


def back_x(slopes, blocks, volume, beside, residual, count, others, pad, scale):
    planes, cells, bins = volume.shape
    views = slopes.shape[1]

    def body(*refs):
        back_x_kernel(*refs, blocks=count, others=others, pad=pad, scale=scale)

    smem = pl.BlockSpec(memory_space=pltpu.SMEM)
    vmem = pl.BlockSpec(memory_space=pltpu.VMEM)
    return pl.pallas_call(
        body,
        out_shape=(jax.ShapeDtypeStruct(volume.shape, F32), jax.ShapeDtypeStruct((views, planes, bins), F32)),
        in_specs=[smem, smem, vmem, vmem, vmem],
        out_specs=(vmem, vmem),
        scratch_shapes=[
            pltpu.VMEM((cells, LEVELS * views), BF16),
            pltpu.VMEM((LEVELS * views, bins), BF16),
            pltpu.VMEM((planes * views, bins), F32),
        ],
        interpret=interpreted(),
        name="back_x",
    )(slopes, blocks, volume, beside, residual)


def back_y(slopes, blocks, partial, residual, count, others, pad, scale):
    planes, bins, cells = partial.shape
    views = slopes.shape[1]

    def body(*refs):
        back_y_kernel(*refs, blocks=count, others=others, pad=pad, scale=scale)

    smem = pl.BlockSpec(memory_space=pltpu.SMEM)
    vmem = pl.BlockSpec(memory_space=pltpu.VMEM)
    return pl.pallas_call(
        body,
        out_shape=(jax.ShapeDtypeStruct(partial.shape, F32), jax.ShapeDtypeStruct((views, planes, bins), F32)),
        in_specs=[smem, smem, vmem, vmem],
        out_specs=(vmem, vmem),
        scratch_shapes=[
            pltpu.VMEM((LEVELS * views, cells), BF16),
            pltpu.VMEM((LEVELS * views, bins), BF16),
            pltpu.VMEM((planes * views, bins), F32),
        ],
        interpret=interpreted(),
        name="back_y",
    )(slopes, blocks, partial, residual)


def meet(value, axis, width):
    size = lax.axis_size(axis)
    up = [(i, i + 1) for i in range(size - 1)]
    down = [(i + 1, i) for i in range(size - 1)]
    length = value.shape[1]
    left = lax.ppermute(value[:, length - width :], axis, up)
    right = lax.ppermute(value[:, :width], axis, down)
    middle = value[:, width : length - width]
    return jnp.concatenate([value[:, :width] + left, middle, value[:, length - width :] + right], axis=1)


def swap(value, axis, bit):
    return lax.ppermute(value, axis, [(i, i ^ bit) for i in range(lax.axis_size(axis))])


def on_device(volume, view_slopes, measured_x, measured_y):
    planes, cells_x, cells_y = volume.shape
    count_x = lax.axis_size("gx")
    count_y = lax.axis_size("gy")
    scale_x = float(cells_x * count_x) ** (-0.5)
    scale_y = float(cells_y * count_y) ** (-0.5)
    here_x = lax.axis_index("gx")
    here_y = lax.axis_index("gy")
    band = lax.axis_index("pa")
    blocks = jnp.stack([here_x, here_y, band]).astype(jnp.int32)
    pad_x, pad_y = 64, 128
    near = lax.dynamic_index_in_dim(volume, 1 - band, 0, True)
    beside = lax.ppermute(near, "pa", [(0, 1), (1, 0)])

    sum_y = forward(view_slopes, blocks[1:2], volume, measured_y, 1, count_y, pad_y, scale_y)
    sum_y, ready = lax.optimization_barrier((sum_y, measured_x))
    sum_x = forward(view_slopes, blocks[0:1], volume, ready, 0, count_x, pad_x, scale_x)
    sum_y = meet(sum_y, "gx", 2 * pad_y)
    sum_x = meet(sum_x, "gy", 2 * pad_x)

    rows = sum_y.shape[0] // 2
    odd = here_y & 1
    kept = lax.dynamic_slice_in_dim(sum_y, odd * rows, rows, 0)
    sent = lax.dynamic_slice_in_dim(sum_y, (1 - odd) * rows, rows, 0)
    half = kept + swap(sent, "gy", 1)
    for bit in (2, 4, 8):
        half = half + swap(half, "gy", bit)
    rest = swap(half, "gy", 1)
    full_y = jnp.where(odd == 0, jnp.concatenate([half, rest]), jnp.concatenate([rest, half]))
    full_x = sum_x
    for bit in (1, 2, 4):
        full_x = full_x + swap(full_x, "gx", bit)

    partial, residual_x = back_x(view_slopes, blocks, volume, beside, full_x, count_x, count_y, pad_x, scale_x)
    gradient, residual_y = back_y(view_slopes, blocks, partial, full_y, count_y, count_x, pad_y, scale_y)
    return (gradient, residual_x, residual_y)


def solution(mesh):
    return jax.shard_map(
        on_device,
        mesh=mesh,
        in_specs=(P("pa", "gx", "gy"), P(), P(None, "pa", "gy"), P(None, "pa", "gx")),
        out_specs=(P("pa", "gx", "gy"), P(None, "pa", "gy"), P(None, "pa", "gx")),
        check_vma=False,
    )
```

```python
import jax
import jax.numpy as jnp
from jax import lax
from jax.experimental import pallas as pl
from jax.experimental.pallas import tpu as pltpu
from jax.sharding import PartitionSpec as P


LEVELS = 16
SMEM = pltpu.SMEM
VMEM = pltpu.VMEM
F32 = jnp.float32
BF16 = jnp.bfloat16


def interpreted():
    return False


def fill(slopes_ref, family, shape, dim):
    views = slopes_ref.shape[1]
    view = lax.broadcasted_iota(jnp.int32, shape, dim) % views
    slopes = jnp.zeros(shape, jnp.int32)
    for v in range(views):
        slopes = jnp.where(view == v, slopes_ref[family, v], slopes)
    return slopes


def lowest_shift(slopes, block, blocks):
    return slopes * (block - blocks // 2) + jnp.minimum(slopes, 0)


def barrel(value, amounts, bits):
    for bit in range(bits):
        taken = ((amounts >> bit) & 1) == 1
        value = jnp.where(taken, pltpu.roll(value, 1 << bit, 1), value)
    return value


def offsets(slopes_ref, family, block, blocks, cells):
    views = slopes_ref.shape[1]
    slopes = fill(slopes_ref, family, (views, cells), 0)
    cell = lax.broadcasted_iota(jnp.int32, (views, cells), 1) + (block * cells - blocks * cells // 2)
    lowest = lowest_shift(slopes, block, blocks)
    return (slopes * cell - lowest * cells).astype(F32) * (1.0 / cells)


def hat(offset, level):
    return jnp.maximum(1.0 - jnp.abs(offset - level), 0.0)


def in_vmem(value):
    if interpreted():
        return value
    return pltpu.with_memory_space_constraint(value, VMEM)


def out_vmem(shape, dtype):
    if interpreted():
        return jax.ShapeDtypeStruct(shape, dtype)
    return VMEM(shape, dtype)


def anywhere():
    return pl.BlockSpec(memory_space=pl.ANY)


def vmem():
    return pl.BlockSpec(memory_space=VMEM)


def forward_kernel(*refs, family, axis, blocks, pad, scale, views):
    slopes_hbm, volume_hbm, measured_hbm, out_ref = refs[:4]
    rest = list(refs[4:])
    if family == 1:
        table_ref, near_ref = rest.pop(0), rest.pop(0)
    else:
        table_ref = rest.pop(0)
    slopes_ref, volume_ref, measured_ref, rows_ref, sems = rest
    planes = volume_ref.shape[0]
    bins = volume_ref.shape[2 - family]
    cells = volume_ref.shape[1 + family]
    width = out_ref.shape[1]
    fetch_slopes = pltpu.make_async_copy(slopes_hbm, slopes_ref, sems.at[0])
    fetch_volume = pltpu.make_async_copy(volume_hbm, volume_ref, sems.at[1])
    fetch_measured = pltpu.make_async_copy(measured_hbm, measured_ref, sems.at[2])
    fetch_slopes.start()
    fetch_volume.start()
    fetch_measured.start()
    if family == 1:
        far = 1 - lax.axis_index("pa")
        fetch_near = pltpu.make_async_copy(volume_hbm.at[pl.ds(far, 1)], near_ref, sems.at[3])
        fetch_near.start()
    block = lax.axis_index(axis)
    first = (block == 0).astype(F32)
    fetch_slopes.wait()
    offset = offsets(slopes_ref, family, block, blocks, cells)
    for level in range(LEVELS):
        table_ref[level * views : (level + 1) * views, :] = hat(offset, float(level)).astype(BF16)
    slopes = fill(slopes_ref, family, (views, width), 0)
    amounts = pad - lowest_shift(slopes, block, blocks)
    bits = max(1, (2 * pad).bit_length() - 1)
    empty = jnp.zeros((views, width - bins), F32)
    fetch_measured.wait()
    for plane in range(planes):
        for v in range(views):
            rows_ref[plane * views + v : plane * views + v + 1, :] = measured_ref[v, plane : plane + 1, :]
    fetch_volume.wait()
    for plane in range(planes):
        dims = (((1,), (family,)), ((), ()))
        summands = lax.dot_general(table_ref[...], volume_ref[plane], dims, preferred_element_type=F32)
        total = None
        for level in reversed(range(LEVELS)):
            piece = jnp.concatenate([summands[level * views : (level + 1) * views, :], empty], axis=1)
            total = piece if total is None else pltpu.roll(total, width - 1, 1) + piece
        total = barrel(total, amounts, bits) * scale
        known = jnp.concatenate([rows_ref[plane * views : (plane + 1) * views, :] * first, empty], axis=1)
        out_ref[plane * views : (plane + 1) * views, :] = total - pltpu.roll(known, pad, 1)
    if family == 1:
        fetch_near.wait()


def forward(slopes, volume, measured, family, axis, blocks, pad, scale):
    views, planes, bins = measured.shape
    width = bins + 2 * pad
    cells = volume.shape[1 + family]

    def body(*refs):
        forward_kernel(*refs, family=family, axis=axis, blocks=blocks, pad=pad, scale=scale, views=views)

    outs = [out_vmem((planes * views, width), F32)]
    scratch = []
    if family == 1:
        outs.append(out_vmem((LEVELS * views, cells), BF16))
        outs.append(out_vmem((1,) + volume.shape[1:], BF16))
    else:
        scratch.append(VMEM((LEVELS * views, cells), BF16))
    scratch += [
        SMEM(slopes.shape, jnp.int32),
        VMEM(volume.shape, BF16),
        VMEM(measured.shape, F32),
        VMEM((planes * views, bins), F32),
        pltpu.SemaphoreType.DMA((4,)),
    ]
    return pl.pallas_call(
        body,
        out_shape=tuple(outs),
        in_specs=[anywhere(), anywhere(), anywhere()],
        out_specs=tuple(vmem() for _ in outs),
        scratch_shapes=scratch,
        interpret=interpreted(),
    )(slopes, volume, measured)


def spread_into(value, slopes_ref, family, block, blocks, other, others, pad, scale, spread_ref):
    views, width = value.shape
    bins = width - 2 * pad
    slopes = fill(slopes_ref, family, (views, width), 0)
    bits = max(1, (2 * pad).bit_length() - 1)
    place = lax.broadcasted_iota(jnp.int32, (views, width), 1)
    inside = (place >= jnp.where(other == 0, pad, 0)) & (place < jnp.where(other == others - 1, pad + bins, width))
    value = jnp.where(inside, value * scale, 0.0).astype(BF16).astype(F32)
    amounts = lowest_shift(slopes, block, blocks) + pad
    value = pltpu.roll(barrel(value, amounts, bits), width - 2 * pad, 1)
    for level in range(LEVELS):
        spread_ref[level * views : (level + 1) * views, :] = value[:, :bins].astype(BF16)
        value = pltpu.roll(value, 1, 1)


def middle(value, pad):
    width = value.shape[1]
    return pltpu.roll(value, width - pad, 1)[:, : width - 2 * pad]


def back_x_kernel(slopes_hbm, volume_hbm, beside_ref, residual_ref, out_ref, rest_ref, slopes_ref, volume_ref, table_ref, spread_ref, rows_ref, sems, *, blocks, others, pad, scale, views):
    planes, cells, _ = volume_ref.shape
    fetch_slopes = pltpu.make_async_copy(slopes_hbm, slopes_ref, sems.at[0])
    fetch_volume = pltpu.make_async_copy(volume_hbm, volume_ref, sems.at[1])
    fetch_slopes.start()
    fetch_volume.start()
    block, other, band = lax.axis_index("gx"), lax.axis_index("gy"), lax.axis_index("pa")
    shape = (cells, LEVELS * views)
    fetch_slopes.wait()
    slopes = fill(slopes_ref, 0, (8, shape[1]), 1)
    level = lax.broadcasted_iota(jnp.int32, (8, shape[1]), 1) // views
    base = (lowest_shift(slopes, block, blocks) + level).astype(F32)[:1]
    slopes = slopes.astype(F32)[:1]
    cell = lax.broadcasted_iota(jnp.int32, shape, 0).astype(F32) * (1.0 / cells) + (block - blocks // 2).astype(F32)
    table_ref[...] = jnp.maximum(1.0 - jnp.abs(cell * slopes - base), 0.0).astype(BF16)
    fetch_volume.wait()
    for plane in range(planes):
        residual = residual_ref[plane * views : (plane + 1) * views, :]
        spread_into(residual, slopes_ref, 0, block, blocks, other, others, pad, scale, spread_ref)
        value = jnp.dot(table_ref[...], spread_ref[...], preferred_element_type=F32)
        here = volume_ref[plane].astype(F32)
        beside = beside_ref[0].astype(F32) * (band == 1 - plane).astype(F32)
        within = volume_ref[1 - plane].astype(F32)
        out_ref[plane] = value + 0.02 * (2.0 * here - beside - within)
        rows_ref[plane * views : (plane + 1) * views, :] = middle(residual, pad)
    for plane in range(planes):
        for v in range(views):
            rest_ref[v, plane : plane + 1, :] = rows_ref[plane * views + v : plane * views + v + 1, :]


def back_x(slopes, volume, beside, residual, blocks, others, pad, scale):
    planes, cells, bins = volume.shape
    views = slopes.shape[1]

    def body(*refs):
        back_x_kernel(*refs, blocks=blocks, others=others, pad=pad, scale=scale, views=views)

    return pl.pallas_call(
        body,
        out_shape=(out_vmem(volume.shape, F32), jax.ShapeDtypeStruct((views, planes, bins), F32)),
        in_specs=[anywhere(), anywhere(), vmem(), vmem()],
        out_specs=(vmem(), vmem()),
        scratch_shapes=[
            SMEM(slopes.shape, jnp.int32),
            VMEM(volume.shape, BF16),
            VMEM((cells, LEVELS * views), BF16),
            VMEM((LEVELS * views, bins), BF16),
            VMEM((planes * views, bins), F32),
            pltpu.SemaphoreType.DMA((2,)),
        ],
        interpret=interpreted(),
        name="back_x",
    )(slopes, volume, in_vmem(beside), in_vmem(residual))


def back_y_kernel(*refs, last, blocks, others, pad, scale, views):
    slopes_hbm, table_ref, partial_ref, half_ref = refs[:4]
    rest = list(refs[4:])
    if last:
        other_ref = rest.pop(0)
        rest.pop(0)
        rest_ref = rest.pop(1)
    out_hbm, slopes_ref, sum_ref, spread_ref, rows_ref, sems = rest
    fetch_slopes = pltpu.make_async_copy(slopes_hbm, slopes_ref, sems.at[0])
    fetch_slopes.start()
    block, other = lax.axis_index("gy"), lax.axis_index("gx")
    mine = lax.axis_index("gy") % 2
    plane = 1 - mine if last else mine
    value = other_ref[...] if last else half_ref[...]
    fetch_slopes.wait()
    spread_into(value, slopes_ref, 1, block, blocks, other, others, pad, scale, spread_ref)
    dims = (((0,), (0,)), ((), ()))
    back = lax.dot_general(spread_ref[...], table_ref[...], dims, preferred_element_type=F32)
    sum_ref[...] = partial_ref[pl.ds(plane, 1)] + back[None]
    store = pltpu.make_async_copy(sum_ref, out_hbm.at[pl.ds(plane, 1)], sems.at[1])
    store.start()
    if last:
        odd = mine == 1
        rows_ref[:views, :] = middle(jnp.where(odd, other_ref[...], half_ref[...]), pad)
        rows_ref[views:, :] = middle(jnp.where(odd, half_ref[...], other_ref[...]), pad)
        for p in range(2):
            for v in range(views):
                rest_ref[v, p : p + 1, :] = rows_ref[p * views + v : p * views + v + 1, :]
    store.wait()


def back_y(slopes, table, partial, half, rest, blocks, others, pad, scale):
    planes, bins, cells = partial.shape
    views = slopes.shape[1]
    last = rest is not None

    def body(*refs):
        back_y_kernel(*refs, last=last, blocks=blocks, others=others, pad=pad, scale=scale, views=views)

    operands = [slopes, in_vmem(table), in_vmem(partial), in_vmem(half)]
    specs = [anywhere(), vmem(), vmem(), vmem()]
    shapes = [jax.ShapeDtypeStruct(partial.shape, F32)]
    out_specs = [anywhere()]
    aliases = {}
    if last:
        other, gradient = rest
        operands += [in_vmem(other), gradient]
        specs += [vmem(), anywhere()]
        shapes.append(jax.ShapeDtypeStruct((views, planes, bins), F32))
        out_specs.append(vmem())
        aliases = {5: 0}
    return pl.pallas_call(
        body,
        out_shape=tuple(shapes),
        in_specs=specs,
        out_specs=tuple(out_specs),
        scratch_shapes=[
            SMEM(slopes.shape, jnp.int32),
            VMEM((1, bins, cells), F32),
            VMEM((LEVELS * views, bins), BF16),
            VMEM((planes * views, bins), F32),
            pltpu.SemaphoreType.DMA((2,)),
        ],
        input_output_aliases=aliases,
        interpret=interpreted(),
        name="back_y_last" if last else "back_y_own",
    )(*operands)


def edges(value, axis, width):
    size = lax.axis_size(axis)
    up = [(i, i + 1) for i in range(size - 1)]
    down = [(i + 1, i) for i in range(size - 1)]
    length = value.shape[1]
    left = lax.ppermute(value[:, length - width :], axis, up)
    right = lax.ppermute(value[:, :width], axis, down)
    return left, right


def meet(value, left, right):
    width = left.shape[1]
    length = value.shape[1]
    return jnp.concatenate(
        [value[:, :width] + left, value[:, width : length - width], value[:, length - width :] + right], axis=1
    )


def swap(value, axis, bit):
    return lax.ppermute(value, axis, [(i, i ^ bit) for i in range(lax.axis_size(axis))])


def steps(volume, view_slopes, measured_x, measured_y):
    _, cells_x, cells_y = volume.shape
    count_x = lax.axis_size("gx")
    count_y = lax.axis_size("gy")
    scale_x = float(cells_x * count_x) ** (-0.5)
    scale_y = float(cells_y * count_y) ** (-0.5)
    pad_x, pad_y = 64, 128

    sum_y, table_y, near = forward(view_slopes, volume, measured_y, 1, "gy", count_y, pad_y, scale_y)
    sides_y = edges(sum_y, "gx", 2 * pad_y)
    beside = lax.ppermute(near, "pa", [(0, 1), (1, 0)])
    (sum_x,) = forward(view_slopes, volume, measured_x, 0, "gx", count_x, pad_x, scale_x)
    sides_x = edges(sum_x, "gy", 2 * pad_x)

    sum_y = meet(sum_y, *sides_y)
    rows = sum_y.shape[0] // 2
    odd = lax.axis_index("gy") % 2
    kept = lax.dynamic_slice_in_dim(sum_y, odd * rows, rows, 0)
    sent = lax.dynamic_slice_in_dim(sum_y, (1 - odd) * rows, rows, 0)
    half = kept + swap(sent, "gy", 1)
    sum_x, half = lax.optimization_barrier((sum_x, half))
    sum_x = meet(sum_x, *sides_x)
    half = half + swap(half, "gy", 2)
    sum_x = sum_x + swap(sum_x, "gx", 1)
    half = half + swap(half, "gy", 4)
    sum_x = sum_x + swap(sum_x, "gx", 2)
    half = half + swap(half, "gy", 8)
    sum_x = sum_x + swap(sum_x, "gx", 4)
    other = swap(half, "gy", 1)

    partial, residual_x = back_x(view_slopes, volume, beside, sum_x, count_x, count_y, pad_x, scale_x)
    (gradient,) = back_y(view_slopes, table_y, partial, half, None, count_y, count_x, pad_y, scale_y)
    gradient, residual_y = back_y(
        view_slopes, table_y, partial, half, (other, gradient), count_y, count_x, pad_y, scale_y
    )
    return (gradient, residual_x, residual_y)


def solution(mesh):
    return jax.shard_map(
        steps,
        mesh=mesh,
        in_specs=(P("pa", "gx", "gy"), P(), P(None, "pa", "gy"), P(None, "pa", "gx")),
        out_specs=(P("pa", "gx", "gy"), P(None, "pa", "gy"), P(None, "pa", "gx")),
        check_vma=False,
    )
```

```python
import jax
import jax.numpy as jnp
from jax import lax
from jax.experimental import pallas as pl
from jax.experimental.pallas import tpu as pltpu
from jax.sharding import PartitionSpec as P


LEVELS = 16
SMEM = pltpu.SMEM
VMEM = pltpu.VMEM
F32 = jnp.float32
BF16 = jnp.bfloat16


def interpreted():
    return False


def fill(slopes_ref, family, shape, dim):
    views = slopes_ref.shape[1]
    view = lax.broadcasted_iota(jnp.int32, shape, dim) % views
    slopes = jnp.zeros(shape, jnp.int32)
    for v in range(views):
        slopes = jnp.where(view == v, slopes_ref[family, v], slopes)
    return slopes


def lowest_shift(slopes, block, blocks):
    return slopes * (block - blocks // 2) + jnp.minimum(slopes, 0)


def barrel(value, amounts, bits):
    for bit in range(bits):
        taken = ((amounts >> bit) & 1) == 1
        value = jnp.where(taken, pltpu.roll(value, 1 << bit, 1), value)
    return value


def offsets(slopes_ref, family, block, blocks, cells):
    views = slopes_ref.shape[1]
    slopes = fill(slopes_ref, family, (views, cells), 0)
    cell = lax.broadcasted_iota(jnp.int32, (views, cells), 1) + (block * cells - blocks * cells // 2)
    lowest = lowest_shift(slopes, block, blocks)
    return (slopes * cell - lowest * cells).astype(F32) * (1.0 / cells)


def hat(offset, level):
    return jnp.maximum(1.0 - jnp.abs(offset - level), 0.0)


def in_vmem(value):
    if interpreted():
        return value
    return pltpu.with_memory_space_constraint(value, VMEM)


def out_vmem(shape, dtype):
    if interpreted():
        return jax.ShapeDtypeStruct(shape, dtype)
    return VMEM(shape, dtype)


def anywhere():
    return pl.BlockSpec(memory_space=pl.ANY)


def vmem():
    return pl.BlockSpec(memory_space=VMEM)


def in_roles(value, odd):
    edge = value.shape[1] // 3
    lead, mid, trail = value[:, :edge], value[:, edge : 2 * edge], value[:, 2 * edge :]
    return jnp.concatenate([jnp.where(odd, lead, trail), mid, jnp.where(odd, trail, lead)], axis=1)


def from_roles(value, odd):
    edge = value.shape[1] // 3
    a, mid, b = value[:, :edge], value[:, edge : 2 * edge], value[:, 2 * edge :]
    return jnp.concatenate([jnp.where(odd, a, b), mid, jnp.where(odd, b, a)], axis=1)


def on_grid(value):
    return jnp.round(value * 32768.0) * (1.0 / 32768.0)


def project(table_ref, volume_ref, rows_ref, slopes_ref, out_ref, family, block, blocks, odd, pad, scale):
    planes = volume_ref.shape[0]
    views = slopes_ref.shape[1]
    bins = volume_ref.shape[2 - family]
    width = out_ref.shape[1]
    first = (block == 0).astype(F32)
    slopes = fill(slopes_ref, family, (views, width), 0)
    amounts = pad - lowest_shift(slopes, block, blocks)
    bits = max(1, (2 * pad).bit_length() - 1)
    empty = jnp.zeros((views, width - bins), F32)
    for plane in range(planes):
        dims = (((1,), (family,)), ((), ()))
        summands = lax.dot_general(table_ref[...], volume_ref[plane], dims, preferred_element_type=F32)
        total = None
        for level in reversed(range(LEVELS)):
            piece = jnp.concatenate([summands[level * views : (level + 1) * views, :], empty], axis=1)
            total = piece if total is None else pltpu.roll(total, width - 1, 1) + piece
        total = barrel(total, amounts, bits) * scale
        known = jnp.concatenate([rows_ref[plane * views : (plane + 1) * views, :] * first, empty], axis=1)
        total = on_grid(total - pltpu.roll(known, pad, 1))
        out_ref[plane * views : (plane + 1) * views, :] = in_roles(total, odd)


def build_table(slopes_ref, family, block, blocks, cells, table_ref):
    views = slopes_ref.shape[1]
    offset = offsets(slopes_ref, family, block, blocks, cells)
    for level in range(LEVELS):
        table_ref[level * views : (level + 1) * views, :] = hat(offset, float(level)).astype(BF16)


def gather_rows(measured_ref, rows_ref):
    views, planes, _ = measured_ref.shape
    for plane in range(planes):
        for v in range(views):
            rows_ref[plane * views + v : plane * views + v + 1, :] = measured_ref[v, plane : plane + 1, :]


def forward_kernel(
    slopes_hbm, volume_hbm, mx_hbm, my_hbm, x_ref, y_ref, table_y_ref, near_ref,
    table_x_ref, slopes_ref, volume_ref, mx_ref, my_ref, rows_x_ref, rows_y_ref, sems,
    *, count_x, count_y, pad_x, pad_y, scale_x, scale_y,
):
    _, cells_x, cells_y = volume_ref.shape
    fetches = [
        pltpu.make_async_copy(slopes_hbm, slopes_ref, sems.at[0]),
        pltpu.make_async_copy(volume_hbm, volume_ref, sems.at[1]),
        pltpu.make_async_copy(mx_hbm, mx_ref, sems.at[2]),
        pltpu.make_async_copy(my_hbm, my_ref, sems.at[3]),
        pltpu.make_async_copy(volume_hbm.at[pl.ds(1 - lax.axis_index("pa"), 1)], near_ref, sems.at[4]),
    ]
    for fetch in fetches:
        fetch.start()
    here_x, here_y = lax.axis_index("gx"), lax.axis_index("gy")
    fetches[0].wait()
    build_table(slopes_ref, 1, here_y, count_y, cells_y, table_y_ref)
    build_table(slopes_ref, 0, here_x, count_x, cells_x, table_x_ref)
    fetches[2].wait()
    fetches[3].wait()
    gather_rows(mx_ref, rows_x_ref)
    gather_rows(my_ref, rows_y_ref)
    fetches[1].wait()
    project(table_y_ref, volume_ref, rows_y_ref, slopes_ref, y_ref, 1, here_y, count_y, here_x % 2 == 1, pad_y, scale_y)
    project(table_x_ref, volume_ref, rows_x_ref, slopes_ref, x_ref, 0, here_x, count_x, here_y % 2 == 1, pad_x, scale_x)
    fetches[4].wait()


def forward(slopes, volume, measured_x, measured_y, count_x, count_y, pad_x, pad_y, scale_x, scale_y):
    views = slopes.shape[1]
    planes, cells_x, cells_y = volume.shape

    def body(*refs):
        forward_kernel(
            *refs, count_x=count_x, count_y=count_y, pad_x=pad_x, pad_y=pad_y, scale_x=scale_x, scale_y=scale_y
        )

    return pl.pallas_call(
        body,
        out_shape=(
            out_vmem((planes * views, cells_y + 2 * pad_x), F32),
            out_vmem((planes * views, cells_x + 2 * pad_y), F32),
            out_vmem((LEVELS * views, cells_y), BF16),
            out_vmem((1,) + volume.shape[1:], BF16),
        ),
        in_specs=[anywhere()] * 4,
        out_specs=(vmem(),) * 4,
        scratch_shapes=[
            VMEM((LEVELS * views, cells_x), BF16),
            SMEM(slopes.shape, jnp.int32),
            VMEM(volume.shape, BF16),
            VMEM(measured_x.shape, F32),
            VMEM(measured_y.shape, F32),
            VMEM((planes * views, cells_y), F32),
            VMEM((planes * views, cells_x), F32),
            pltpu.SemaphoreType.DMA((5,)),
        ],
        interpret=interpreted(),
        name="forward",
    )(slopes, volume, measured_x, measured_y)


def half_of(index):
    return ((index + 1) // 2) % 2


def spread_into(value, slopes_ref, family, block, blocks, other, others, pad, scale, spread_ref):
    views, width = value.shape
    bins = width - 2 * pad
    slopes = fill(slopes_ref, family, (views, width), 0)
    bits = max(1, (2 * pad).bit_length() - 1)
    place = lax.broadcasted_iota(jnp.int32, (views, width), 1)
    inside = (place >= jnp.where(other == 0, pad, 0)) & (place < jnp.where(other == others - 1, pad + bins, width))
    value = jnp.where(inside, value * scale, 0.0).astype(BF16).astype(F32)
    amounts = lowest_shift(slopes, block, blocks) + pad
    value = pltpu.roll(barrel(value, amounts, bits), width - 2 * pad, 1)
    for level in range(LEVELS):
        spread_ref[level * views : (level + 1) * views, :] = value[:, :bins].astype(BF16)
        value = pltpu.roll(value, 1, 1)


def middle(value, pad):
    width = value.shape[1]
    return pltpu.roll(value, width - pad, 1)[:, : width - 2 * pad]


def back_x_kernel(slopes_hbm, volume_hbm, beside_ref, residual_ref, out_ref, rest_ref, slopes_ref, volume_ref, table_ref, spread_ref, rows_ref, sems, *, blocks, others, pad, scale, views):
    planes, cells, _ = volume_ref.shape
    fetch_slopes = pltpu.make_async_copy(slopes_hbm, slopes_ref, sems.at[0])
    fetch_volume = pltpu.make_async_copy(volume_hbm, volume_ref, sems.at[1])
    fetch_slopes.start()
    fetch_volume.start()
    block, other, band = lax.axis_index("gx"), lax.axis_index("gy"), lax.axis_index("pa")
    shape = (cells, LEVELS * views)
    fetch_slopes.wait()
    slopes = fill(slopes_ref, 0, (8, shape[1]), 1)
    level = lax.broadcasted_iota(jnp.int32, (8, shape[1]), 1) // views
    base = (lowest_shift(slopes, block, blocks) + level).astype(F32)[:1]
    slopes = slopes.astype(F32)[:1]
    cell = lax.broadcasted_iota(jnp.int32, shape, 0).astype(F32) * (1.0 / cells) + (block - blocks // 2).astype(F32)
    table_ref[...] = jnp.maximum(1.0 - jnp.abs(cell * slopes - base), 0.0).astype(BF16)
    fetch_volume.wait()
    for plane in range(planes):
        residual = from_roles(residual_ref[plane * views : (plane + 1) * views, :], other % 2 == 1)
        spread_into(residual, slopes_ref, 0, block, blocks, other, others, pad, scale, spread_ref)
        value = jnp.dot(table_ref[...], spread_ref[...], preferred_element_type=F32)
        here = volume_ref[plane].astype(F32)
        beside = beside_ref[0].astype(F32) * (band == 1 - plane).astype(F32)
        within = volume_ref[1 - plane].astype(F32)
        out_ref[plane] = value + 0.02 * (2.0 * here - beside - within)
        rows_ref[plane * views : (plane + 1) * views, :] = middle(residual, pad)
    for plane in range(planes):
        for v in range(views):
            rest_ref[v, plane : plane + 1, :] = rows_ref[plane * views + v : plane * views + v + 1, :]


def back_x(slopes, volume, beside, residual, blocks, others, pad, scale):
    planes, cells, bins = volume.shape
    views = slopes.shape[1]

    def body(*refs):
        back_x_kernel(*refs, blocks=blocks, others=others, pad=pad, scale=scale, views=views)

    return pl.pallas_call(
        body,
        out_shape=(out_vmem(volume.shape, F32), jax.ShapeDtypeStruct((views, planes, bins), F32)),
        in_specs=[anywhere(), anywhere(), vmem(), vmem()],
        out_specs=(vmem(), vmem()),
        scratch_shapes=[
            SMEM(slopes.shape, jnp.int32),
            VMEM(volume.shape, BF16),
            VMEM((cells, LEVELS * views), BF16),
            VMEM((LEVELS * views, bins), BF16),
            VMEM((planes * views, bins), F32),
            pltpu.SemaphoreType.DMA((2,)),
        ],
        interpret=interpreted(),
        name="back_x",
    )(slopes, volume, in_vmem(beside), in_vmem(residual))


def back_y_kernel(*refs, last, blocks, others, pad, scale, views):
    slopes_hbm, table_ref, partial_ref, half_ref = refs[:4]
    rest = list(refs[4:])
    if last:
        other_ref = rest.pop(0)
        rest.pop(0)
        rest_ref = rest.pop(1)
    out_hbm, slopes_ref, sum_ref, spread_ref, rows_ref, sems = rest
    fetch_slopes = pltpu.make_async_copy(slopes_hbm, slopes_ref, sems.at[0])
    fetch_slopes.start()
    block, other = lax.axis_index("gy"), lax.axis_index("gx")
    mine = half_of(lax.axis_index("gy"))
    flip = other % 2 == 1
    plane = 1 - mine if last else mine
    value = from_roles(other_ref[...] if last else half_ref[...], flip)
    fetch_slopes.wait()
    spread_into(value, slopes_ref, 1, block, blocks, other, others, pad, scale, spread_ref)
    dims = (((0,), (0,)), ((), ()))
    back = lax.dot_general(spread_ref[...], table_ref[...], dims, preferred_element_type=F32)
    sum_ref[...] = partial_ref[pl.ds(plane, 1)] + back[None]
    store = pltpu.make_async_copy(sum_ref, out_hbm.at[pl.ds(plane, 1)], sems.at[1])
    store.start()
    if last:
        odd = mine == 1
        rows_ref[:views, :] = middle(from_roles(jnp.where(odd, other_ref[...], half_ref[...]), flip), pad)
        rows_ref[views:, :] = middle(from_roles(jnp.where(odd, half_ref[...], other_ref[...]), flip), pad)
        for p in range(2):
            for v in range(views):
                rest_ref[v, p : p + 1, :] = rows_ref[p * views + v : p * views + v + 1, :]
    store.wait()


def back_y(slopes, table, partial, half, rest, blocks, others, pad, scale):
    planes, bins, cells = partial.shape
    views = slopes.shape[1]
    last = rest is not None

    def body(*refs):
        back_y_kernel(*refs, last=last, blocks=blocks, others=others, pad=pad, scale=scale, views=views)

    operands = [slopes, in_vmem(table), in_vmem(partial), in_vmem(half)]
    specs = [anywhere(), vmem(), vmem(), vmem()]
    shapes = [jax.ShapeDtypeStruct(partial.shape, F32)]
    out_specs = [anywhere()]
    aliases = {}
    if last:
        other, gradient = rest
        operands += [in_vmem(other), gradient]
        specs += [vmem(), anywhere()]
        shapes.append(jax.ShapeDtypeStruct((views, planes, bins), F32))
        out_specs.append(vmem())
        aliases = {5: 0}
    return pl.pallas_call(
        body,
        out_shape=tuple(shapes),
        in_specs=specs,
        out_specs=tuple(out_specs),
        scratch_shapes=[
            SMEM(slopes.shape, jnp.int32),
            VMEM((1, bins, cells), F32),
            VMEM((LEVELS * views, bins), BF16),
            VMEM((planes * views, bins), F32),
            pltpu.SemaphoreType.DMA((2,)),
        ],
        input_output_aliases=aliases,
        interpret=interpreted(),
        name="back_y_last" if last else "back_y_own",
    )(*operands)


def swap(value, axis, bit):
    return lax.ppermute(value, axis, [(i, i ^ bit) for i in range(lax.axis_size(axis))])


def swap_odd(value, axis):
    size = lax.axis_size(axis)
    return lax.ppermute(value, axis, [(i, (i + (1 if i % 2 else -1)) % size) for i in range(size)])


def inner(axis):
    index = lax.axis_index(axis)
    return ((index > 0) & (index < lax.axis_size(axis) - 1)).astype(F32)


def steps(volume, view_slopes, measured_x, measured_y):
    _, cells_x, cells_y = volume.shape
    count_x = lax.axis_size("gx")
    count_y = lax.axis_size("gy")
    scale_x = float(cells_x * count_x) ** (-0.5)
    scale_y = float(cells_y * count_y) ** (-0.5)
    pad_x, pad_y = 64, 128

    sum_x, sum_y, table_y, near = forward(
        view_slopes, volume, measured_x, measured_y, count_x, count_y, pad_x, pad_y, scale_x, scale_y
    )
    wide = sum_x.shape[1]
    edge_x, edge_y = wide // 3, sum_y.shape[1] // 3
    y_a, y_mid, y_b = sum_y[:, :edge_y], sum_y[:, edge_y : 2 * edge_y], sum_y[:, 2 * edge_y :]

    got = swap(jnp.concatenate([sum_x, y_a], axis=1), "gx", 1)
    sum_x, y_a = sum_x + got[:, :wide], y_a + got[:, wide:]
    got = swap_odd(jnp.concatenate([sum_x, y_b], axis=1), "gx")
    sum_x, y_b = sum_x + got[:, :wide], y_b + got[:, wide:] * inner("gx")
    sum_y = jnp.concatenate([y_a, y_mid, y_b], axis=1)
    x_a, x_mid, x_b = sum_x[:, :edge_x], sum_x[:, edge_x : 2 * edge_x], sum_x[:, 2 * edge_x :]

    rows = sum_y.shape[0] // 2
    long = sum_y.shape[1]
    owns = half_of(lax.axis_index("gy")) == 0
    kept = jnp.where(owns, sum_y[:rows], sum_y[rows:])
    sent = jnp.where(owns, sum_y[rows:], sum_y[:rows])
    got = swap(jnp.concatenate([sent, x_a[:rows], x_a[rows:]], axis=1), "gy", 1)
    half = kept + got[:, :long]
    x_a = x_a + jnp.concatenate([got[:, long : long + edge_x], got[:, long + edge_x :]], axis=0)
    got = swap_odd(jnp.concatenate([half, x_b[:rows], x_b[rows:]], axis=1), "gy")
    half = half + got[:, :long]
    got = jnp.concatenate([got[:, long : long + edge_x], got[:, long + edge_x :]], axis=0)
    x_b = x_b + got * inner("gy")
    sum_x = jnp.concatenate([x_a, x_mid, x_b], axis=1)

    half = half + swap(half, "gy", 4)
    sum_x = sum_x + swap(sum_x, "gx", 4)
    beside = lax.ppermute(near, "pa", [(0, 1), (1, 0)])
    half = half + swap(half, "gy", 8)
    other = swap(half, "gy", 1)

    partial, residual_x = back_x(view_slopes, volume, beside, sum_x, count_x, count_y, pad_x, scale_x)
    (gradient,) = back_y(view_slopes, table_y, partial, half, None, count_y, count_x, pad_y, scale_y)
    gradient, residual_y = back_y(
        view_slopes, table_y, partial, half, (other, gradient), count_y, count_x, pad_y, scale_y
    )
    return (gradient, residual_x, residual_y)


def solution(mesh):
    return jax.shard_map(
        steps,
        mesh=mesh,
        in_specs=(P("pa", "gx", "gy"), P(), P(None, "pa", "gy"), P(None, "pa", "gx")),
        out_specs=(P("pa", "gx", "gy"), P(None, "pa", "gy"), P(None, "pa", "gx")),
        check_vma=False,
    )
```

```python
import jax
import jax.numpy as jnp
from jax import lax
from jax.experimental import pallas as pl
from jax.experimental.pallas import tpu as pltpu
from jax.sharding import PartitionSpec as P


LEVELS = 16
RING = 8
SMEM = pltpu.SMEM
VMEM = pltpu.VMEM
F32 = jnp.float32
BF16 = jnp.bfloat16


def interpreted():
    return False


def fill(slopes_ref, family, shape, dim):
    views = slopes_ref.shape[1]
    view = lax.broadcasted_iota(jnp.int32, shape, dim) % views
    slopes = jnp.zeros(shape, jnp.int32)
    for v in range(views):
        slopes = jnp.where(view == v, slopes_ref[family, v], slopes)
    return slopes


def tiled(value, width):
    return jnp.concatenate([value] * (width // value.shape[1]), axis=1)


def lowest_shift(slopes, block, blocks):
    return slopes * (block - blocks // 2) + jnp.minimum(slopes, 0)


def barrel(value, amounts, bits):
    for bit in range(bits):
        taken = ((amounts >> bit) & 1) == 1
        value = jnp.where(taken, pltpu.roll(value, 1 << bit, 1), value)
    return value


def offsets(slopes, block, blocks, cells):
    views = slopes.shape[0]
    lowest = tiled(lowest_shift(slopes, block, blocks).astype(F32), cells)
    cell = lax.broadcasted_iota(jnp.int32, (views, cells), 1) + (block * cells - blocks * cells // 2)
    return tiled(slopes.astype(F32), cells) * (cell.astype(F32) * (1.0 / cells)) - lowest


def hat(offset, level):
    return jnp.maximum(1.0 - jnp.abs(offset - level), 0.0)


def in_vmem(value):
    if interpreted():
        return value
    return pltpu.with_memory_space_constraint(value, VMEM)


def out_vmem(shape, dtype):
    if interpreted():
        return jax.ShapeDtypeStruct(shape, dtype)
    return VMEM(shape, dtype)


def anywhere():
    return pl.BlockSpec(memory_space=pl.ANY)


def vmem():
    return pl.BlockSpec(memory_space=VMEM)


def in_roles(value, odd):
    edge = value.shape[1] // 3
    lead, mid, trail = value[:, :edge], value[:, edge : 2 * edge], value[:, 2 * edge :]
    return jnp.concatenate([jnp.where(odd, lead, trail), mid, jnp.where(odd, trail, lead)], axis=1)


def from_roles(value, odd):
    edge = value.shape[1] // 3
    a, mid, b = value[:, :edge], value[:, edge : 2 * edge], value[:, 2 * edge :]
    return jnp.concatenate([jnp.where(odd, a, b), mid, jnp.where(odd, b, a)], axis=1)


def on_grid(value):
    return jnp.round(value * 32768.0) * (1.0 / 32768.0)


def project(table_ref, volume_ref, rows_ref, slopes, out_ref, family, block, blocks, odd, pad, scale):
    planes = volume_ref.shape[0]
    views = slopes.shape[0]
    bins = volume_ref.shape[2 - family]
    width = out_ref.shape[1]
    first = (block == 0).astype(F32)
    amounts = tiled(pad - lowest_shift(slopes, block, blocks), width)
    bits = max(1, (2 * pad).bit_length() - 1)
    empty = jnp.zeros((views, width - bins), F32)
    for plane in range(planes):
        dims = (((1,), (family,)), ((), ()))
        summands = lax.dot_general(table_ref[...], volume_ref[plane], dims, preferred_element_type=F32)
        total = None
        for level in reversed(range(LEVELS)):
            piece = jnp.concatenate([summands[level * views : (level + 1) * views, :], empty], axis=1)
            total = piece if total is None else pltpu.roll(total, width - 1, 1) + piece
        total = barrel(total, amounts, bits) * scale
        known = jnp.concatenate([rows_ref[plane * views : (plane + 1) * views, :] * first, empty], axis=1)
        total = on_grid(total - pltpu.roll(known, pad, 1))
        out_ref[plane * views : (plane + 1) * views, :] = in_roles(total, odd)


def build_table(slopes, block, blocks, cells, table_ref):
    views = slopes.shape[0]
    offset = offsets(slopes, block, blocks, cells)
    for level in range(LEVELS):
        table_ref[level * views : (level + 1) * views, :] = hat(offset, float(level)).astype(BF16)


def gather_rows(measured_ref, rows_ref):
    views, planes, _ = measured_ref.shape
    for plane in range(planes):
        for v in range(views):
            rows_ref[plane * views + v : plane * views + v + 1, :] = measured_ref[v, plane : plane + 1, :]


def forward_kernel(
    slopes_hbm, volume_hbm, mx_hbm, my_hbm,
    x_ref, y_ref, table_y_ref, near_ref, volume_ref, column_x_ref, column_y_ref, lane_ref,
    table_x_ref, slopes_ref, mx_ref, my_ref, rows_x_ref, rows_y_ref, sems,
    *, count_x, count_y, pad_x, pad_y, scale_x, scale_y,
):
    _, cells_x, cells_y = volume_ref.shape
    fetches = [
        pltpu.make_async_copy(slopes_hbm, slopes_ref, sems.at[0]),
        pltpu.make_async_copy(volume_hbm, volume_ref, sems.at[1]),
        pltpu.make_async_copy(mx_hbm, mx_ref, sems.at[2]),
        pltpu.make_async_copy(my_hbm, my_ref, sems.at[3]),
        pltpu.make_async_copy(volume_hbm.at[pl.ds(1 - lax.axis_index("pa"), 1)], near_ref, sems.at[4]),
    ]
    for fetch in fetches:
        fetch.start()
    here_x, here_y = lax.axis_index("gx"), lax.axis_index("gy")
    fetches[0].wait()
    column_x = fill(slopes_ref, 0, column_x_ref.shape, 0)
    column_y = fill(slopes_ref, 1, column_y_ref.shape, 0)
    column_x_ref[...] = column_x
    column_y_ref[...] = column_y
    lane_ref[...] = fill(slopes_ref, 0, lane_ref.shape, 1)
    build_table(column_y, here_y, count_y, cells_y, table_y_ref)
    build_table(column_x, here_x, count_x, cells_x, table_x_ref)
    fetches[2].wait()
    fetches[3].wait()
    gather_rows(mx_ref, rows_x_ref)
    gather_rows(my_ref, rows_y_ref)
    fetches[1].wait()
    project(table_y_ref, volume_ref, rows_y_ref, column_y, y_ref, 1, here_y, count_y, here_x % 2 == 1, pad_y, scale_y)
    project(table_x_ref, volume_ref, rows_x_ref, column_x, x_ref, 0, here_x, count_x, here_y % 2 == 1, pad_x, scale_x)
    fetches[4].wait()


def forward(slopes, volume, measured_x, measured_y, count_x, count_y, pad_x, pad_y, scale_x, scale_y):
    views = slopes.shape[1]
    planes, cells_x, cells_y = volume.shape

    def body(*refs):
        forward_kernel(
            *refs, count_x=count_x, count_y=count_y, pad_x=pad_x, pad_y=pad_y, scale_x=scale_x, scale_y=scale_y
        )

    return pl.pallas_call(
        body,
        out_shape=(
            out_vmem((planes * views, cells_y + 2 * pad_x), F32),
            out_vmem((planes * views, cells_x + 2 * pad_y), F32),
            out_vmem((LEVELS * views, cells_y), BF16),
            out_vmem((1,) + volume.shape[1:], BF16),
            out_vmem(volume.shape, BF16),
            out_vmem((views, 128), jnp.int32),
            out_vmem((views, 128), jnp.int32),
            out_vmem((8, LEVELS * views), jnp.int32),
        ),
        in_specs=[anywhere()] * 4,
        out_specs=(vmem(),) * 8,
        scratch_shapes=[
            VMEM((LEVELS * views, cells_x), BF16),
            SMEM(slopes.shape, jnp.int32),
            VMEM(measured_x.shape, F32),
            VMEM(measured_y.shape, F32),
            VMEM((planes * views, cells_y), F32),
            VMEM((planes * views, cells_x), F32),
            pltpu.SemaphoreType.DMA((5,)),
        ],
        interpret=interpreted(),
        name="forward",
    )(slopes, volume, measured_x, measured_y)


def half_of(index):
    return ((index + 1) // 2) % 2


def spread_into(value, slopes, block, blocks, other, others, pad, scale, spread_ref):
    views, width = value.shape
    bins = width - 2 * pad
    bits = max(1, (2 * pad).bit_length() - 1)
    place = lax.broadcasted_iota(jnp.int32, (views, width), 1)
    inside = (place >= jnp.where(other == 0, pad, 0)) & (place < jnp.where(other == others - 1, pad + bins, width))
    value = jnp.where(inside, value * scale, 0.0).astype(BF16).astype(F32)
    amounts = tiled(lowest_shift(slopes, block, blocks) + pad, width)
    value = pltpu.roll(barrel(value, amounts, bits), width - 2 * pad, 1)
    for level in range(LEVELS):
        spread_ref[level * views : (level + 1) * views, :] = value[:, :bins].astype(BF16)
        value = pltpu.roll(value, 1, 1)


def middle(value, pad):
    width = value.shape[1]
    return pltpu.roll(value, width - pad, 1)[:, : width - 2 * pad]


def prepare_kernel(lane_ref, volume_ref, beside_ref, table_ref, base_ref, *, blocks):
    planes, cells, _ = volume_ref.shape
    block, band = lax.axis_index("gx"), lax.axis_index("pa")
    slopes = lane_ref[...]
    views = slopes.shape[1] // LEVELS
    level = lax.broadcasted_iota(jnp.int32, slopes.shape, 1) // views
    base = (lowest_shift(slopes, block, blocks) + level).astype(F32)[:1]
    slopes = slopes.astype(F32)[:1]
    shape = (cells, LEVELS * views)
    cell = lax.broadcasted_iota(jnp.int32, shape, 0).astype(F32) * (1.0 / cells) + (block - blocks // 2).astype(F32)
    table_ref[...] = jnp.maximum(1.0 - jnp.abs(cell * slopes - base), 0.0).astype(BF16)
    for plane in range(planes):
        here = volume_ref[plane].astype(F32)
        beside = beside_ref[0].astype(F32) * (band == 1 - plane).astype(F32)
        within = volume_ref[1 - plane].astype(F32)
        base_ref[plane] = 0.02 * (2.0 * here - beside - within)


def prepare(lane, volume, beside, blocks):
    def body(*refs):
        prepare_kernel(*refs, blocks=blocks)

    return pl.pallas_call(
        body,
        out_shape=(out_vmem((volume.shape[1], lane.shape[1]), BF16), out_vmem(volume.shape, F32)),
        in_specs=[vmem()] * 3,
        out_specs=(vmem(), vmem()),
        interpret=interpreted(),
        name="prepare",
    )(*(in_vmem(value) for value in (lane, volume, beside)))


def back_x_kernel(column_ref, table_ref, base_ref, residual_ref, out_ref, rest_hbm, spread_ref, rows_ref, rest_ref, sem, *, blocks, others, pad, scale):
    planes, _, _ = base_ref.shape
    views = column_ref.shape[0]
    block, other = lax.axis_index("gx"), lax.axis_index("gy")
    column = column_ref[...]
    residuals = [from_roles(residual_ref[p * views : (p + 1) * views, :], other % 2 == 1) for p in range(planes)]
    for plane in range(planes):
        rows_ref[plane * views : (plane + 1) * views, :] = middle(residuals[plane], pad)
    for plane in range(planes):
        for v in range(views):
            rest_ref[v, plane : plane + 1, :] = rows_ref[plane * views + v : plane * views + v + 1, :]
    store = pltpu.make_async_copy(rest_ref, rest_hbm, sem)
    store.start()
    for plane in range(planes):
        spread_into(residuals[plane], column, block, blocks, other, others, pad, scale, spread_ref)
        out_ref[plane] = base_ref[plane] + jnp.dot(table_ref[...], spread_ref[...], preferred_element_type=F32)
    store.wait()


def back_x(column, table, base, residual, blocks, others, pad, scale):
    planes, _, bins = base.shape
    views = column.shape[0]

    def body(*refs):
        back_x_kernel(*refs, blocks=blocks, others=others, pad=pad, scale=scale)

    return pl.pallas_call(
        body,
        out_shape=(out_vmem(base.shape, F32), jax.ShapeDtypeStruct((views, planes, bins), F32)),
        in_specs=[vmem()] * 4,
        out_specs=(vmem(), anywhere()),
        scratch_shapes=[
            VMEM((LEVELS * views, bins), BF16),
            VMEM((planes * views, bins), F32),
            VMEM((views, planes, bins), F32),
            pltpu.SemaphoreType.DMA,
        ],
        interpret=interpreted(),
        name="back_x",
    )(*(in_vmem(value) for value in (column, table, base, residual)))


def back_y_kernel(*refs, last, blocks, others, pad, scale, views):
    column_ref, table_ref, partial_ref, half_ref = refs[:4]
    rest = list(refs[4:])
    if last:
        other_ref = rest.pop(0)
        rest.pop(0)
        rest_hbm = rest.pop(1)
        rest_ref = rest.pop()
    out_hbm, sum_ref, spread_ref, rows_ref, sems = rest
    block, other = lax.axis_index("gy"), lax.axis_index("gx")
    mine = half_of(lax.axis_index("gy"))
    flip = other % 2 == 1
    plane = 1 - mine if last else mine
    value = from_roles(other_ref[...] if last else half_ref[...], flip)
    spread_into(value, column_ref[...], block, blocks, other, others, pad, scale, spread_ref)
    dims = (((0,), (0,)), ((), ()))
    back = lax.dot_general(spread_ref[...], table_ref[...], dims, preferred_element_type=F32)
    sum_ref[...] = partial_ref[pl.ds(plane, 1)] + back[None]
    store = pltpu.make_async_copy(sum_ref, out_hbm.at[pl.ds(plane, 1)], sems.at[1])
    store.start()
    if last:
        odd = mine == 1
        rows_ref[:views, :] = middle(from_roles(jnp.where(odd, other_ref[...], half_ref[...]), flip), pad)
        rows_ref[views:, :] = middle(from_roles(jnp.where(odd, half_ref[...], other_ref[...]), flip), pad)
        for p in range(2):
            for v in range(views):
                rest_ref[v, p : p + 1, :] = rows_ref[p * views + v : p * views + v + 1, :]
        also = pltpu.make_async_copy(rest_ref, rest_hbm, sems.at[0])
        also.start()
        also.wait()
    store.wait()


def back_y(column, table, partial, half, rest, blocks, others, pad, scale):
    planes, bins, cells = partial.shape
    views = column.shape[0]
    last = rest is not None

    def body(*refs):
        back_y_kernel(*refs, last=last, blocks=blocks, others=others, pad=pad, scale=scale, views=views)

    operands = [in_vmem(column), in_vmem(table), in_vmem(partial), in_vmem(half)]
    specs = [vmem()] * 4
    shapes = [jax.ShapeDtypeStruct(partial.shape, F32)]
    out_specs = [anywhere()]
    aliases = {}
    if last:
        other, gradient = rest
        operands += [in_vmem(other), gradient]
        specs += [vmem(), anywhere()]
        shapes.append(jax.ShapeDtypeStruct((views, planes, bins), F32))
        out_specs.append(anywhere())
        aliases = {5: 0}
    scratch = [
        VMEM((1, bins, cells), F32),
        VMEM((LEVELS * views, bins), BF16),
        VMEM((planes * views, bins), F32),
        pltpu.SemaphoreType.DMA((2,)),
    ]
    if last:
        scratch.append(VMEM((views, planes, bins), F32))
    return pl.pallas_call(
        body,
        out_shape=tuple(shapes),
        in_specs=specs,
        out_specs=tuple(out_specs),
        scratch_shapes=scratch,
        input_output_aliases=aliases,
        interpret=interpreted(),
        name="back_y_last" if last else "back_y_own",
    )(*operands)


def exchange(value, axis, partner):
    return lax.ppermute(value, axis, [(i, partner(i)) for i in range(lax.axis_size(axis))])


def twin(i):
    return i ^ 1


def odd_twin(i):
    return i - i % RING + (i + (1 if i % 2 else -1)) % RING


def across(i):
    return i - i % RING + (i + (-3 if i % 2 else 3)) % RING


def at_end(size, axis):
    index = lax.axis_index(axis) % size
    return (index == 0) | (index == size - 1)


def steps(volume, view_slopes, measured_x, measured_y):
    _, cells_x, cells_y = volume.shape
    count_x = lax.axis_size("gx")
    count_y = lax.axis_size("gy")
    scale_x = float(cells_x * count_x) ** (-0.5)
    scale_y = float(cells_y * count_y) ** (-0.5)
    pad_x, pad_y = 64, 128

    sum_x, sum_y, table_y, near, volume, column_x, column_y, lane = forward(
        view_slopes, volume, measured_x, measured_y, count_x, count_y, pad_x, pad_y, scale_x, scale_y
    )
    wide = sum_x.shape[1]
    edge_x, edge_y = wide // 3, sum_y.shape[1] // 3
    y_a, y_mid, y_b = sum_y[:, :edge_y], sum_y[:, edge_y : 2 * edge_y], sum_y[:, 2 * edge_y :]

    got = exchange(jnp.concatenate([sum_x, y_a], axis=1), "gx", twin)
    beside = lax.ppermute(near, "pa", [(0, 1), (1, 0)])
    sum_x, y_a = sum_x + got[:, :wide], y_a + got[:, wide:]
    got = exchange(jnp.concatenate([sum_x, y_b], axis=1), "gx", odd_twin)
    sum_x, y_b = sum_x + got[:, :wide], y_b + jnp.where(at_end(count_x, "gx"), 0.0, got[:, wide:])
    sum_y = jnp.concatenate([y_a, y_mid, y_b], axis=1)
    x_a, x_mid, x_b = sum_x[:, :edge_x], sum_x[:, edge_x : 2 * edge_x], sum_x[:, 2 * edge_x :]

    rows = sum_y.shape[0] // 2
    long = sum_y.shape[1]
    owns = half_of(lax.axis_index("gy")) == 0
    kept = jnp.where(owns, sum_y[:rows], sum_y[rows:])
    sent = jnp.where(owns, sum_y[rows:], sum_y[:rows])
    got = exchange(jnp.concatenate([sent, x_a[:rows], x_a[rows:]], axis=1), "gy", twin)
    half = kept + got[:, :long]
    x_a = x_a + jnp.concatenate([got[:, long : long + edge_x], got[:, long + edge_x :]], axis=0)
    got = exchange(jnp.concatenate([half, x_b[:rows], x_b[rows:]], axis=1), "gy", lambda i: i ^ RING)
    half = half + got[:, :long]
    sent_b = jnp.where(at_end(RING, "gy"), got[:, long:], jnp.concatenate([x_b[:rows], x_b[rows:]], axis=1))
    got = exchange(jnp.concatenate([half, sent_b], axis=1), "gy", odd_twin)
    half = half + got[:, :long]
    got = jnp.where(at_end(count_y, "gy"), 0.0, got)
    half, x_b, got = lax.optimization_barrier((half, x_b, got))
    x_b = x_b + jnp.concatenate([got[:, long : long + edge_x], got[:, long + edge_x :]], axis=0)
    sum_x = jnp.concatenate([x_a, x_mid, x_b], axis=1)

    half = half + exchange(half, "gy", across)
    sum_x = sum_x + exchange(sum_x, "gx", across)
    other = exchange(half, "gy", twin)

    table_x, base = prepare(lane, volume, beside, count_x)
    partial, residual_x = back_x(column_x, table_x, base, sum_x, count_x, count_y, pad_x, scale_x)
    (gradient,) = back_y(column_y, table_y, partial, half, None, count_y, count_x, pad_y, scale_y)
    gradient, residual_y = back_y(column_y, table_y, partial, half, (other, gradient), count_y, count_x, pad_y, scale_y)
    return (gradient, residual_x, residual_y)


def solution(mesh):
    return jax.shard_map(
        steps,
        mesh=mesh,
        in_specs=(P("pa", "gx", "gy"), P(), P(None, "pa", "gy"), P(None, "pa", "gx")),
        out_specs=(P("pa", "gx", "gy"), P(None, "pa", "gy"), P(None, "pa", "gx")),
        check_vma=False,
    )
```

```python
import jax
import jax.numpy as jnp
from jax import lax
from jax.experimental import pallas as pl
from jax.experimental.pallas import tpu as pltpu
from jax.sharding import PartitionSpec as P


LEVELS = 16
RING = 8
CHUNKS = 2
LIMIT = pltpu.CompilerParams(vmem_limit_bytes=8 * 1024 * 1024)
SMEM = pltpu.SMEM
VMEM = pltpu.VMEM
F32 = jnp.float32
BF16 = jnp.bfloat16


def interpreted():
    return False


def fill(slopes_ref, family, shape, dim):
    views = slopes_ref.shape[1]
    view = lax.broadcasted_iota(jnp.int32, shape, dim) % views
    slopes = jnp.zeros(shape, jnp.int32)
    for v in range(views):
        slopes = jnp.where(view == v, slopes_ref[family, v], slopes)
    return slopes


def tiled(value, width):
    return jnp.concatenate([value] * (width // value.shape[1]), axis=1)


def lowest_shift(slopes, block, blocks):
    return slopes * (block - blocks // 2) + jnp.minimum(slopes, 0)


def tiles_of(value):
    return [value[:, k : k + 128] for k in range(0, value.shape[1], 128)]


def shifted(tiles, amount, count):
    if amount == 0:
        return tiles[:count]
    lane = lax.broadcasted_iota(jnp.int32, tiles[0].shape, 1)
    rolled = [None if tile is None else pltpu.roll(tile, amount, 1) for tile in tiles]
    out = []
    for k in range(count):
        here, before = rolled[k], rolled[k - 1]
        if here is None and before is None:
            out.append(None)
        elif here is None:
            out.append(jnp.where(lane < amount, before, 0.0))
        elif before is None:
            out.append(jnp.where(lane < amount, 0.0, here))
        else:
            out.append(jnp.where(lane < amount, before, here))
    return out


def barrel(tiles, amounts):
    lane = lax.broadcasted_iota(jnp.int32, amounts.shape, 1)
    low = amounts & 127
    source = (lane - amounts) & 127
    zero = jnp.zeros(amounts.shape, F32)
    turned = [zero if tile is None else jnp.take_along_axis(tile, source, axis=1) for tile in tiles]
    near = [jnp.where(lane < low, turned[k - 1], turned[k]) for k in range(len(tiles))]
    return [jnp.where(amounts >= 128, near[k - 1], near[k]) for k in range(len(tiles))]


def offsets(slopes, block, blocks, cells):
    views = slopes.shape[0]
    lowest = tiled(lowest_shift(slopes, block, blocks).astype(F32), cells)
    cell = lax.broadcasted_iota(jnp.int32, (views, cells), 1) + (block * cells - blocks * cells // 2)
    return tiled(slopes.astype(F32), cells) * (cell.astype(F32) * (1.0 / cells)) - lowest


def hat(offset, level):
    return jnp.maximum(1.0 - jnp.abs(offset - level), 0.0)


def in_vmem(value):
    if interpreted():
        return value
    return pltpu.with_memory_space_constraint(value, VMEM)


def in_hbm(value):
    if interpreted():
        return value
    return pltpu.with_memory_space_constraint(value, pltpu.HBM)


def out_vmem(shape, dtype):
    if interpreted():
        return jax.ShapeDtypeStruct(shape, dtype)
    return VMEM(shape, dtype)


def anywhere():
    return pl.BlockSpec(memory_space=pltpu.HBM)


def vmem():
    return pl.BlockSpec(memory_space=VMEM)


def in_roles(value, odd):
    edge = value.shape[1] // 3
    lead, mid, trail = value[:, :edge], value[:, edge : 2 * edge], value[:, 2 * edge :]
    return jnp.concatenate([jnp.where(odd, lead, trail), mid, jnp.where(odd, trail, lead)], axis=1)


def from_roles(value, odd):
    edge = value.shape[1] // 3
    a, mid, b = value[:, :edge], value[:, edge : 2 * edge], value[:, 2 * edge :]
    return jnp.concatenate([jnp.where(odd, a, b), mid, jnp.where(odd, b, a)], axis=1)


def on_grid(value):
    return jnp.round(value * 32768.0) * (1.0 / 32768.0)


def project(table_ref, volume_ref, rows_ref, slopes, out_ref, family, block, blocks, odd, pad, scale):
    planes = volume_ref.shape[0]
    views = slopes.shape[0]
    bins = volume_ref.shape[2 - family]
    width = out_ref.shape[1]
    first = (block == 0).astype(F32)
    amounts = pad - LEVELS + 1 - lowest_shift(slopes, block, blocks)
    count = width // 128
    data = bins // 128
    for plane in range(planes):
        dims = (((1,), (family,)), ((), ()))
        summands = lax.dot_general(table_ref[...], volume_ref[plane], dims, preferred_element_type=F32)
        total = [None] * count
        for level in range(LEVELS):
            piece = tiles_of(summands[level * views : (level + 1) * views, :]) + [None] * (count - data)
            piece = shifted(piece, LEVELS - 1 - level, count)
            total = [p if t is None else t if p is None else t + p for t, p in zip(total, piece)]
        total = jnp.concatenate(barrel(total, amounts), axis=1) * scale
        known = tiles_of(rows_ref[plane * views : (plane + 1) * views, :] * first) + [None] * (count - data)
        known = [None] * (pad // 128) + shifted(known, pad % 128, count - pad // 128)
        known = jnp.concatenate([jnp.zeros((views, 128), F32) if k is None else k for k in known], axis=1)
        total = on_grid(total - known)
        out_ref[plane * views : (plane + 1) * views, :] = in_roles(total, odd)


def build_table(slopes, block, blocks, cells, table_ref):
    views = slopes.shape[0]
    offset = offsets(slopes, block, blocks, cells)
    for level in range(LEVELS):
        table_ref[level * views : (level + 1) * views, :] = hat(offset, float(level)).astype(BF16)


def gather_rows(measured_ref, rows_ref):
    views, planes, _ = measured_ref.shape
    for plane in range(planes):
        for v in range(views):
            rows_ref[plane * views + v : plane * views + v + 1, :] = measured_ref[v, plane : plane + 1, :]


def forward_kernel(
    slopes_hbm, volume_hbm, mx_hbm, my_hbm,
    x_ref, y_ref, table_y_ref, near_ref, volume_ref, column_x_ref, column_y_ref, lane_ref,
    table_x_ref, slopes_ref, mx_ref, my_ref, rows_x_ref, rows_y_ref, sems,
    *, count_x, count_y, pad_x, pad_y, scale_x, scale_y,
):
    _, cells_x, cells_y = volume_ref.shape
    fetches = [
        pltpu.make_async_copy(slopes_hbm, slopes_ref, sems.at[0]),
        pltpu.make_async_copy(volume_hbm, volume_ref, sems.at[1]),
        pltpu.make_async_copy(mx_hbm, mx_ref, sems.at[2]),
        pltpu.make_async_copy(my_hbm, my_ref, sems.at[3]),
        pltpu.make_async_copy(volume_hbm.at[pl.ds(1 - lax.axis_index("pa"), 1)], near_ref, sems.at[4]),
    ]
    for fetch in fetches:
        fetch.start()
    here_x, here_y = lax.axis_index("gx"), lax.axis_index("gy")
    fetches[0].wait()
    column_x = fill(slopes_ref, 0, column_x_ref.shape, 0)
    column_y = fill(slopes_ref, 1, column_y_ref.shape, 0)
    column_x_ref[...] = column_x
    column_y_ref[...] = column_y
    lane_ref[...] = fill(slopes_ref, 0, lane_ref.shape, 1)
    build_table(column_y, here_y, count_y, cells_y, table_y_ref)
    build_table(column_x, here_x, count_x, cells_x, table_x_ref)
    fetches[2].wait()
    fetches[3].wait()
    gather_rows(mx_ref, rows_x_ref)
    gather_rows(my_ref, rows_y_ref)
    fetches[1].wait()
    project(table_y_ref, volume_ref, rows_y_ref, column_y, y_ref, 1, here_y, count_y, here_x % 2 == 1, pad_y, scale_y)
    project(table_x_ref, volume_ref, rows_x_ref, column_x, x_ref, 0, here_x, count_x, here_y % 2 == 1, pad_x, scale_x)
    fetches[4].wait()


def forward(slopes, volume, measured_x, measured_y, count_x, count_y, pad_x, pad_y, scale_x, scale_y):
    views = slopes.shape[1]
    planes, cells_x, cells_y = volume.shape

    def body(*refs):
        forward_kernel(
            *refs, count_x=count_x, count_y=count_y, pad_x=pad_x, pad_y=pad_y, scale_x=scale_x, scale_y=scale_y
        )

    return pl.pallas_call(
        body,
        out_shape=(
            out_vmem((planes * views, cells_y + 2 * pad_x), F32),
            out_vmem((planes * views, cells_x + 2 * pad_y), F32),
            out_vmem((LEVELS * views, cells_y), BF16),
            out_vmem((1,) + volume.shape[1:], BF16),
            out_vmem(volume.shape, BF16),
            out_vmem((views, 128), jnp.int32),
            out_vmem((views, 128), jnp.int32),
            out_vmem((8, LEVELS * views), jnp.int32),
        ),
        in_specs=[anywhere()] * 4,
        out_specs=(vmem(),) * 8,
        scratch_shapes=[
            VMEM((LEVELS * views, cells_x), BF16),
            SMEM(slopes.shape, jnp.int32),
            VMEM(measured_x.shape, F32),
            VMEM(measured_y.shape, F32),
            VMEM((planes * views, cells_y), F32),
            VMEM((planes * views, cells_x), F32),
            pltpu.SemaphoreType.DMA((5,)),
        ],
        compiler_params=LIMIT,
        interpret=interpreted(),
        name="forward",
    )(*(in_hbm(value) for value in (slopes, volume, measured_x, measured_y)))


def half_of(index):
    return ((index + 1) // 2) % 2


def spread_into(value, slopes, block, blocks, other, others, pad, scale, spread_ref):
    views, width = value.shape
    bins = width - 2 * pad
    place = lax.broadcasted_iota(jnp.int32, (views, width), 1)
    inside = (place >= jnp.where(other == 0, pad, 0)) & (place < jnp.where(other == others - 1, pad + bins, width))
    value = jnp.where(inside, value * scale, 0.0).astype(BF16).astype(F32)
    tiles = barrel(tiles_of(value), lowest_shift(slopes, block, blocks) + pad)
    skip = 2 * pad // 128
    tiles = tiles[skip:] + tiles[:skip]
    for level in range(LEVELS):
        piece = jnp.concatenate(shifted(tiles, level, bins // 128), axis=1)
        spread_ref[level * views : (level + 1) * views, :] = piece.astype(BF16)


def middle(value, pad):
    tiles = tiles_of(value)
    skip = pad // 128
    tiles = tiles[skip:] + tiles[:skip]
    count = (value.shape[1] - 2 * pad) // 128
    if pad % 128 == 0:
        return jnp.concatenate(tiles[:count], axis=1)
    tiles = tiles[1:] + tiles[:1]
    return jnp.concatenate(shifted(tiles, 128 - pad % 128, count), axis=1)


def prepare_kernel(lane_ref, volume_ref, beside_ref, table_ref, base_ref, *, blocks):
    planes, cells, _ = volume_ref.shape
    block, band = lax.axis_index("gx"), lax.axis_index("pa")
    slopes = lane_ref[...]
    views = slopes.shape[1] // LEVELS
    level = lax.broadcasted_iota(jnp.int32, slopes.shape, 1) // views
    base = (lowest_shift(slopes, block, blocks) + level).astype(F32)[:1]
    slopes = slopes.astype(F32)[:1]
    shape = (cells, LEVELS * views)
    cell = lax.broadcasted_iota(jnp.int32, shape, 0).astype(F32) * (1.0 / cells) + (block - blocks // 2).astype(F32)
    table_ref[...] = jnp.maximum(1.0 - jnp.abs(cell * slopes - base), 0.0).astype(BF16)
    for plane in range(planes):
        here = volume_ref[plane].astype(F32)
        beside = beside_ref[0].astype(F32) * (band == 1 - plane).astype(F32)
        within = volume_ref[1 - plane].astype(F32)
        base_ref[plane] = 0.02 * (2.0 * here - beside - within)


def prepare(lane, volume, beside, blocks):
    def body(*refs):
        prepare_kernel(*refs, blocks=blocks)

    return pl.pallas_call(
        body,
        out_shape=(out_vmem((volume.shape[1], lane.shape[1]), BF16), out_vmem(volume.shape, F32)),
        in_specs=[vmem()] * 3,
        out_specs=(vmem(), vmem()),
        compiler_params=LIMIT,
        interpret=interpreted(),
        name="prepare",
    )(*(in_vmem(value) for value in (lane, volume, beside)))


def back_x_kernel(column_ref, table_ref, base_ref, residual_ref, out_ref, rest_hbm, spread_ref, rows_ref, rest_ref, sem, *, blocks, others, pad, scale):
    planes, _, _ = base_ref.shape
    views = column_ref.shape[0]
    block, other = lax.axis_index("gx"), lax.axis_index("gy")
    column = column_ref[...]
    residuals = [from_roles(residual_ref[p * views : (p + 1) * views, :], other % 2 == 1) for p in range(planes)]
    for plane in range(planes):
        rows_ref[plane * views : (plane + 1) * views, :] = middle(residuals[plane], pad)
    for plane in range(planes):
        for v in range(views):
            rest_ref[v, plane : plane + 1, :] = rows_ref[plane * views + v : plane * views + v + 1, :]
    store = pltpu.make_async_copy(rest_ref, rest_hbm, sem)
    store.start()
    for plane in range(planes):
        spread_into(residuals[plane], column, block, blocks, other, others, pad, scale, spread_ref)
        out_ref[plane] = base_ref[plane] + jnp.dot(table_ref[...], spread_ref[...], preferred_element_type=F32)
    store.wait()


def back_x(column, table, base, residual, blocks, others, pad, scale):
    planes, _, bins = base.shape
    views = column.shape[0]

    def body(*refs):
        back_x_kernel(*refs, blocks=blocks, others=others, pad=pad, scale=scale)

    return pl.pallas_call(
        body,
        out_shape=(out_vmem(base.shape, F32), jax.ShapeDtypeStruct((views, planes, bins), F32)),
        in_specs=[vmem()] * 4,
        out_specs=(vmem(), anywhere()),
        scratch_shapes=[
            VMEM((LEVELS * views, bins), BF16),
            VMEM((planes * views, bins), F32),
            VMEM((views, planes, bins), F32),
            pltpu.SemaphoreType.DMA,
        ],
        compiler_params=LIMIT,
        interpret=interpreted(),
        name="back_x",
    )(*(in_vmem(value) for value in (column, table, base, residual)))


def back_y_kernel(*refs, last, blocks, others, pad, scale, views):
    column_ref, table_ref, partial_ref, half_ref = refs[:4]
    rest = list(refs[4:])
    if last:
        other_ref = rest.pop(0)
        rest.pop(0)
        rest_hbm = rest.pop(1)
        rest_ref = rest.pop()
    out_hbm, sum_ref, spread_ref, rows_ref, sems = rest
    block, other = lax.axis_index("gy"), lax.axis_index("gx")
    mine = half_of(lax.axis_index("gy"))
    flip = other % 2 == 1
    plane = 1 - mine if last else mine
    value = from_roles(other_ref[...] if last else half_ref[...], flip)
    spread_into(value, column_ref[...], block, blocks, other, others, pad, scale, spread_ref)
    dims = (((0,), (0,)), ((), ()))
    stores = []
    rows = sum_ref.shape[1] // CHUNKS
    for c in range(CHUNKS):
        part = pl.ds(c * rows, rows)
        back = lax.dot_general(spread_ref[:, c * rows : (c + 1) * rows], table_ref[...], dims, preferred_element_type=F32)
        sum_ref[:, part, :] = partial_ref[pl.ds(plane, 1), part, :] + back[None]
        store = pltpu.make_async_copy(sum_ref.at[:, part], out_hbm.at[pl.ds(plane, 1), part], sems.at[1 + c])
        store.start()
        stores.append(store)
    if last:
        odd = mine == 1
        rows_ref[:views, :] = middle(from_roles(jnp.where(odd, other_ref[...], half_ref[...]), flip), pad)
        rows_ref[views:, :] = middle(from_roles(jnp.where(odd, half_ref[...], other_ref[...]), flip), pad)
        for p in range(2):
            for v in range(views):
                rest_ref[v, p : p + 1, :] = rows_ref[p * views + v : p * views + v + 1, :]
        also = pltpu.make_async_copy(rest_ref, rest_hbm, sems.at[0])
        also.start()
        also.wait()
    for store in stores:
        store.wait()


def back_y(column, table, partial, half, rest, blocks, others, pad, scale):
    planes, bins, cells = partial.shape
    views = column.shape[0]
    last = rest is not None

    def body(*refs):
        back_y_kernel(*refs, last=last, blocks=blocks, others=others, pad=pad, scale=scale, views=views)

    operands = [in_vmem(column), in_vmem(table), in_vmem(partial), in_vmem(half)]
    specs = [vmem()] * 4
    shapes = [jax.ShapeDtypeStruct(partial.shape, F32)]
    out_specs = [anywhere()]
    aliases = {}
    if last:
        other, gradient = rest
        operands += [in_vmem(other), gradient]
        specs += [vmem(), anywhere()]
        shapes.append(jax.ShapeDtypeStruct((views, planes, bins), F32))
        out_specs.append(anywhere())
        aliases = {5: 0}
    scratch = [
        VMEM((1, bins, cells), F32),
        VMEM((LEVELS * views, bins), BF16),
        VMEM((planes * views, bins), F32),
        pltpu.SemaphoreType.DMA((1 + CHUNKS,)),
    ]
    if last:
        scratch.append(VMEM((views, planes, bins), F32))
    return pl.pallas_call(
        body,
        out_shape=tuple(shapes),
        in_specs=specs,
        out_specs=tuple(out_specs),
        scratch_shapes=scratch,
        input_output_aliases=aliases,
        compiler_params=LIMIT,
        interpret=interpreted(),
        name="back_y_last" if last else "back_y_own",
    )(*operands)


def exchange(value, axis, partner):
    return lax.ppermute(value, axis, [(i, partner(i)) for i in range(lax.axis_size(axis))])


def twin(i):
    return i ^ 1


def odd_twin(i):
    return i - i % RING + (i + (1 if i % 2 else -1)) % RING


def across(i):
    return i - i % RING + (i + (-3 if i % 2 else 3)) % RING


def at_end(size, axis):
    index = lax.axis_index(axis) % size
    return (index == 0) | (index == size - 1)


def steps(volume, view_slopes, measured_x, measured_y):
    _, cells_x, cells_y = volume.shape
    count_x = lax.axis_size("gx")
    count_y = lax.axis_size("gy")
    scale_x = float(cells_x * count_x) ** (-0.5)
    scale_y = float(cells_y * count_y) ** (-0.5)
    pad_x, pad_y = 64, 128

    sum_x, sum_y, table_y, near, volume, column_x, column_y, lane = forward(
        view_slopes, volume, measured_x, measured_y, count_x, count_y, pad_x, pad_y, scale_x, scale_y
    )
    wide = sum_x.shape[1]
    edge_x, edge_y = wide // 3, sum_y.shape[1] // 3
    y_a, y_mid, y_b = sum_y[:, :edge_y], sum_y[:, edge_y : 2 * edge_y], sum_y[:, 2 * edge_y :]

    got = exchange(jnp.concatenate([sum_x, y_a], axis=1), "gx", twin)
    beside = lax.ppermute(near, "pa", [(0, 1), (1, 0)])
    sum_x, y_a = sum_x + got[:, :wide], y_a + got[:, wide:]
    got = exchange(jnp.concatenate([sum_x, y_b], axis=1), "gx", odd_twin)
    sum_x, y_b = sum_x + got[:, :wide], y_b + jnp.where(at_end(count_x, "gx"), 0.0, got[:, wide:])
    sum_y = jnp.concatenate([y_a, y_mid, y_b], axis=1)
    x_a, x_mid, x_b = sum_x[:, :edge_x], sum_x[:, edge_x : 2 * edge_x], sum_x[:, 2 * edge_x :]

    rows = sum_y.shape[0] // 2
    long = sum_y.shape[1]
    owns = half_of(lax.axis_index("gy")) == 0
    kept = jnp.where(owns, sum_y[:rows], sum_y[rows:])
    sent = jnp.where(owns, sum_y[rows:], sum_y[:rows])
    got = exchange(jnp.concatenate([sent, x_a[:rows], x_a[rows:]], axis=1), "gy", twin)
    half = kept + got[:, :long]
    x_a = x_a + jnp.concatenate([got[:, long : long + edge_x], got[:, long + edge_x :]], axis=0)
    got = exchange(jnp.concatenate([half, x_b[:rows], x_b[rows:]], axis=1), "gy", lambda i: i ^ RING)
    half = half + got[:, :long]
    sent_b = jnp.where(at_end(RING, "gy"), got[:, long:], jnp.concatenate([x_b[:rows], x_b[rows:]], axis=1))
    got = exchange(jnp.concatenate([half, sent_b], axis=1), "gy", odd_twin)
    half = half + got[:, :long]
    got = jnp.where(at_end(count_y, "gy"), 0.0, got)
    half, x_b, got = lax.optimization_barrier((half, x_b, got))
    x_b = x_b + jnp.concatenate([got[:, long : long + edge_x], got[:, long + edge_x :]], axis=0)
    sum_x = jnp.concatenate([x_a, x_mid, x_b], axis=1)

    half = half + exchange(half, "gy", across)
    sum_x = sum_x + exchange(sum_x, "gx", across)
    other = exchange(half, "gy", twin)

    table_x, base = prepare(lane, volume, beside, count_x)
    partial, residual_x = back_x(column_x, table_x, base, sum_x, count_x, count_y, pad_x, scale_x)
    (gradient,) = back_y(column_y, table_y, partial, half, None, count_y, count_x, pad_y, scale_y)
    gradient, residual_y = back_y(column_y, table_y, partial, half, (other, gradient), count_y, count_x, pad_y, scale_y)
    return (gradient, residual_x, residual_y)


def solution(mesh):
    return jax.shard_map(
        steps,
        mesh=mesh,
        in_specs=(P("pa", "gx", "gy"), P(), P(None, "pa", "gy"), P(None, "pa", "gx")),
        out_specs=(P("pa", "gx", "gy"), P(None, "pa", "gy"), P(None, "pa", "gx")),
        check_vma=False,
    )
```

```python
import jax
import jax.numpy as jnp
from jax import lax
from jax.experimental import pallas as pl
from jax.experimental.pallas import tpu as pltpu
from jax.sharding import PartitionSpec as P


LEVELS = 16
RING = 8
CHUNKS = 2
LIMIT = pltpu.CompilerParams(vmem_limit_bytes=8 * 1024 * 1024)
SMEM = pltpu.SMEM
VMEM = pltpu.VMEM
F32 = jnp.float32
BF16 = jnp.bfloat16


def interpreted():
    return False


def fill(slopes_ref, family, shape, dim):
    views = slopes_ref.shape[1]
    view = lax.broadcasted_iota(jnp.int32, shape, dim) % views
    slopes = jnp.zeros(shape, jnp.int32)
    for v in range(views):
        slopes = jnp.where(view == v, slopes_ref[family, v], slopes)
    return slopes


def tiled(value, width):
    return jnp.concatenate([value] * (width // value.shape[1]), axis=1)


def lowest_shift(slopes, block, blocks):
    return slopes * (block - blocks // 2) + jnp.minimum(slopes, 0)


def tiles_of(value):
    return [value[:, k : k + 128] for k in range(0, value.shape[1], 128)]


def shifted(tiles, amount, count):
    if amount == 0:
        return tiles[:count]
    lane = lax.broadcasted_iota(jnp.int32, tiles[0].shape, 1)
    rolled = [None if tile is None else pltpu.roll(tile, amount, 1) for tile in tiles]
    out = []
    for k in range(count):
        here, before = rolled[k], rolled[k - 1]
        if here is None and before is None:
            out.append(None)
        elif here is None:
            out.append(jnp.where(lane < amount, before, 0.0))
        elif before is None:
            out.append(jnp.where(lane < amount, 0.0, here))
        else:
            out.append(jnp.where(lane < amount, before, here))
    return out


def barrel(tiles, amounts):
    lane = lax.broadcasted_iota(jnp.int32, amounts.shape, 1)
    low = amounts & 127
    source = (lane - amounts) & 127
    zero = jnp.zeros(amounts.shape, F32)
    turned = [zero if tile is None else jnp.take_along_axis(tile, source, axis=1) for tile in tiles]
    near = [jnp.where(lane < low, turned[k - 1], turned[k]) for k in range(len(tiles))]
    return [jnp.where(amounts >= 128, near[k - 1], near[k]) for k in range(len(tiles))]


def offsets(slopes, block, blocks, cells):
    views = slopes.shape[0]
    lowest = tiled(lowest_shift(slopes, block, blocks).astype(F32), cells)
    cell = lax.broadcasted_iota(jnp.int32, (views, cells), 1) + (block * cells - blocks * cells // 2)
    return tiled(slopes.astype(F32), cells) * (cell.astype(F32) * (1.0 / cells)) - lowest


def hat(offset, level):
    return jnp.maximum(1.0 - jnp.abs(offset - level), 0.0)


def in_vmem(value):
    if interpreted():
        return value
    return pltpu.with_memory_space_constraint(value, VMEM)


def in_hbm(value):
    if interpreted():
        return value
    return pltpu.with_memory_space_constraint(value, pltpu.HBM)


def out_vmem(shape, dtype):
    if interpreted():
        return jax.ShapeDtypeStruct(shape, dtype)
    return VMEM(shape, dtype)


def anywhere():
    return pl.BlockSpec(memory_space=pltpu.HBM)


def vmem():
    return pl.BlockSpec(memory_space=VMEM)


def in_roles(value, odd):
    edge = value.shape[1] // 3
    lead, mid, trail = value[:, :edge], value[:, edge : 2 * edge], value[:, 2 * edge :]
    return jnp.concatenate([jnp.where(odd, lead, trail), mid, jnp.where(odd, trail, lead)], axis=1)


def from_roles(value, odd):
    edge = value.shape[1] // 3
    a, mid, b = value[:, :edge], value[:, edge : 2 * edge], value[:, 2 * edge :]
    return jnp.concatenate([jnp.where(odd, a, b), mid, jnp.where(odd, b, a)], axis=1)


def on_grid(value):
    return jnp.round(value * 32768.0) * (1.0 / 32768.0)


def project(table_ref, volume_ref, rows_ref, slopes, out_ref, family, block, blocks, odd, pad, scale):
    planes = volume_ref.shape[0]
    views = slopes.shape[0]
    bins = volume_ref.shape[2 - family]
    width = out_ref.shape[1]
    first = (block == 0).astype(F32)
    amounts = pad - LEVELS + 1 - lowest_shift(slopes, block, blocks)
    count = width // 128
    data = bins // 128
    for plane in range(planes):
        dims = (((1,), (family,)), ((), ()))
        summands = lax.dot_general(table_ref[...], volume_ref[plane], dims, preferred_element_type=F32)
        total = [None] * count
        for level in range(LEVELS):
            piece = tiles_of(summands[level * views : (level + 1) * views, :]) + [None] * (count - data)
            piece = shifted(piece, LEVELS - 1 - level, count)
            total = [p if t is None else t if p is None else t + p for t, p in zip(total, piece)]
        total = jnp.concatenate(barrel(total, amounts), axis=1) * scale
        known = tiles_of(rows_ref[plane * views : (plane + 1) * views, :] * first) + [None] * (count - data)
        known = [None] * (pad // 128) + shifted(known, pad % 128, count - pad // 128)
        known = jnp.concatenate([jnp.zeros((views, 128), F32) if k is None else k for k in known], axis=1)
        total = on_grid(total - known)
        out_ref[plane * views : (plane + 1) * views, :] = in_roles(total, odd)


def build_table(slopes, block, blocks, cells, table_ref):
    views = slopes.shape[0]
    offset = offsets(slopes, block, blocks, cells)
    for level in range(LEVELS):
        table_ref[level * views : (level + 1) * views, :] = hat(offset, float(level)).astype(BF16)


def gather_rows(measured_ref, rows_ref):
    views, planes, _ = measured_ref.shape
    for plane in range(planes):
        for v in range(views):
            rows_ref[plane * views + v : plane * views + v + 1, :] = measured_ref[v, plane : plane + 1, :]


def forward_kernel(
    slopes_hbm, volume_hbm, mx_hbm, my_hbm,
    x_ref, y_ref, table_y_ref, near_ref, volume_ref, column_x_ref, column_y_ref, lane_ref,
    table_x_ref, slopes_ref, mx_ref, my_ref, rows_x_ref, rows_y_ref, sems,
    *, count_x, count_y, pad_x, pad_y, scale_x, scale_y,
):
    _, cells_x, cells_y = volume_ref.shape
    fetches = [
        pltpu.make_async_copy(slopes_hbm, slopes_ref, sems.at[0]),
        pltpu.make_async_copy(volume_hbm, volume_ref, sems.at[1]),
        pltpu.make_async_copy(mx_hbm, mx_ref, sems.at[2]),
        pltpu.make_async_copy(my_hbm, my_ref, sems.at[3]),
        pltpu.make_async_copy(volume_hbm.at[pl.ds(1 - lax.axis_index("pa"), 1)], near_ref, sems.at[4]),
    ]
    for fetch in fetches:
        fetch.start()
    here_x, here_y = lax.axis_index("gx"), lax.axis_index("gy")
    fetches[0].wait()
    column_x = fill(slopes_ref, 0, column_x_ref.shape, 0)
    column_y = fill(slopes_ref, 1, column_y_ref.shape, 0)
    column_x_ref[...] = column_x
    column_y_ref[...] = column_y
    lane_ref[...] = fill(slopes_ref, 0, lane_ref.shape, 1)
    build_table(column_y, here_y, count_y, cells_y, table_y_ref)
    build_table(column_x, here_x, count_x, cells_x, table_x_ref)
    fetches[2].wait()
    fetches[3].wait()
    gather_rows(mx_ref, rows_x_ref)
    gather_rows(my_ref, rows_y_ref)
    fetches[1].wait()
    project(table_y_ref, volume_ref, rows_y_ref, column_y, y_ref, 1, here_y, count_y, here_x % 2 == 1, pad_y, scale_y)
    project(table_x_ref, volume_ref, rows_x_ref, column_x, x_ref, 0, here_x, count_x, here_y % 2 == 1, pad_x, scale_x)
    fetches[4].wait()


def forward(slopes, volume, measured_x, measured_y, count_x, count_y, pad_x, pad_y, scale_x, scale_y):
    views = slopes.shape[1]
    planes, cells_x, cells_y = volume.shape

    def body(*refs):
        forward_kernel(
            *refs, count_x=count_x, count_y=count_y, pad_x=pad_x, pad_y=pad_y, scale_x=scale_x, scale_y=scale_y
        )

    return pl.pallas_call(
        body,
        out_shape=(
            out_vmem((planes * views, cells_y + 2 * pad_x), F32),
            out_vmem((planes * views, cells_x + 2 * pad_y), F32),
            out_vmem((LEVELS * views, cells_y), BF16),
            out_vmem((1,) + volume.shape[1:], BF16),
            out_vmem(volume.shape, BF16),
            out_vmem((views, 128), jnp.int32),
            out_vmem((views, 128), jnp.int32),
            out_vmem((8, LEVELS * views), jnp.int32),
        ),
        in_specs=[anywhere()] * 4,
        out_specs=(vmem(),) * 8,
        scratch_shapes=[
            VMEM((LEVELS * views, cells_x), BF16),
            SMEM(slopes.shape, jnp.int32),
            VMEM(measured_x.shape, F32),
            VMEM(measured_y.shape, F32),
            VMEM((planes * views, cells_y), F32),
            VMEM((planes * views, cells_x), F32),
            pltpu.SemaphoreType.DMA((5,)),
        ],
        compiler_params=LIMIT,
        interpret=interpreted(),
        name="forward",
    )(*(in_hbm(value) for value in (slopes, volume, measured_x, measured_y)))


def half_of(index):
    return ((index + 1) // 2) % 2


def spread_into(value, slopes, block, blocks, other, others, pad, scale, spread_ref):
    views, width = value.shape
    bins = width - 2 * pad
    place = lax.broadcasted_iota(jnp.int32, (views, width), 1)
    inside = (place >= jnp.where(other == 0, pad, 0)) & (place < jnp.where(other == others - 1, pad + bins, width))
    value = jnp.where(inside, value * scale, 0.0).astype(BF16).astype(F32)
    tiles = barrel(tiles_of(value), lowest_shift(slopes, block, blocks) + pad)
    skip = 2 * pad // 128
    tiles = tiles[skip:] + tiles[:skip]
    for level in range(LEVELS):
        piece = jnp.concatenate(shifted(tiles, level, bins // 128), axis=1)
        spread_ref[level * views : (level + 1) * views, :] = piece.astype(BF16)


def middle(value, pad):
    tiles = tiles_of(value)
    skip = pad // 128
    tiles = tiles[skip:] + tiles[:skip]
    count = (value.shape[1] - 2 * pad) // 128
    if pad % 128 == 0:
        return jnp.concatenate(tiles[:count], axis=1)
    tiles = tiles[1:] + tiles[:1]
    return jnp.concatenate(shifted(tiles, 128 - pad % 128, count), axis=1)


def prepare_kernel(lane_ref, volume_ref, beside_ref, table_ref, base_ref, *, blocks):
    planes, cells, _ = volume_ref.shape
    block, band = lax.axis_index("gx"), lax.axis_index("pa")
    slopes = lane_ref[...]
    views = slopes.shape[1] // LEVELS
    level = lax.broadcasted_iota(jnp.int32, slopes.shape, 1) // views
    base = (lowest_shift(slopes, block, blocks) + level).astype(F32)[:1]
    slopes = slopes.astype(F32)[:1]
    shape = (cells, LEVELS * views)
    cell = lax.broadcasted_iota(jnp.int32, shape, 0).astype(F32) * (1.0 / cells) + (block - blocks // 2).astype(F32)
    table_ref[...] = jnp.maximum(1.0 - jnp.abs(cell * slopes - base), 0.0).astype(BF16)
    for plane in range(planes):
        here = volume_ref[plane].astype(F32)
        beside = beside_ref[0].astype(F32) * (band == 1 - plane).astype(F32)
        within = volume_ref[1 - plane].astype(F32)
        base_ref[plane] = 0.02 * (2.0 * here - beside - within)


def prepare(lane, volume, beside, blocks):
    def body(*refs):
        prepare_kernel(*refs, blocks=blocks)

    return pl.pallas_call(
        body,
        out_shape=(out_vmem((volume.shape[1], lane.shape[1]), BF16), out_vmem(volume.shape, F32)),
        in_specs=[vmem()] * 3,
        out_specs=(vmem(), vmem()),
        compiler_params=LIMIT,
        interpret=interpreted(),
        name="prepare",
    )(*(in_vmem(value) for value in (lane, volume, beside)))


def store_rows(values, rest_ref, rows_ref):
    planes, views = len(values), rest_ref.shape[0]
    for plane in range(planes):
        rows_ref[plane * views : (plane + 1) * views, :] = values[plane]
    for plane in range(planes):
        for v in range(views):
            rest_ref[v, plane : plane + 1, :] = rows_ref[plane * views + v : plane * views + v + 1, :]


def back_own_kernel(column_ref, table_ref, half_ref, out_ref, spread_ref, *, blocks, others, pad, scale):
    block, other = lax.axis_index("gy"), lax.axis_index("gx")
    value = from_roles(half_ref[...], other % 2 == 1)
    spread_into(value, column_ref[...], block, blocks, other, others, pad, scale, spread_ref)
    dims = (((0,), (0,)), ((), ()))
    out_ref[...] = lax.dot_general(spread_ref[...], table_ref[...], dims, preferred_element_type=F32)


def back_own(column, table, half, bins, blocks, others, pad, scale):
    def body(*refs):
        back_own_kernel(*refs, blocks=blocks, others=others, pad=pad, scale=scale)

    return pl.pallas_call(
        body,
        out_shape=out_vmem((bins, table.shape[1]), F32),
        in_specs=[vmem()] * 3,
        out_specs=vmem(),
        scratch_shapes=[VMEM((table.shape[0], bins), BF16)],
        compiler_params=LIMIT,
        interpret=interpreted(),
        name="back_own",
    )(*(in_vmem(value) for value in (column, table, half)))


def back_x_kernel(
    column_ref, table_ref, base_ref, residual_ref, own_ref, out_hbm, rest_hbm, partial_ref,
    spread_ref, sum_ref, rows_ref, rest_ref, sems, *, blocks, others, pad, scale,
):
    planes, cells, _ = base_ref.shape
    views = column_ref.shape[0]
    block, other = lax.axis_index("gx"), lax.axis_index("gy")
    column = column_ref[...]
    flip = other % 2 == 1
    mine = half_of(other)
    size = cells // CHUNKS
    copies = []
    for last in range(planes):
        plane = 1 - mine if last else mine
        start = pl.multiple_of(plane * views, views)
        residual = from_roles(residual_ref[pl.ds(start, views), :], flip)
        spread_into(residual, column, block, blocks, other, others, pad, scale, spread_ref)
        for c in range(CHUNKS):
            part = pl.ds(c * size, size)
            value = jnp.dot(table_ref[part, :], spread_ref[...], preferred_element_type=F32)
            value = base_ref[pl.ds(plane, 1), part, :] + value[None]
            if last:
                partial_ref[part, :] = value[0]
            else:
                sum_ref[:, part, :] = value + own_ref[part, :][None]
                copies.append(
                    pltpu.make_async_copy(sum_ref.at[:, part], out_hbm.at[pl.ds(plane, 1), part], sems.at[1 + c])
                )
                copies[-1].start()
    residuals = [from_roles(residual_ref[p * views : (p + 1) * views, :], flip) for p in range(planes)]
    store_rows([middle(residual, pad) for residual in residuals], rest_ref, rows_ref)
    copies.append(pltpu.make_async_copy(rest_ref, rest_hbm, sems.at[0]))
    copies[-1].start()
    for copy in copies:
        copy.wait()


def back_x(column, table, base, residual, own, blocks, others, pad, scale):
    planes, cells, bins = base.shape
    views = column.shape[0]

    def body(*refs):
        back_x_kernel(*refs, blocks=blocks, others=others, pad=pad, scale=scale)

    return pl.pallas_call(
        body,
        out_shape=(
            jax.ShapeDtypeStruct(base.shape, F32),
            jax.ShapeDtypeStruct((views, planes, bins), F32),
            out_vmem((cells, bins), F32),
        ),
        in_specs=[vmem()] * 5,
        out_specs=(anywhere(), anywhere(), vmem()),
        scratch_shapes=[
            VMEM((LEVELS * views, bins), BF16),
            VMEM((1, cells, bins), F32),
            VMEM((planes * views, bins), F32),
            VMEM((views, planes, bins), F32),
            pltpu.SemaphoreType.DMA((1 + CHUNKS,)),
        ],
        compiler_params=LIMIT,
        interpret=interpreted(),
        name="back_x",
    )(*(in_vmem(value) for value in (column, table, base, residual, own)))


def back_last_kernel(
    column_ref, table_ref, partial_ref, half_ref, other_ref, gradient_hbm, out_hbm, rest_hbm,
    spread_ref, sum_ref, rows_ref, rest_ref, sems, *, blocks, others, pad, scale,
):
    bins, _ = partial_ref.shape
    block, other = lax.axis_index("gy"), lax.axis_index("gx")
    flip = other % 2 == 1
    mine = half_of(block)
    value = from_roles(other_ref[...], flip)
    spread_into(value, column_ref[...], block, blocks, other, others, pad, scale, spread_ref)
    dims = (((0,), (0,)), ((), ()))
    size = bins // CHUNKS
    copies = []
    for c in range(CHUNKS):
        part = pl.ds(c * size, size)
        back = lax.dot_general(spread_ref[:, c * size : (c + 1) * size], table_ref[...], dims, preferred_element_type=F32)
        sum_ref[:, part, :] = (partial_ref[part, :] + back)[None]
        copies.append(pltpu.make_async_copy(sum_ref.at[:, part], out_hbm.at[pl.ds(1 - mine, 1), part], sems.at[1 + c]))
        copies[-1].start()
    odd = mine == 1
    low = from_roles(jnp.where(odd, other_ref[...], half_ref[...]), flip)
    high = from_roles(jnp.where(odd, half_ref[...], other_ref[...]), flip)
    store_rows([middle(low, pad), middle(high, pad)], rest_ref, rows_ref)
    copies.append(pltpu.make_async_copy(rest_ref, rest_hbm, sems.at[0]))
    copies[-1].start()
    for copy in copies:
        copy.wait()


def back_last(column, table, partial, half, other, gradient, blocks, others, pad, scale):
    bins, cells = partial.shape
    planes = gradient.shape[0]
    views = column.shape[0]

    def body(*refs):
        back_last_kernel(*refs, blocks=blocks, others=others, pad=pad, scale=scale)

    return pl.pallas_call(
        body,
        out_shape=(
            jax.ShapeDtypeStruct(gradient.shape, F32),
            jax.ShapeDtypeStruct((views, planes, bins), F32),
        ),
        in_specs=[vmem()] * 5 + [anywhere()],
        out_specs=(anywhere(), anywhere()),
        scratch_shapes=[
            VMEM((LEVELS * views, bins), BF16),
            VMEM((1, bins, cells), F32),
            VMEM((planes * views, bins), F32),
            VMEM((views, planes, bins), F32),
            pltpu.SemaphoreType.DMA((1 + CHUNKS,)),
        ],
        input_output_aliases={5: 0},
        compiler_params=LIMIT,
        interpret=interpreted(),
        name="back_last",
    )(*(in_vmem(value) for value in (column, table, partial, half, other)), gradient)


def exchange(value, axis, partner):
    return lax.ppermute(value, axis, [(i, partner(i)) for i in range(lax.axis_size(axis))])


def twin(i):
    return i ^ 1


def odd_twin(i):
    return i - i % RING + (i + (1 if i % 2 else -1)) % RING


def across(i):
    return i - i % RING + (i + (-3 if i % 2 else 3)) % RING


def at_end(size, axis):
    index = lax.axis_index(axis) % size
    return (index == 0) | (index == size - 1)


def steps(volume, view_slopes, measured_x, measured_y):
    _, cells_x, cells_y = volume.shape
    count_x = lax.axis_size("gx")
    count_y = lax.axis_size("gy")
    scale_x = float(cells_x * count_x) ** (-0.5)
    scale_y = float(cells_y * count_y) ** (-0.5)
    pad_x, pad_y = 64, 128

    sum_x, sum_y, table_y, near, volume, column_x, column_y, lane = forward(
        view_slopes, volume, measured_x, measured_y, count_x, count_y, pad_x, pad_y, scale_x, scale_y
    )
    wide = sum_x.shape[1]
    edge_x, edge_y = wide // 3, sum_y.shape[1] // 3
    y_a, y_mid, y_b = sum_y[:, :edge_y], sum_y[:, edge_y : 2 * edge_y], sum_y[:, 2 * edge_y :]

    got = exchange(jnp.concatenate([sum_x, y_a], axis=1), "gx", twin)
    beside = lax.ppermute(near, "pa", [(0, 1), (1, 0)])
    sum_x, y_a = sum_x + got[:, :wide], y_a + got[:, wide:]
    got = exchange(jnp.concatenate([sum_x, y_b], axis=1), "gx", odd_twin)
    sum_x, y_b = sum_x + got[:, :wide], y_b + jnp.where(at_end(count_x, "gx"), 0.0, got[:, wide:])
    sum_y = jnp.concatenate([y_a, y_mid, y_b], axis=1)
    x_a, x_mid, x_b = sum_x[:, :edge_x], sum_x[:, edge_x : 2 * edge_x], sum_x[:, 2 * edge_x :]

    rows = sum_y.shape[0] // 2
    long = sum_y.shape[1]
    owns = half_of(lax.axis_index("gy")) == 0
    kept = jnp.where(owns, sum_y[:rows], sum_y[rows:])
    sent = jnp.where(owns, sum_y[rows:], sum_y[:rows])
    got = exchange(jnp.concatenate([sent, x_a[:rows], x_a[rows:]], axis=1), "gy", twin)
    half = kept + got[:, :long]
    x_a = x_a + jnp.concatenate([got[:, long : long + edge_x], got[:, long + edge_x :]], axis=0)
    got = exchange(jnp.concatenate([half, x_b[:rows], x_b[rows:]], axis=1), "gy", lambda i: i ^ RING)
    half = half + got[:, :long]
    sent_b = jnp.where(at_end(RING, "gy"), got[:, long:], jnp.concatenate([x_b[:rows], x_b[rows:]], axis=1))
    got = exchange(jnp.concatenate([half, sent_b], axis=1), "gy", odd_twin)
    half = half + got[:, :long]
    got = jnp.where(at_end(count_y, "gy"), 0.0, got)
    half, x_b, got = lax.optimization_barrier((half, x_b, got))
    x_b = x_b + jnp.concatenate([got[:, long : long + edge_x], got[:, long + edge_x :]], axis=0)
    sum_x = jnp.concatenate([x_a, x_mid, x_b], axis=1)

    half = half + exchange(half, "gy", across)
    other = exchange(half, "gy", twin)
    sum_x = sum_x + exchange(sum_x, "gx", across)

    table_x, base = prepare(lane, volume, beside, count_x)
    own = back_own(column_y, table_y, half, cells_x, count_y, count_x, pad_y, scale_y)
    gradient, residual_x, partial = back_x(
        column_x, table_x, base, sum_x, own, count_x, count_y, pad_x, scale_x
    )
    gradient, residual_y = back_last(
        column_y, table_y, partial, half, other, gradient, count_y, count_x, pad_y, scale_y
    )
    return (gradient, residual_x, residual_y)


def solution(mesh):
    return jax.shard_map(
        steps,
        mesh=mesh,
        in_specs=(P("pa", "gx", "gy"), P(), P(None, "pa", "gy"), P(None, "pa", "gx")),
        out_specs=(P("pa", "gx", "gy"), P(None, "pa", "gy"), P(None, "pa", "gx")),
        check_vma=False,
    )
```

```python
import jax
import jax.numpy as jnp
from jax import lax
from jax.experimental import pallas as pl
from jax.experimental.pallas import tpu as pltpu
from jax.sharding import PartitionSpec as P


LEVELS = 16
RING = 8
CHUNKS = 2
PIECES = 4
LIMIT = pltpu.CompilerParams(vmem_limit_bytes=8 * 1024 * 1024)
SMEM = pltpu.SMEM
VMEM = pltpu.VMEM
F32 = jnp.float32
BF16 = jnp.bfloat16


def interpreted():
    return False


def fill(slopes_ref, family, shape, dim):
    views = slopes_ref.shape[1]
    view = lax.broadcasted_iota(jnp.int32, shape, dim) % views
    slopes = jnp.zeros(shape, jnp.int32)
    for v in range(views):
        slopes = jnp.where(view == v, slopes_ref[family, v], slopes)
    return slopes


def tiled(value, width):
    return jnp.concatenate([value] * (width // value.shape[1]), axis=1)


def lowest_shift(slopes, block, blocks):
    return slopes * (block - blocks // 2) + jnp.minimum(slopes, 0)


def tiles_of(value):
    return [value[:, k : k + 128] for k in range(0, value.shape[1], 128)]


def shifted(tiles, amount, count):
    if amount == 0:
        return tiles[:count]
    lane = lax.broadcasted_iota(jnp.int32, tiles[0].shape, 1)
    rolled = [None if tile is None else pltpu.roll(tile, amount, 1) for tile in tiles]
    out = []
    for k in range(count):
        here, before = rolled[k], rolled[k - 1]
        if here is None and before is None:
            out.append(None)
        elif here is None:
            out.append(jnp.where(lane < amount, before, 0.0))
        elif before is None:
            out.append(jnp.where(lane < amount, 0.0, here))
        else:
            out.append(jnp.where(lane < amount, before, here))
    return out


def barrel(tiles, amounts):
    lane = lax.broadcasted_iota(jnp.int32, amounts.shape, 1)
    low = amounts & 127
    source = (lane - amounts) & 127
    zero = jnp.zeros(amounts.shape, F32)
    turned = [zero if tile is None else jnp.take_along_axis(tile, source, axis=1) for tile in tiles]
    near = [jnp.where(lane < low, turned[k - 1], turned[k]) for k in range(len(tiles))]
    return [jnp.where(amounts >= 128, near[k - 1], near[k]) for k in range(len(tiles))]


def offsets(slopes, block, blocks, cells):
    views = slopes.shape[0]
    lowest = tiled(lowest_shift(slopes, block, blocks).astype(F32), cells)
    cell = lax.broadcasted_iota(jnp.int32, (views, cells), 1) + (block * cells - blocks * cells // 2)
    return tiled(slopes.astype(F32), cells) * (cell.astype(F32) * (1.0 / cells)) - lowest


def hat(offset, level):
    return jnp.maximum(1.0 - jnp.abs(offset - level), 0.0)


def in_vmem(value):
    if interpreted():
        return value
    return pltpu.with_memory_space_constraint(value, VMEM)


def in_hbm(value):
    if interpreted():
        return value
    return pltpu.with_memory_space_constraint(value, pltpu.HBM)


def out_vmem(shape, dtype):
    if interpreted():
        return jax.ShapeDtypeStruct(shape, dtype)
    return VMEM(shape, dtype)


def anywhere():
    return pl.BlockSpec(memory_space=pltpu.HBM)


def vmem():
    return pl.BlockSpec(memory_space=VMEM)


def in_roles(value, odd):
    edge = value.shape[1] // 3
    lead, mid, trail = value[:, :edge], value[:, edge : 2 * edge], value[:, 2 * edge :]
    return jnp.concatenate([jnp.where(odd, lead, trail), mid, jnp.where(odd, trail, lead)], axis=1)


def from_roles(value, odd):
    edge = value.shape[1] // 3
    a, mid, b = value[:, :edge], value[:, edge : 2 * edge], value[:, 2 * edge :]
    return jnp.concatenate([jnp.where(odd, a, b), mid, jnp.where(odd, b, a)], axis=1)


def on_grid(value):
    return jnp.round(value * 32768.0) * (1.0 / 32768.0)


def project(table_ref, volume_ref, rows_ref, slopes, out_ref, plane, family, block, blocks, odd, pad, scale):
    views = slopes.shape[0]
    bins = volume_ref.shape[2 - family]
    width = out_ref.shape[1]
    first = (block == 0).astype(F32)
    amounts = pad - LEVELS + 1 - lowest_shift(slopes, block, blocks)
    count = width // 128
    data = bins // 128
    dims = (((1,), (family,)), ((), ()))
    summands = lax.dot_general(table_ref[...], volume_ref[plane], dims, preferred_element_type=F32)
    total = [None] * count
    for level in range(LEVELS):
        piece = tiles_of(summands[level * views : (level + 1) * views, :]) + [None] * (count - data)
        piece = shifted(piece, LEVELS - 1 - level, count)
        total = [p if t is None else t if p is None else t + p for t, p in zip(total, piece)]
    total = jnp.concatenate(barrel(total, amounts), axis=1) * scale
    known = tiles_of(rows_ref[plane * views : (plane + 1) * views, :] * first) + [None] * (count - data)
    known = [None] * (pad // 128) + shifted(known, pad % 128, count - pad // 128)
    known = jnp.concatenate([jnp.zeros((views, 128), F32) if k is None else k for k in known], axis=1)
    total = on_grid(total - known)
    out_ref[plane * views : (plane + 1) * views, :] = in_roles(total, odd)


def build_table(slopes, block, blocks, cells, table_ref):
    views = slopes.shape[0]
    offset = offsets(slopes, block, blocks, cells)
    for level in range(LEVELS):
        table_ref[level * views : (level + 1) * views, :] = hat(offset, float(level)).astype(BF16)


def gather_rows(measured_ref, rows_ref):
    views, planes, _ = measured_ref.shape
    for plane in range(planes):
        for v in range(views):
            rows_ref[plane * views + v : plane * views + v + 1, :] = measured_ref[v, plane : plane + 1, :]


def forward_kernel(
    slopes_hbm, volume_hbm, mx_hbm, my_hbm,
    x_ref, y_ref, table_y_ref, near_ref, volume_ref, column_x_ref, column_y_ref, lane_ref,
    table_x_ref, slopes_ref, mx_ref, my_ref, rows_x_ref, rows_y_ref, sems,
    *, count_x, count_y, pad_x, pad_y, scale_x, scale_y,
):
    planes, cells_x, cells_y = volume_ref.shape
    fetches = [
        pltpu.make_async_copy(slopes_hbm, slopes_ref, sems.at[0]),
        pltpu.make_async_copy(volume_hbm.at[0:1], volume_ref.at[0:1], sems.at[1]),
        pltpu.make_async_copy(mx_hbm, mx_ref, sems.at[2]),
        pltpu.make_async_copy(my_hbm, my_ref, sems.at[3]),
        pltpu.make_async_copy(volume_hbm.at[1:2], volume_ref.at[1:2], sems.at[5]),
        pltpu.make_async_copy(volume_hbm.at[pl.ds(1 - lax.axis_index("pa"), 1)], near_ref, sems.at[4]),
    ]
    for fetch in fetches:
        fetch.start()
    here_x, here_y = lax.axis_index("gx"), lax.axis_index("gy")
    fetches[0].wait()
    column_x = fill(slopes_ref, 0, column_x_ref.shape, 0)
    column_y = fill(slopes_ref, 1, column_y_ref.shape, 0)
    column_x_ref[...] = column_x
    column_y_ref[...] = column_y
    lane_ref[...] = fill(slopes_ref, 0, lane_ref.shape, 1)
    build_table(column_y, here_y, count_y, cells_y, table_y_ref)
    build_table(column_x, here_x, count_x, cells_x, table_x_ref)
    fetches[2].wait()
    fetches[3].wait()
    gather_rows(mx_ref, rows_x_ref)
    gather_rows(my_ref, rows_y_ref)
    for plane in range(planes):
        fetches[1 if plane == 0 else 4].wait()
        project(
            table_y_ref, volume_ref, rows_y_ref, column_y, y_ref, plane, 1, here_y, count_y, here_x % 2 == 1, pad_y, scale_y
        )
        project(
            table_x_ref, volume_ref, rows_x_ref, column_x, x_ref, plane, 0, here_x, count_x, here_y % 2 == 1, pad_x, scale_x
        )
    fetches[5].wait()


def forward(slopes, volume, measured_x, measured_y, count_x, count_y, pad_x, pad_y, scale_x, scale_y):
    views = slopes.shape[1]
    planes, cells_x, cells_y = volume.shape

    def body(*refs):
        forward_kernel(
            *refs, count_x=count_x, count_y=count_y, pad_x=pad_x, pad_y=pad_y, scale_x=scale_x, scale_y=scale_y
        )

    return pl.pallas_call(
        body,
        out_shape=(
            out_vmem((planes * views, cells_y + 2 * pad_x), F32),
            out_vmem((planes * views, cells_x + 2 * pad_y), F32),
            out_vmem((LEVELS * views, cells_y), BF16),
            out_vmem((1,) + volume.shape[1:], BF16),
            out_vmem(volume.shape, BF16),
            out_vmem((views, 128), jnp.int32),
            out_vmem((views, 128), jnp.int32),
            out_vmem((8, LEVELS * views), jnp.int32),
        ),
        in_specs=[anywhere()] * 4,
        out_specs=(vmem(),) * 8,
        scratch_shapes=[
            VMEM((LEVELS * views, cells_x), BF16),
            SMEM(slopes.shape, jnp.int32),
            VMEM(measured_x.shape, F32),
            VMEM(measured_y.shape, F32),
            VMEM((planes * views, cells_y), F32),
            VMEM((planes * views, cells_x), F32),
            pltpu.SemaphoreType.DMA((6,)),
        ],
        compiler_params=LIMIT,
        interpret=interpreted(),
        name="forward",
    )(*(in_hbm(value) for value in (slopes, volume, measured_x, measured_y)))


def half_of(index):
    return ((index + 1) // 2) % 2


def spread_into(value, slopes, block, blocks, other, others, pad, scale, spread_ref):
    views, width = value.shape
    bins = width - 2 * pad
    place = lax.broadcasted_iota(jnp.int32, (views, width), 1)
    inside = (place >= jnp.where(other == 0, pad, 0)) & (place < jnp.where(other == others - 1, pad + bins, width))
    value = jnp.where(inside, value * scale, 0.0).astype(BF16).astype(F32)
    tiles = barrel(tiles_of(value), lowest_shift(slopes, block, blocks) + pad)
    skip = 2 * pad // 128
    tiles = tiles[skip:] + tiles[:skip]
    for level in range(LEVELS):
        piece = jnp.concatenate(shifted(tiles, level, bins // 128), axis=1)
        spread_ref[level * views : (level + 1) * views, :] = piece.astype(BF16)


def middle(value, pad):
    tiles = tiles_of(value)
    skip = pad // 128
    tiles = tiles[skip:] + tiles[:skip]
    count = (value.shape[1] - 2 * pad) // 128
    if pad % 128 == 0:
        return jnp.concatenate(tiles[:count], axis=1)
    tiles = tiles[1:] + tiles[:1]
    return jnp.concatenate(shifted(tiles, 128 - pad % 128, count), axis=1)


def prepare_kernel(lane_ref, volume_ref, beside_ref, table_ref, base_ref, *, blocks):
    planes, cells, _ = volume_ref.shape
    block, band = lax.axis_index("gx"), lax.axis_index("pa")
    slopes = lane_ref[...]
    views = slopes.shape[1] // LEVELS
    level = lax.broadcasted_iota(jnp.int32, slopes.shape, 1) // views
    base = (lowest_shift(slopes, block, blocks) + level).astype(F32)[:1]
    slopes = slopes.astype(F32)[:1]
    shape = (cells, LEVELS * views)
    cell = lax.broadcasted_iota(jnp.int32, shape, 0).astype(F32) * (1.0 / cells) + (block - blocks // 2).astype(F32)
    table_ref[...] = jnp.maximum(1.0 - jnp.abs(cell * slopes - base), 0.0).astype(BF16)
    for plane in range(planes):
        here = volume_ref[plane].astype(F32)
        beside = beside_ref[0].astype(F32) * (band == 1 - plane).astype(F32)
        within = volume_ref[1 - plane].astype(F32)
        base_ref[plane] = 0.02 * (2.0 * here - beside - within)


def prepare(lane, volume, beside, blocks):
    def body(*refs):
        prepare_kernel(*refs, blocks=blocks)

    return pl.pallas_call(
        body,
        out_shape=(out_vmem((volume.shape[1], lane.shape[1]), BF16), out_vmem(volume.shape, F32)),
        in_specs=[vmem()] * 3,
        out_specs=(vmem(), vmem()),
        compiler_params=LIMIT,
        interpret=interpreted(),
        name="prepare",
    )(*(in_vmem(value) for value in (lane, volume, beside)))


def store_rows(values, rest_ref, rows_ref):
    planes, views = len(values), rest_ref.shape[0]
    for plane in range(planes):
        rows_ref[plane * views : (plane + 1) * views, :] = values[plane]
    for plane in range(planes):
        for v in range(views):
            rest_ref[v, plane : plane + 1, :] = rows_ref[plane * views + v : plane * views + v + 1, :]


def back_own_kernel(column_ref, table_ref, half_ref, out_ref, spread_ref, *, blocks, others, pad, scale):
    block, other = lax.axis_index("gy"), lax.axis_index("gx")
    value = from_roles(half_ref[...], other % 2 == 1)
    spread_into(value, column_ref[...], block, blocks, other, others, pad, scale, spread_ref)
    dims = (((0,), (0,)), ((), ()))
    out_ref[...] = lax.dot_general(spread_ref[...], table_ref[...], dims, preferred_element_type=F32)


def back_own(column, table, half, bins, blocks, others, pad, scale):
    def body(*refs):
        back_own_kernel(*refs, blocks=blocks, others=others, pad=pad, scale=scale)

    return pl.pallas_call(
        body,
        out_shape=out_vmem((bins, table.shape[1]), F32),
        in_specs=[vmem()] * 3,
        out_specs=vmem(),
        scratch_shapes=[VMEM((table.shape[0], bins), BF16)],
        compiler_params=LIMIT,
        interpret=interpreted(),
        name="back_own",
    )(*(in_vmem(value) for value in (column, table, half)))


def back_x_kernel(
    column_ref, table_ref, base_ref, half_ref, away_ref, own_ref, out_hbm, rest_hbm, partial_ref,
    spread_ref, sum_ref, rows_ref, rest_ref, sems, *, blocks, others, pad, scale,
):
    planes, cells, _ = base_ref.shape
    block, other = lax.axis_index("gx"), lax.axis_index("gy")
    column = column_ref[...]
    flip = other % 2 == 1
    mine = half_of(other)
    held = half_of(block)
    size = cells // CHUNKS
    copies = []

    def residual_of(plane):
        return from_roles(jnp.where(plane == held, half_ref[...], away_ref[...]), flip)

    for last in range(planes):
        plane = 1 - mine if last else mine
        spread_into(residual_of(plane), column, block, blocks, other, others, pad, scale, spread_ref)
        for c in range(CHUNKS):
            part = pl.ds(c * size, size)
            value = jnp.dot(table_ref[part, :], spread_ref[...], preferred_element_type=F32)
            value = base_ref[pl.ds(plane, 1), part, :] + value[None]
            if last:
                partial_ref[part, :] = value[0]
            else:
                sum_ref[:, part, :] = value + own_ref[part, :][None]
                copies.append(
                    pltpu.make_async_copy(sum_ref.at[:, part], out_hbm.at[pl.ds(plane, 1), part], sems.at[1 + c])
                )
                copies[-1].start()
    store_rows([middle(residual_of(p), pad) for p in range(planes)], rest_ref, rows_ref)
    copies.append(pltpu.make_async_copy(rest_ref, rest_hbm, sems.at[0]))
    copies[-1].start()
    for copy in copies:
        copy.wait()


def back_x(column, table, base, half, away, own, blocks, others, pad, scale):
    planes, cells, bins = base.shape
    views = column.shape[0]

    def body(*refs):
        back_x_kernel(*refs, blocks=blocks, others=others, pad=pad, scale=scale)

    return pl.pallas_call(
        body,
        out_shape=(
            jax.ShapeDtypeStruct(base.shape, F32),
            jax.ShapeDtypeStruct((views, planes, bins), F32),
            out_vmem((cells, bins), F32),
        ),
        in_specs=[vmem()] * 6,
        out_specs=(anywhere(), anywhere(), vmem()),
        scratch_shapes=[
            VMEM((LEVELS * views, bins), BF16),
            VMEM((1, cells, bins), F32),
            VMEM((planes * views, bins), F32),
            VMEM((views, planes, bins), F32),
            pltpu.SemaphoreType.DMA((1 + CHUNKS,)),
        ],
        compiler_params=LIMIT,
        interpret=interpreted(),
        name="back_x",
    )(*(in_vmem(value) for value in (column, table, base, half, away, own)))


def back_last_kernel(
    column_ref, table_ref, partial_ref, half_ref, other_ref, gradient_hbm, out_hbm, rest_hbm,
    spread_ref, sum_ref, rows_ref, rest_ref, sems, *, blocks, others, pad, scale,
):
    bins, _ = partial_ref.shape
    block, other = lax.axis_index("gy"), lax.axis_index("gx")
    flip = other % 2 == 1
    mine = half_of(block)
    value = from_roles(other_ref[...], flip)
    spread_into(value, column_ref[...], block, blocks, other, others, pad, scale, spread_ref)
    dims = (((0,), (0,)), ((), ()))
    size = bins // PIECES
    copies = []
    for c in range(PIECES):
        part = pl.ds(c * size, size)
        back = lax.dot_general(spread_ref[:, c * size : (c + 1) * size], table_ref[...], dims, preferred_element_type=F32)
        sum_ref[:, part, :] = (partial_ref[part, :] + back)[None]
        copies.append(pltpu.make_async_copy(sum_ref.at[:, part], out_hbm.at[pl.ds(1 - mine, 1), part], sems.at[1 + c]))
        copies[-1].start()
    odd = mine == 1
    low = from_roles(jnp.where(odd, other_ref[...], half_ref[...]), flip)
    high = from_roles(jnp.where(odd, half_ref[...], other_ref[...]), flip)
    store_rows([middle(low, pad), middle(high, pad)], rest_ref, rows_ref)
    copies.append(pltpu.make_async_copy(rest_ref, rest_hbm, sems.at[0]))
    copies[-1].start()
    for copy in copies:
        copy.wait()


def back_last(column, table, partial, half, other, gradient, blocks, others, pad, scale):
    bins, cells = partial.shape
    planes = gradient.shape[0]
    views = column.shape[0]

    def body(*refs):
        back_last_kernel(*refs, blocks=blocks, others=others, pad=pad, scale=scale)

    return pl.pallas_call(
        body,
        out_shape=(
            jax.ShapeDtypeStruct(gradient.shape, F32),
            jax.ShapeDtypeStruct((views, planes, bins), F32),
        ),
        in_specs=[vmem()] * 5 + [anywhere()],
        out_specs=(anywhere(), anywhere()),
        scratch_shapes=[
            VMEM((LEVELS * views, bins), BF16),
            VMEM((1, bins, cells), F32),
            VMEM((planes * views, bins), F32),
            VMEM((views, planes, bins), F32),
            pltpu.SemaphoreType.DMA((1 + PIECES,)),
        ],
        input_output_aliases={5: 0},
        compiler_params=LIMIT,
        interpret=interpreted(),
        name="back_last",
    )(*(in_vmem(value) for value in (column, table, partial, half, other)), gradient)


def exchange(value, axis, partner):
    return lax.ppermute(value, axis, [(i, partner(i)) for i in range(lax.axis_size(axis))])


def twin(i):
    return i ^ 1


def odd_twin(i):
    return i - i % RING + (i + (1 if i % 2 else -1)) % RING


def across(i):
    return i - i % RING + (i + (-3 if i % 2 else 3)) % RING


def at_end(size, axis):
    index = lax.axis_index(axis) % size
    return (index == 0) | (index == size - 1)


def steps(volume, view_slopes, measured_x, measured_y):
    _, cells_x, cells_y = volume.shape
    count_x = lax.axis_size("gx")
    count_y = lax.axis_size("gy")
    scale_x = float(cells_x * count_x) ** (-0.5)
    scale_y = float(cells_y * count_y) ** (-0.5)
    pad_x, pad_y = 64, 128

    sum_x, sum_y, table_y, near, volume, column_x, column_y, lane = forward(
        view_slopes, volume, measured_x, measured_y, count_x, count_y, pad_x, pad_y, scale_x, scale_y
    )
    wide, long = sum_x.shape[1], sum_y.shape[1]
    edge_x, edge_y = wide // 3, long // 3
    rows = sum_x.shape[0] // 2

    def side_by_side(value):
        return jnp.concatenate([value[:rows], value[rows:]], axis=1)

    def one_above(value):
        return jnp.concatenate([value[:, : value.shape[1] // 2], value[:, value.shape[1] // 2 :]], axis=0)

    def split(value, axis):
        owns = half_of(lax.axis_index(axis)) == 0
        low, high = value[:rows], value[rows:]
        return jnp.where(owns, low, high), jnp.where(owns, high, low)

    y_a, y_mid, y_b = sum_y[:, :edge_y], sum_y[:, edge_y : 2 * edge_y], sum_y[:, 2 * edge_y :]
    half_x, sent = split(sum_x, "gx")
    got = exchange(jnp.concatenate([sent, side_by_side(y_a)], axis=1), "gx", twin)
    beside = lax.ppermute(near, "pa", [(0, 1), (1, 0)])
    half_x, y_a = half_x + got[:, :wide], y_a + one_above(got[:, wide:])
    got = exchange(jnp.concatenate([half_x, side_by_side(y_b)], axis=1), "gx", odd_twin)
    half_x = half_x + got[:, :wide]
    y_b = y_b + jnp.where(at_end(count_x, "gx"), 0.0, one_above(got[:, wide:]))
    sum_y = jnp.concatenate([y_a, y_mid, y_b], axis=1)
    x_a, x_mid, x_b = half_x[:, :edge_x], half_x[:, edge_x : 2 * edge_x], half_x[:, 2 * edge_x :]

    half, sent = split(sum_y, "gy")
    got = exchange(jnp.concatenate([sent, x_a], axis=1), "gy", twin)
    half, x_a = half + got[:, :long], x_a + got[:, long:]
    got = exchange(jnp.concatenate([half, x_b], axis=1), "gy", lambda i: i ^ RING)
    half = half + got[:, :long]
    sent_b = jnp.where(at_end(RING, "gy"), got[:, long:], x_b)
    got = exchange(jnp.concatenate([half, sent_b], axis=1), "gy", odd_twin)
    half = half + got[:, :long]
    got = jnp.where(at_end(count_y, "gy"), 0.0, got[:, long:])
    half, x_b, got = lax.optimization_barrier((half, x_b, got))
    half_x = jnp.concatenate([x_a, x_mid, x_b + got], axis=1)

    half = half + exchange(half, "gy", across)
    got = exchange(half_x, "gx", across)
    other = exchange(half, "gy", twin)
    half_x, half = lax.optimization_barrier((half_x, half))
    half_x = half_x + got
    away_x = exchange(half_x, "gx", twin)

    table_x, base = prepare(lane, volume, beside, count_x)
    own = back_own(column_y, table_y, half, cells_x, count_y, count_x, pad_y, scale_y)
    gradient, residual_x, partial = back_x(
        column_x, table_x, base, half_x, away_x, own, count_x, count_y, pad_x, scale_x
    )
    gradient, residual_y = back_last(
        column_y, table_y, partial, half, other, gradient, count_y, count_x, pad_y, scale_y
    )
    return (gradient, residual_x, residual_y)


def solution(mesh):
    return jax.shard_map(
        steps,
        mesh=mesh,
        in_specs=(P("pa", "gx", "gy"), P(), P(None, "pa", "gy"), P(None, "pa", "gx")),
        out_specs=(P("pa", "gx", "gy"), P(None, "pa", "gy"), P(None, "pa", "gx")),
        check_vma=False,
    )
```

```python
import jax
import jax.numpy as jnp
from jax import lax
from jax.experimental import pallas as pl
from jax.experimental.pallas import tpu as pltpu
from jax.sharding import PartitionSpec as P


LEVELS = 16
RING = 8
CHUNKS = 2
PIECES = 4
LIMIT = pltpu.CompilerParams(vmem_limit_bytes=8 * 1024 * 1024)
SMEM = pltpu.SMEM
VMEM = pltpu.VMEM
F32 = jnp.float32
BF16 = jnp.bfloat16


def interpreted():
    return False


def fill(slopes_ref, family, shape, dim):
    views = slopes_ref.shape[1]
    view = lax.broadcasted_iota(jnp.int32, shape, dim) % views
    slopes = jnp.zeros(shape, jnp.int32)
    for v in range(views):
        slopes = jnp.where(view == v, slopes_ref[family, v], slopes)
    return slopes


def tiled(value, width):
    return jnp.concatenate([value] * (width // value.shape[1]), axis=1)


def lowest_shift(slopes, block, blocks):
    return slopes * (block - blocks // 2) + jnp.minimum(slopes, 0)


def tiles_of(value):
    return [value[:, k : k + 128] for k in range(0, value.shape[1], 128)]


def shifted(tiles, amount, count):
    if amount == 0:
        return tiles[:count]
    lane = lax.broadcasted_iota(jnp.int32, tiles[0].shape, 1)
    rolled = [None if tile is None else pltpu.roll(tile, amount, 1) for tile in tiles]
    out = []
    for k in range(count):
        here, before = rolled[k], rolled[k - 1]
        if here is None and before is None:
            out.append(None)
        elif here is None:
            out.append(jnp.where(lane < amount, before, 0.0))
        elif before is None:
            out.append(jnp.where(lane < amount, 0.0, here))
        else:
            out.append(jnp.where(lane < amount, before, here))
    return out


def barrel(tiles, amounts):
    lane = lax.broadcasted_iota(jnp.int32, amounts.shape, 1)
    low = amounts & 127
    source = (lane - amounts) & 127
    zero = jnp.zeros(amounts.shape, F32)
    turned = [zero if tile is None else jnp.take_along_axis(tile, source, axis=1) for tile in tiles]
    near = [jnp.where(lane < low, turned[k - 1], turned[k]) for k in range(len(tiles))]
    return [jnp.where(amounts >= 128, near[k - 1], near[k]) for k in range(len(tiles))]


def offsets(slopes, block, blocks, cells):
    views = slopes.shape[0]
    lowest = tiled(lowest_shift(slopes, block, blocks).astype(F32), cells)
    cell = lax.broadcasted_iota(jnp.int32, (views, cells), 1) + (block * cells - blocks * cells // 2)
    return tiled(slopes.astype(F32), cells) * (cell.astype(F32) * (1.0 / cells)) - lowest


def hat(offset, level):
    return jnp.maximum(1.0 - jnp.abs(offset - level), 0.0)


def in_vmem(value):
    if interpreted():
        return value
    return pltpu.with_memory_space_constraint(value, VMEM)


def in_hbm(value):
    if interpreted():
        return value
    return pltpu.with_memory_space_constraint(value, pltpu.HBM)


def out_vmem(shape, dtype):
    if interpreted():
        return jax.ShapeDtypeStruct(shape, dtype)
    return VMEM(shape, dtype)


def anywhere():
    return pl.BlockSpec(memory_space=pltpu.HBM)


def vmem():
    return pl.BlockSpec(memory_space=VMEM)


def in_roles(value, odd):
    edge = value.shape[1] // 3
    lead, mid, trail = value[:, :edge], value[:, edge : 2 * edge], value[:, 2 * edge :]
    return jnp.concatenate([jnp.where(odd, lead, trail), mid, jnp.where(odd, trail, lead)], axis=1)


def from_roles(value, odd):
    edge = value.shape[1] // 3
    a, mid, b = value[:, :edge], value[:, edge : 2 * edge], value[:, 2 * edge :]
    return jnp.concatenate([jnp.where(odd, a, b), mid, jnp.where(odd, b, a)], axis=1)


def on_grid(value):
    return jnp.round(value * 32768.0) * (1.0 / 32768.0)


def project(table_ref, volume_ref, rows_ref, slopes, out_ref, plane, family, block, blocks, odd, pad, scale):
    views = slopes.shape[0]
    bins = volume_ref.shape[2 - family]
    width = out_ref.shape[1]
    first = (block == 0).astype(F32)
    amounts = pad - LEVELS + 1 - lowest_shift(slopes, block, blocks)
    count = width // 128
    data = bins // 128
    dims = (((1,), (family,)), ((), ()))
    summands = lax.dot_general(table_ref[...], volume_ref[plane], dims, preferred_element_type=F32)
    total = [None] * count
    for level in range(LEVELS):
        piece = tiles_of(summands[level * views : (level + 1) * views, :]) + [None] * (count - data)
        piece = shifted(piece, LEVELS - 1 - level, count)
        total = [p if t is None else t if p is None else t + p for t, p in zip(total, piece)]
    total = jnp.concatenate(barrel(total, amounts), axis=1) * scale
    known = tiles_of(rows_ref[plane * views : (plane + 1) * views, :] * first) + [None] * (count - data)
    known = [None] * (pad // 128) + shifted(known, pad % 128, count - pad // 128)
    known = jnp.concatenate([jnp.zeros((views, 128), F32) if k is None else k for k in known], axis=1)
    total = on_grid(total - known)
    out_ref[plane * views : (plane + 1) * views, :] = in_roles(total, odd)


def build_table(slopes, block, blocks, cells, table_ref):
    views = slopes.shape[0]
    offset = offsets(slopes, block, blocks, cells)
    for level in range(LEVELS):
        table_ref[level * views : (level + 1) * views, :] = hat(offset, float(level)).astype(BF16)


def gather_rows(measured_ref, rows_ref):
    views, planes, _ = measured_ref.shape
    for plane in range(planes):
        for v in range(views):
            rows_ref[plane * views + v : plane * views + v + 1, :] = measured_ref[v, plane : plane + 1, :]


def forward_kernel(
    slopes_hbm, volume_hbm, mx_hbm, my_hbm,
    x_ref, y_ref, table_y_ref, near_ref, volume_ref, column_x_ref, column_y_ref, lane_ref,
    table_x_ref, slopes_ref, mx_ref, my_ref, rows_x_ref, rows_y_ref, sems,
    *, count_x, count_y, pad_x, pad_y, scale_x, scale_y,
):
    planes, cells_x, cells_y = volume_ref.shape
    fetches = [
        pltpu.make_async_copy(slopes_hbm, slopes_ref, sems.at[0]),
        pltpu.make_async_copy(volume_hbm, volume_ref, sems.at[1]),
        pltpu.make_async_copy(mx_hbm, mx_ref, sems.at[2]),
        pltpu.make_async_copy(my_hbm, my_ref, sems.at[3]),
        pltpu.make_async_copy(volume_hbm.at[pl.ds(1 - lax.axis_index("pa"), 1)], near_ref, sems.at[4]),
    ]
    for fetch in fetches:
        fetch.start()
    here_x, here_y = lax.axis_index("gx"), lax.axis_index("gy")
    fetches[0].wait()
    column_x = fill(slopes_ref, 0, column_x_ref.shape, 0)
    column_y = fill(slopes_ref, 1, column_y_ref.shape, 0)
    column_x_ref[...] = column_x
    column_y_ref[...] = column_y
    lane_ref[...] = fill(slopes_ref, 0, lane_ref.shape, 1)
    build_table(column_y, here_y, count_y, cells_y, table_y_ref)
    build_table(column_x, here_x, count_x, cells_x, table_x_ref)
    fetches[2].wait()
    fetches[3].wait()
    gather_rows(mx_ref, rows_x_ref)
    gather_rows(my_ref, rows_y_ref)
    fetches[1].wait()
    for plane in range(planes):
        project(
            table_y_ref, volume_ref, rows_y_ref, column_y, y_ref, plane, 1, here_y, count_y, here_x % 2 == 1, pad_y, scale_y
        )
    for plane in range(planes):
        project(
            table_x_ref, volume_ref, rows_x_ref, column_x, x_ref, plane, 0, here_x, count_x, here_y % 2 == 1, pad_x, scale_x
        )
    fetches[4].wait()


def forward(slopes, volume, measured_x, measured_y, count_x, count_y, pad_x, pad_y, scale_x, scale_y):
    views = slopes.shape[1]
    planes, cells_x, cells_y = volume.shape

    def body(*refs):
        forward_kernel(
            *refs, count_x=count_x, count_y=count_y, pad_x=pad_x, pad_y=pad_y, scale_x=scale_x, scale_y=scale_y
        )

    return pl.pallas_call(
        body,
        out_shape=(
            out_vmem((planes * views, cells_y + 2 * pad_x), F32),
            out_vmem((planes * views, cells_x + 2 * pad_y), F32),
            out_vmem((LEVELS * views, cells_y), BF16),
            out_vmem((1,) + volume.shape[1:], BF16),
            out_vmem(volume.shape, BF16),
            out_vmem((views, 128), jnp.int32),
            out_vmem((views, 128), jnp.int32),
            out_vmem((8, LEVELS * views), jnp.int32),
        ),
        in_specs=[anywhere()] * 4,
        out_specs=(vmem(),) * 8,
        scratch_shapes=[
            VMEM((LEVELS * views, cells_x), BF16),
            SMEM(slopes.shape, jnp.int32),
            VMEM(measured_x.shape, F32),
            VMEM(measured_y.shape, F32),
            VMEM((planes * views, cells_y), F32),
            VMEM((planes * views, cells_x), F32),
            pltpu.SemaphoreType.DMA((5,)),
        ],
        compiler_params=LIMIT,
        interpret=interpreted(),
        name="forward",
    )(*(in_hbm(value) for value in (slopes, volume, measured_x, measured_y)))


def half_of(index):
    return ((index + 1) // 2) % 2


def spread_into(value, slopes, block, blocks, other, others, pad, scale, spread_ref):
    views, width = value.shape
    bins = width - 2 * pad
    place = lax.broadcasted_iota(jnp.int32, (views, width), 1)
    inside = (place >= jnp.where(other == 0, pad, 0)) & (place < jnp.where(other == others - 1, pad + bins, width))
    value = jnp.where(inside, value * scale, 0.0).astype(BF16).astype(F32)
    tiles = barrel(tiles_of(value), lowest_shift(slopes, block, blocks) + pad)
    skip = 2 * pad // 128
    tiles = tiles[skip:] + tiles[:skip]
    for level in range(LEVELS):
        piece = jnp.concatenate(shifted(tiles, level, bins // 128), axis=1)
        spread_ref[level * views : (level + 1) * views, :] = piece.astype(BF16)


def middle(value, pad):
    tiles = tiles_of(value)
    skip = pad // 128
    tiles = tiles[skip:] + tiles[:skip]
    count = (value.shape[1] - 2 * pad) // 128
    if pad % 128 == 0:
        return jnp.concatenate(tiles[:count], axis=1)
    tiles = tiles[1:] + tiles[:1]
    return jnp.concatenate(shifted(tiles, 128 - pad % 128, count), axis=1)


def prepare_kernel(lane_ref, volume_ref, beside_ref, table_ref, base_ref, *, blocks):
    planes, cells, _ = volume_ref.shape
    block, band = lax.axis_index("gx"), lax.axis_index("pa")
    slopes = lane_ref[...]
    views = slopes.shape[1] // LEVELS
    level = lax.broadcasted_iota(jnp.int32, slopes.shape, 1) // views
    base = (lowest_shift(slopes, block, blocks) + level).astype(F32)[:1]
    slopes = slopes.astype(F32)[:1]
    shape = (cells, LEVELS * views)
    cell = lax.broadcasted_iota(jnp.int32, shape, 0).astype(F32) * (1.0 / cells) + (block - blocks // 2).astype(F32)
    table_ref[...] = jnp.maximum(1.0 - jnp.abs(cell * slopes - base), 0.0).astype(BF16)
    for plane in range(planes):
        here = volume_ref[plane].astype(F32)
        beside = beside_ref[0].astype(F32) * (band == 1 - plane).astype(F32)
        within = volume_ref[1 - plane].astype(F32)
        base_ref[plane] = 0.02 * (2.0 * here - beside - within)


def prepare(lane, volume, beside, blocks):
    def body(*refs):
        prepare_kernel(*refs, blocks=blocks)

    return pl.pallas_call(
        body,
        out_shape=(out_vmem((volume.shape[1], lane.shape[1]), BF16), out_vmem(volume.shape, F32)),
        in_specs=[vmem()] * 3,
        out_specs=(vmem(), vmem()),
        compiler_params=LIMIT,
        interpret=interpreted(),
        name="prepare",
    )(*(in_vmem(value) for value in (lane, volume, beside)))


def store_rows(values, rest_ref, rows_ref):
    planes, views = len(values), rest_ref.shape[0]
    for plane in range(planes):
        rows_ref[plane * views : (plane + 1) * views, :] = values[plane]
    for plane in range(planes):
        for v in range(views):
            rest_ref[v, plane : plane + 1, :] = rows_ref[plane * views + v : plane * views + v + 1, :]


def back_own_kernel(column_ref, table_ref, half_ref, out_ref, spread_ref, *, blocks, others, pad, scale):
    block, other = lax.axis_index("gy"), lax.axis_index("gx")
    value = from_roles(half_ref[...], other % 2 == 1)
    spread_into(value, column_ref[...], block, blocks, other, others, pad, scale, spread_ref)
    dims = (((0,), (0,)), ((), ()))
    out_ref[...] = lax.dot_general(spread_ref[...], table_ref[...], dims, preferred_element_type=F32)


def back_own(column, table, half, bins, blocks, others, pad, scale):
    def body(*refs):
        back_own_kernel(*refs, blocks=blocks, others=others, pad=pad, scale=scale)

    return pl.pallas_call(
        body,
        out_shape=out_vmem((bins, table.shape[1]), F32),
        in_specs=[vmem()] * 3,
        out_specs=vmem(),
        scratch_shapes=[VMEM((table.shape[0], bins), BF16)],
        compiler_params=LIMIT,
        interpret=interpreted(),
        name="back_own",
    )(*(in_vmem(value) for value in (column, table, half)))


def back_x_kernel(
    column_ref, table_ref, base_ref, half_ref, away_ref, own_ref, out_hbm, rest_hbm, partial_ref,
    spread_ref, sum_ref, rows_ref, rest_ref, sems, *, blocks, others, pad, scale,
):
    planes, cells, _ = base_ref.shape
    block, other = lax.axis_index("gx"), lax.axis_index("gy")
    column = column_ref[...]
    flip = other % 2 == 1
    mine = half_of(other)
    held = half_of(block)
    size = cells // CHUNKS
    copies = []

    def residual_of(plane):
        return from_roles(jnp.where(plane == held, half_ref[...], away_ref[...]), flip)

    for last in range(planes):
        plane = 1 - mine if last else mine
        spread_into(residual_of(plane), column, block, blocks, other, others, pad, scale, spread_ref)
        for c in range(CHUNKS):
            part = pl.ds(c * size, size)
            value = jnp.dot(table_ref[part, :], spread_ref[...], preferred_element_type=F32)
            value = base_ref[pl.ds(plane, 1), part, :] + value[None]
            if last:
                partial_ref[part, :] = value[0]
            else:
                sum_ref[:, part, :] = value + own_ref[part, :][None]
                copies.append(
                    pltpu.make_async_copy(sum_ref.at[:, part], out_hbm.at[pl.ds(plane, 1), part], sems.at[1 + c])
                )
                copies[-1].start()
    store_rows([middle(residual_of(p), pad) for p in range(planes)], rest_ref, rows_ref)
    copies.append(pltpu.make_async_copy(rest_ref, rest_hbm, sems.at[0]))
    copies[-1].start()
    for copy in copies:
        copy.wait()


def back_x(column, table, base, half, away, own, blocks, others, pad, scale):
    planes, cells, bins = base.shape
    views = column.shape[0]

    def body(*refs):
        back_x_kernel(*refs, blocks=blocks, others=others, pad=pad, scale=scale)

    return pl.pallas_call(
        body,
        out_shape=(
            jax.ShapeDtypeStruct(base.shape, F32),
            jax.ShapeDtypeStruct((views, planes, bins), F32),
            out_vmem((cells, bins), F32),
        ),
        in_specs=[vmem()] * 6,
        out_specs=(anywhere(), anywhere(), vmem()),
        scratch_shapes=[
            VMEM((LEVELS * views, bins), BF16),
            VMEM((1, cells, bins), F32),
            VMEM((planes * views, bins), F32),
            VMEM((views, planes, bins), F32),
            pltpu.SemaphoreType.DMA((1 + CHUNKS,)),
        ],
        compiler_params=LIMIT,
        interpret=interpreted(),
        name="back_x",
    )(*(in_vmem(value) for value in (column, table, base, half, away, own)))


def back_last_kernel(
    column_ref, table_ref, partial_ref, half_ref, other_ref, gradient_hbm, out_hbm, rest_hbm,
    spread_ref, sum_ref, rows_ref, rest_ref, sems, *, blocks, others, pad, scale,
):
    bins, _ = partial_ref.shape
    block, other = lax.axis_index("gy"), lax.axis_index("gx")
    flip = other % 2 == 1
    mine = half_of(block)
    value = from_roles(other_ref[...], flip)
    spread_into(value, column_ref[...], block, blocks, other, others, pad, scale, spread_ref)
    dims = (((0,), (0,)), ((), ()))
    size = bins // PIECES
    copies = []
    for c in range(PIECES):
        part = pl.ds(c * size, size)
        back = lax.dot_general(spread_ref[:, c * size : (c + 1) * size], table_ref[...], dims, preferred_element_type=F32)
        sum_ref[:, part, :] = (partial_ref[part, :] + back)[None]
        copies.append(pltpu.make_async_copy(sum_ref.at[:, part], out_hbm.at[pl.ds(1 - mine, 1), part], sems.at[1 + c]))
        copies[-1].start()
    odd = mine == 1
    low = from_roles(jnp.where(odd, other_ref[...], half_ref[...]), flip)
    high = from_roles(jnp.where(odd, half_ref[...], other_ref[...]), flip)
    store_rows([middle(low, pad), middle(high, pad)], rest_ref, rows_ref)
    copies.append(pltpu.make_async_copy(rest_ref, rest_hbm, sems.at[0]))
    copies[-1].start()
    for copy in copies:
        copy.wait()


def back_last(column, table, partial, half, other, gradient, blocks, others, pad, scale):
    bins, cells = partial.shape
    planes = gradient.shape[0]
    views = column.shape[0]

    def body(*refs):
        back_last_kernel(*refs, blocks=blocks, others=others, pad=pad, scale=scale)

    return pl.pallas_call(
        body,
        out_shape=(
            jax.ShapeDtypeStruct(gradient.shape, F32),
            jax.ShapeDtypeStruct((views, planes, bins), F32),
        ),
        in_specs=[vmem()] * 5 + [anywhere()],
        out_specs=(anywhere(), anywhere()),
        scratch_shapes=[
            VMEM((LEVELS * views, bins), BF16),
            VMEM((1, bins, cells), F32),
            VMEM((planes * views, bins), F32),
            VMEM((views, planes, bins), F32),
            pltpu.SemaphoreType.DMA((1 + PIECES,)),
        ],
        input_output_aliases={5: 0},
        compiler_params=LIMIT,
        interpret=interpreted(),
        name="back_last",
    )(*(in_vmem(value) for value in (column, table, partial, half, other)), gradient)


def exchange(value, axis, partner):
    return lax.ppermute(value, axis, [(i, partner(i)) for i in range(lax.axis_size(axis)) if partner(i) != i])


def twin(i):
    return i ^ 1


def odd_twin(i):
    return i - i % RING + (i + (1 if i % 2 else -1)) % RING


def next_twin(i):
    return odd_twin(i) if abs(odd_twin(i) - i) == 1 else i


def end_twin(i):
    return i if abs(odd_twin(i) - i) == 1 else odd_twin(i)


def across(i):
    return i - i % RING + (i + (-3 if i % 2 else 3)) % RING


def at_end(size, axis):
    index = lax.axis_index(axis) % size
    return (index == 0) | (index == size - 1)


def steps(volume, view_slopes, measured_x, measured_y):
    _, cells_x, cells_y = volume.shape
    count_x = lax.axis_size("gx")
    count_y = lax.axis_size("gy")
    scale_x = float(cells_x * count_x) ** (-0.5)
    scale_y = float(cells_y * count_y) ** (-0.5)
    pad_x, pad_y = 64, 128

    sum_x, sum_y, table_y, near, volume, column_x, column_y, lane = forward(
        view_slopes, volume, measured_x, measured_y, count_x, count_y, pad_x, pad_y, scale_x, scale_y
    )
    wide, long = sum_x.shape[1], sum_y.shape[1]
    edge_x, edge_y = wide // 3, long // 3
    rows = sum_x.shape[0] // 2

    def side_by_side(value):
        return jnp.concatenate([value[:rows], value[rows:]], axis=1)

    def one_above(value):
        return jnp.concatenate([value[:, : value.shape[1] // 2], value[:, value.shape[1] // 2 :]], axis=0)

    def split(value, axis):
        owns = half_of(lax.axis_index(axis)) == 0
        low, high = value[:rows], value[rows:]
        return jnp.where(owns, low, high), jnp.where(owns, high, low)

    y_a, y_mid, y_b = sum_y[:, :edge_y], sum_y[:, edge_y : 2 * edge_y], sum_y[:, 2 * edge_y :]
    half_x, sent = split(sum_x, "gx")
    got = exchange(jnp.concatenate([sent, side_by_side(y_a)], axis=1), "gx", twin)
    beside = lax.ppermute(near, "pa", [(0, 1), (1, 0)])
    half_x, y_a = half_x + got[:, :wide], y_a + one_above(got[:, wide:])
    got = exchange(jnp.concatenate([half_x, side_by_side(y_b)], axis=1), "gx", next_twin)
    half_x, y_b = half_x + got[:, :wide], y_b + one_above(got[:, wide:])
    sum_y = jnp.concatenate([y_a, y_mid, y_b], axis=1)
    x_a, x_mid, x_b = half_x[:, :edge_x], half_x[:, edge_x : 2 * edge_x], half_x[:, 2 * edge_x :]

    half, sent = split(sum_y, "gy")
    got = exchange(jnp.concatenate([sent, x_a], axis=1), "gy", twin)
    half, x_a = half + got[:, :long], x_a + got[:, long:]
    got = exchange(jnp.concatenate([half, x_b], axis=1), "gy", lambda i: i ^ RING)
    half = half + got[:, :long]
    sent_b = jnp.where(at_end(RING, "gy"), got[:, long:], x_b)
    got = exchange(jnp.concatenate([half, sent_b], axis=1), "gy", odd_twin)
    half = half + got[:, :long]
    got = jnp.where(at_end(count_y, "gy"), 0.0, got[:, long:])
    half, x_b, got = lax.optimization_barrier((half, x_b, got))
    half_x = jnp.concatenate([x_a, x_mid, x_b + got], axis=1)

    half = half + exchange(half, "gy", across)
    half_x = half_x + exchange(half_x, "gx", end_twin)
    got = exchange(half_x, "gx", across)
    other = exchange(half, "gy", twin)
    half_x, half = lax.optimization_barrier((half_x, half))
    half_x = half_x + got
    away_x = exchange(half_x, "gx", twin)

    table_x, base = prepare(lane, volume, beside, count_x)
    own = back_own(column_y, table_y, half, cells_x, count_y, count_x, pad_y, scale_y)
    gradient, residual_x, partial = back_x(
        column_x, table_x, base, half_x, away_x, own, count_x, count_y, pad_x, scale_x
    )
    gradient, residual_y = back_last(
        column_y, table_y, partial, half, other, gradient, count_y, count_x, pad_y, scale_y
    )
    return (gradient, residual_x, residual_y)


def solution(mesh):
    return jax.shard_map(
        steps,
        mesh=mesh,
        in_specs=(P("pa", "gx", "gy"), P(), P(None, "pa", "gy"), P(None, "pa", "gx")),
        out_specs=(P("pa", "gx", "gy"), P(None, "pa", "gy"), P(None, "pa", "gx")),
        check_vma=False,
    )
```

```python
import jax
import jax.numpy as jnp
from jax import lax
from jax.experimental import pallas as pl
from jax.experimental.pallas import tpu as pltpu
from jax.sharding import PartitionSpec as P


LEVELS = 16
RING = 8
CHUNKS = 2
PIECES = 4
LIMIT = pltpu.CompilerParams(vmem_limit_bytes=8 * 1024 * 1024)
SMEM = pltpu.SMEM
VMEM = pltpu.VMEM
F32 = jnp.float32
BF16 = jnp.bfloat16


def interpreted():
    return False


def fill(slopes_ref, family, shape, dim):
    views = slopes_ref.shape[1]
    view = lax.broadcasted_iota(jnp.int32, shape, dim) % views
    slopes = jnp.zeros(shape, jnp.int32)
    for v in range(views):
        slopes = jnp.where(view == v, slopes_ref[family, v], slopes)
    return slopes


def tiled(value, width):
    return jnp.concatenate([value] * (width // value.shape[1]), axis=1)


def lowest_shift(slopes, block, blocks):
    return slopes * (block - blocks // 2) + jnp.minimum(slopes, 0)


def tiles_of(value):
    return [value[:, k : k + 128] for k in range(0, value.shape[1], 128)]


def shifted(tiles, amount, count):
    if amount == 0:
        return tiles[:count]
    lane = lax.broadcasted_iota(jnp.int32, tiles[0].shape, 1)
    rolled = [None if tile is None else pltpu.roll(tile, amount, 1) for tile in tiles]
    out = []
    for k in range(count):
        here, before = rolled[k], rolled[k - 1]
        if here is None and before is None:
            out.append(None)
        elif here is None:
            out.append(jnp.where(lane < amount, before, 0.0))
        elif before is None:
            out.append(jnp.where(lane < amount, 0.0, here))
        else:
            out.append(jnp.where(lane < amount, before, here))
    return out


def barrel(tiles, amounts):
    lane = lax.broadcasted_iota(jnp.int32, amounts.shape, 1)
    low = amounts & 127
    source = (lane - amounts) & 127
    zero = jnp.zeros(amounts.shape, F32)
    turned = [zero if tile is None else jnp.take_along_axis(tile, source, axis=1) for tile in tiles]
    near = [jnp.where(lane < low, turned[k - 1], turned[k]) for k in range(len(tiles))]
    return [jnp.where(amounts >= 128, near[k - 1], near[k]) for k in range(len(tiles))]


def offsets(slopes, block, blocks, cells):
    views = slopes.shape[0]
    lowest = tiled(lowest_shift(slopes, block, blocks).astype(F32), cells)
    cell = lax.broadcasted_iota(jnp.int32, (views, cells), 1) + (block * cells - blocks * cells // 2)
    return tiled(slopes.astype(F32), cells) * (cell.astype(F32) * (1.0 / cells)) - lowest


def hat(offset, level):
    return jnp.maximum(1.0 - jnp.abs(offset - level), 0.0)


def in_vmem(value):
    if interpreted():
        return value
    return pltpu.with_memory_space_constraint(value, VMEM)


def in_hbm(value):
    if interpreted():
        return value
    return pltpu.with_memory_space_constraint(value, pltpu.HBM)


def out_vmem(shape, dtype):
    if interpreted():
        return jax.ShapeDtypeStruct(shape, dtype)
    return VMEM(shape, dtype)


def anywhere():
    return pl.BlockSpec(memory_space=pltpu.HBM)


def vmem():
    return pl.BlockSpec(memory_space=VMEM)


def in_roles(value, odd):
    edge = value.shape[1] // 3
    lead, mid, trail = value[:, :edge], value[:, edge : 2 * edge], value[:, 2 * edge :]
    return jnp.concatenate([jnp.where(odd, lead, trail), mid, jnp.where(odd, trail, lead)], axis=1)


def from_roles(value, odd):
    edge = value.shape[1] // 3
    a, mid, b = value[:, :edge], value[:, edge : 2 * edge], value[:, 2 * edge :]
    return jnp.concatenate([jnp.where(odd, a, b), mid, jnp.where(odd, b, a)], axis=1)


def on_grid(value):
    return jnp.round(value * 32768.0) * (1.0 / 32768.0)


def project(table_ref, volume_ref, rows_ref, slopes, out_ref, plane, family, block, blocks, odd, pad, scale):
    views = slopes.shape[0]
    bins = volume_ref.shape[2 - family]
    width = out_ref.shape[1]
    first = (block == 0).astype(F32)
    amounts = pad - LEVELS + 1 - lowest_shift(slopes, block, blocks)
    count = width // 128
    data = bins // 128
    dims = (((1,), (family,)), ((), ()))
    summands = lax.dot_general(table_ref[...], volume_ref[plane], dims, preferred_element_type=F32)
    total = [None] * count
    for level in range(LEVELS):
        piece = tiles_of(summands[level * views : (level + 1) * views, :]) + [None] * (count - data)
        piece = shifted(piece, LEVELS - 1 - level, count)
        total = [p if t is None else t if p is None else t + p for t, p in zip(total, piece)]
    total = jnp.concatenate(barrel(total, amounts), axis=1) * scale
    known = tiles_of(rows_ref[plane * views : (plane + 1) * views, :] * first) + [None] * (count - data)
    known = [None] * (pad // 128) + shifted(known, pad % 128, count - pad // 128)
    known = jnp.concatenate([jnp.zeros((views, 128), F32) if k is None else k for k in known], axis=1)
    total = on_grid(total - known)
    out_ref[plane * views : (plane + 1) * views, :] = in_roles(total, odd)


def build_table(slopes, block, blocks, cells, table_ref):
    views = slopes.shape[0]
    offset = offsets(slopes, block, blocks, cells)
    for level in range(LEVELS):
        table_ref[level * views : (level + 1) * views, :] = hat(offset, float(level)).astype(BF16)


def gather_rows(measured_ref, rows_ref):
    views, planes, _ = measured_ref.shape
    for plane in range(planes):
        for v in range(views):
            rows_ref[plane * views + v : plane * views + v + 1, :] = measured_ref[v, plane : plane + 1, :]


def forward_kernel(
    slopes_hbm, volume_hbm, mx_hbm, my_hbm,
    x_ref, y_ref, table_y_ref, near_ref, volume_ref, column_x_ref, column_y_ref, lane_ref,
    table_x_ref, slopes_ref, mx_ref, my_ref, rows_x_ref, rows_y_ref, sems,
    *, count_x, count_y, pad_x, pad_y, scale_x, scale_y,
):
    planes, cells_x, cells_y = volume_ref.shape
    fetches = [
        pltpu.make_async_copy(slopes_hbm, slopes_ref, sems.at[0]),
        pltpu.make_async_copy(volume_hbm, volume_ref, sems.at[1]),
        pltpu.make_async_copy(mx_hbm, mx_ref, sems.at[2]),
        pltpu.make_async_copy(my_hbm, my_ref, sems.at[3]),
        pltpu.make_async_copy(volume_hbm.at[pl.ds(1 - lax.axis_index("pa"), 1)], near_ref, sems.at[4]),
    ]
    for fetch in fetches:
        fetch.start()
    here_x, here_y = lax.axis_index("gx"), lax.axis_index("gy")
    fetches[0].wait()
    column_x = fill(slopes_ref, 0, column_x_ref.shape, 0)
    column_y = fill(slopes_ref, 1, column_y_ref.shape, 0)
    column_x_ref[...] = column_x
    column_y_ref[...] = column_y
    lane_ref[...] = fill(slopes_ref, 0, lane_ref.shape, 1)
    build_table(column_y, here_y, count_y, cells_y, table_y_ref)
    build_table(column_x, here_x, count_x, cells_x, table_x_ref)
    fetches[2].wait()
    fetches[3].wait()
    gather_rows(mx_ref, rows_x_ref)
    gather_rows(my_ref, rows_y_ref)
    fetches[1].wait()
    for plane in range(planes):
        project(
            table_y_ref, volume_ref, rows_y_ref, column_y, y_ref, plane, 1, here_y, count_y, here_x % 2 == 1, pad_y, scale_y
        )
    for plane in range(planes):
        project(
            table_x_ref, volume_ref, rows_x_ref, column_x, x_ref, plane, 0, here_x, count_x, here_y % 2 == 1, pad_x, scale_x
        )
    fetches[4].wait()


def forward(slopes, volume, measured_x, measured_y, count_x, count_y, pad_x, pad_y, scale_x, scale_y):
    views = slopes.shape[1]
    planes, cells_x, cells_y = volume.shape

    def body(*refs):
        forward_kernel(
            *refs, count_x=count_x, count_y=count_y, pad_x=pad_x, pad_y=pad_y, scale_x=scale_x, scale_y=scale_y
        )

    return pl.pallas_call(
        body,
        out_shape=(
            out_vmem((planes * views, cells_y + 2 * pad_x), F32),
            out_vmem((planes * views, cells_x + 2 * pad_y), F32),
            out_vmem((LEVELS * views, cells_y), BF16),
            out_vmem((1,) + volume.shape[1:], BF16),
            out_vmem(volume.shape, BF16),
            out_vmem((views, 128), jnp.int32),
            out_vmem((views, 128), jnp.int32),
            out_vmem((8, LEVELS * views), jnp.int32),
        ),
        in_specs=[anywhere()] * 4,
        out_specs=(vmem(),) * 8,
        scratch_shapes=[
            VMEM((LEVELS * views, cells_x), BF16),
            SMEM(slopes.shape, jnp.int32),
            VMEM(measured_x.shape, F32),
            VMEM(measured_y.shape, F32),
            VMEM((planes * views, cells_y), F32),
            VMEM((planes * views, cells_x), F32),
            pltpu.SemaphoreType.DMA((5,)),
        ],
        compiler_params=LIMIT,
        interpret=interpreted(),
        name="forward",
    )(*(in_hbm(value) for value in (slopes, volume, measured_x, measured_y)))


def half_of(index):
    return ((index + 1) // 2) % 2


def spread_into(value, slopes, block, blocks, other, others, pad, scale, spread_ref):
    views, width = value.shape
    bins = width - 2 * pad
    place = lax.broadcasted_iota(jnp.int32, (views, width), 1)
    inside = (place >= jnp.where(other == 0, pad, 0)) & (place < jnp.where(other == others - 1, pad + bins, width))
    value = jnp.where(inside, value * scale, 0.0).astype(BF16).astype(F32)
    tiles = barrel(tiles_of(value), lowest_shift(slopes, block, blocks) + pad)
    skip = 2 * pad // 128
    tiles = tiles[skip:] + tiles[:skip]
    for level in range(LEVELS):
        piece = jnp.concatenate(shifted(tiles, level, bins // 128), axis=1)
        spread_ref[level * views : (level + 1) * views, :] = piece.astype(BF16)


def middle(value, pad):
    tiles = tiles_of(value)
    skip = pad // 128
    tiles = tiles[skip:] + tiles[:skip]
    count = (value.shape[1] - 2 * pad) // 128
    if pad % 128 == 0:
        return jnp.concatenate(tiles[:count], axis=1)
    tiles = tiles[1:] + tiles[:1]
    return jnp.concatenate(shifted(tiles, 128 - pad % 128, count), axis=1)


def prepare_kernel(lane_ref, volume_ref, beside_ref, table_ref, base_ref, *, blocks):
    planes, cells, _ = volume_ref.shape
    block, band = lax.axis_index("gx"), lax.axis_index("pa")
    slopes = lane_ref[...]
    views = slopes.shape[1] // LEVELS
    level = lax.broadcasted_iota(jnp.int32, slopes.shape, 1) // views
    base = (lowest_shift(slopes, block, blocks) + level).astype(F32)[:1]
    slopes = slopes.astype(F32)[:1]
    shape = (cells, LEVELS * views)
    cell = lax.broadcasted_iota(jnp.int32, shape, 0).astype(F32) * (1.0 / cells) + (block - blocks // 2).astype(F32)
    table_ref[...] = jnp.maximum(1.0 - jnp.abs(cell * slopes - base), 0.0).astype(BF16)
    for plane in range(planes):
        here = volume_ref[plane].astype(F32)
        beside = beside_ref[0].astype(F32) * (band == 1 - plane).astype(F32)
        within = volume_ref[1 - plane].astype(F32)
        base_ref[plane] = 0.02 * (2.0 * here - beside - within)


def prepare(lane, volume, beside, blocks):
    def body(*refs):
        prepare_kernel(*refs, blocks=blocks)

    return pl.pallas_call(
        body,
        out_shape=(out_vmem((volume.shape[1], lane.shape[1]), BF16), out_vmem(volume.shape, F32)),
        in_specs=[vmem()] * 3,
        out_specs=(vmem(), vmem()),
        compiler_params=LIMIT,
        interpret=interpreted(),
        name="prepare",
    )(*(in_vmem(value) for value in (lane, volume, beside)))


def store_rows(values, rest_ref, rows_ref):
    planes, views = len(values), rest_ref.shape[0]
    for plane in range(planes):
        rows_ref[plane * views : (plane + 1) * views, :] = values[plane]
    for plane in range(planes):
        for v in range(views):
            rest_ref[v, plane : plane + 1, :] = rows_ref[plane * views + v : plane * views + v + 1, :]


def back_own_kernel(column_ref, table_ref, half_ref, out_ref, spread_ref, *, blocks, others, pad, scale):
    block, other = lax.axis_index("gy"), lax.axis_index("gx")
    value = from_roles(half_ref[...], other % 2 == 1)
    spread_into(value, column_ref[...], block, blocks, other, others, pad, scale, spread_ref)
    dims = (((0,), (0,)), ((), ()))
    out_ref[...] = lax.dot_general(spread_ref[...], table_ref[...], dims, preferred_element_type=F32)


def back_own(column, table, half, bins, blocks, others, pad, scale):
    def body(*refs):
        back_own_kernel(*refs, blocks=blocks, others=others, pad=pad, scale=scale)

    return pl.pallas_call(
        body,
        out_shape=out_vmem((bins, table.shape[1]), F32),
        in_specs=[vmem()] * 3,
        out_specs=vmem(),
        scratch_shapes=[VMEM((table.shape[0], bins), BF16)],
        compiler_params=LIMIT,
        interpret=interpreted(),
        name="back_own",
    )(*(in_vmem(value) for value in (column, table, half)))


def back_x_kernel(
    column_ref, table_ref, base_ref, half_ref, away_ref, own_ref, out_hbm, rest_hbm, partial_ref,
    spread_ref, sum_ref, rows_ref, rest_ref, sems, *, blocks, others, pad, scale,
):
    planes, cells, _ = base_ref.shape
    block, other = lax.axis_index("gx"), lax.axis_index("gy")
    column = column_ref[...]
    flip = other % 2 == 1
    mine = half_of(other)
    held = block % 2
    size = cells // CHUNKS
    copies = []

    def residual_of(plane):
        return from_roles(jnp.where(plane == held, half_ref[...], away_ref[...]), flip)

    for last in range(planes):
        plane = 1 - mine if last else mine
        spread_into(residual_of(plane), column, block, blocks, other, others, pad, scale, spread_ref)
        for c in range(CHUNKS):
            part = pl.ds(c * size, size)
            value = jnp.dot(table_ref[part, :], spread_ref[...], preferred_element_type=F32)
            value = base_ref[pl.ds(plane, 1), part, :] + value[None]
            if last:
                partial_ref[part, :] = value[0]
            else:
                sum_ref[:, part, :] = value + own_ref[part, :][None]
                copies.append(
                    pltpu.make_async_copy(sum_ref.at[:, part], out_hbm.at[pl.ds(plane, 1), part], sems.at[1 + c])
                )
                copies[-1].start()
    store_rows([middle(residual_of(p), pad) for p in range(planes)], rest_ref, rows_ref)
    copies.append(pltpu.make_async_copy(rest_ref, rest_hbm, sems.at[0]))
    copies[-1].start()
    for copy in copies:
        copy.wait()


def back_x(column, table, base, half, away, own, blocks, others, pad, scale):
    planes, cells, bins = base.shape
    views = column.shape[0]

    def body(*refs):
        back_x_kernel(*refs, blocks=blocks, others=others, pad=pad, scale=scale)

    return pl.pallas_call(
        body,
        out_shape=(
            jax.ShapeDtypeStruct(base.shape, F32),
            jax.ShapeDtypeStruct((views, planes, bins), F32),
            out_vmem((cells, bins), F32),
        ),
        in_specs=[vmem()] * 6,
        out_specs=(anywhere(), anywhere(), vmem()),
        scratch_shapes=[
            VMEM((LEVELS * views, bins), BF16),
            VMEM((1, cells, bins), F32),
            VMEM((planes * views, bins), F32),
            VMEM((views, planes, bins), F32),
            pltpu.SemaphoreType.DMA((1 + CHUNKS,)),
        ],
        compiler_params=LIMIT,
        interpret=interpreted(),
        name="back_x",
    )(*(in_vmem(value) for value in (column, table, base, half, away, own)))


def back_last_kernel(
    column_ref, table_ref, partial_ref, half_ref, other_ref, gradient_hbm, out_hbm, rest_hbm,
    spread_ref, sum_ref, rows_ref, rest_ref, sems, *, blocks, others, pad, scale,
):
    bins, _ = partial_ref.shape
    block, other = lax.axis_index("gy"), lax.axis_index("gx")
    flip = other % 2 == 1
    mine = half_of(block)
    value = from_roles(other_ref[...], flip)
    spread_into(value, column_ref[...], block, blocks, other, others, pad, scale, spread_ref)
    dims = (((0,), (0,)), ((), ()))
    size = bins // PIECES
    copies = []
    for c in range(PIECES):
        part = pl.ds(c * size, size)
        back = lax.dot_general(spread_ref[:, c * size : (c + 1) * size], table_ref[...], dims, preferred_element_type=F32)
        sum_ref[:, part, :] = (partial_ref[part, :] + back)[None]
        copies.append(pltpu.make_async_copy(sum_ref.at[:, part], out_hbm.at[pl.ds(1 - mine, 1), part], sems.at[1 + c]))
        copies[-1].start()
    odd = mine == 1
    low = from_roles(jnp.where(odd, other_ref[...], half_ref[...]), flip)
    high = from_roles(jnp.where(odd, half_ref[...], other_ref[...]), flip)
    store_rows([middle(low, pad), middle(high, pad)], rest_ref, rows_ref)
    copies.append(pltpu.make_async_copy(rest_ref, rest_hbm, sems.at[0]))
    copies[-1].start()
    for copy in copies:
        copy.wait()


def back_last(column, table, partial, half, other, gradient, blocks, others, pad, scale):
    bins, cells = partial.shape
    planes = gradient.shape[0]
    views = column.shape[0]

    def body(*refs):
        back_last_kernel(*refs, blocks=blocks, others=others, pad=pad, scale=scale)

    return pl.pallas_call(
        body,
        out_shape=(
            jax.ShapeDtypeStruct(gradient.shape, F32),
            jax.ShapeDtypeStruct((views, planes, bins), F32),
        ),
        in_specs=[vmem()] * 5 + [anywhere()],
        out_specs=(anywhere(), anywhere()),
        scratch_shapes=[
            VMEM((LEVELS * views, bins), BF16),
            VMEM((1, bins, cells), F32),
            VMEM((planes * views, bins), F32),
            VMEM((views, planes, bins), F32),
            pltpu.SemaphoreType.DMA((1 + PIECES,)),
        ],
        input_output_aliases={5: 0},
        compiler_params=LIMIT,
        interpret=interpreted(),
        name="back_last",
    )(*(in_vmem(value) for value in (column, table, partial, half, other)), gradient)


def exchange(value, axis, partner):
    return lax.ppermute(value, axis, [(i, partner(i)) for i in range(lax.axis_size(axis)) if partner(i) != i])


def twin(i):
    return i ^ 1


def odd_twin(i):
    return i - i % RING + (i + (1 if i % 2 else -1)) % RING


def next_twin(i):
    return odd_twin(i) if abs(odd_twin(i) - i) == 1 else i


def across(i):
    return i - i % RING + (i + (-3 if i % 2 else 3)) % RING


def at_end(size, axis):
    index = lax.axis_index(axis) % size
    return (index == 0) | (index == size - 1)


def steps(volume, view_slopes, measured_x, measured_y):
    _, cells_x, cells_y = volume.shape
    count_x = lax.axis_size("gx")
    count_y = lax.axis_size("gy")
    scale_x = float(cells_x * count_x) ** (-0.5)
    scale_y = float(cells_y * count_y) ** (-0.5)
    pad_x, pad_y = 64, 128

    sum_x, sum_y, table_y, near, volume, column_x, column_y, lane = forward(
        view_slopes, volume, measured_x, measured_y, count_x, count_y, pad_x, pad_y, scale_x, scale_y
    )
    wide, long = sum_x.shape[1], sum_y.shape[1]
    edge_x, edge_y = wide // 3, long // 3
    rows = sum_x.shape[0] // 2

    def side_by_side(value):
        return jnp.concatenate([value[:rows], value[rows:]], axis=1)

    def one_above(value):
        return jnp.concatenate([value[:, : value.shape[1] // 2], value[:, value.shape[1] // 2 :]], axis=0)

    def split(value, held):
        owns = held == 0
        low, high = value[:rows], value[rows:]
        return jnp.where(owns, low, high), jnp.where(owns, high, low)

    y_a, y_mid, y_b = sum_y[:, :edge_y], sum_y[:, edge_y : 2 * edge_y], sum_y[:, 2 * edge_y :]
    half_x, sent = split(sum_x, lax.axis_index("gx") % 2)
    got = exchange(jnp.concatenate([sent, side_by_side(y_a)], axis=1), "gx", twin)
    got_b = exchange(y_b, "gx", next_twin)
    beside = lax.ppermute(near, "pa", [(0, 1), (1, 0)])
    half_x, y_a = half_x + got[:, :wide], y_a + one_above(got[:, wide:])
    y_b = y_b + got_b
    sum_y = jnp.concatenate([y_a, y_mid, y_b], axis=1)
    x_a, x_mid, x_b = half_x[:, :edge_x], half_x[:, edge_x : 2 * edge_x], half_x[:, 2 * edge_x :]

    half, sent = split(sum_y, half_of(lax.axis_index("gy")))
    got = exchange(jnp.concatenate([sent, x_a], axis=1), "gy", twin)
    half, x_a = half + got[:, :long], x_a + got[:, long:]
    got = exchange(jnp.concatenate([half, x_b], axis=1), "gy", lambda i: i ^ RING)
    half = half + got[:, :long]
    sent_b = jnp.where(at_end(RING, "gy"), got[:, long:], x_b)
    got = exchange(jnp.concatenate([half, sent_b], axis=1), "gy", odd_twin)
    half = half + got[:, :long]
    got = jnp.where(at_end(count_y, "gy"), 0.0, got[:, long:])
    half, x_b, got = lax.optimization_barrier((half, x_b, got))
    half_x = jnp.concatenate([x_a, x_mid, x_b + got], axis=1)

    half = half + exchange(half, "gy", across)
    got = [exchange(half_x, "gx", lambda i: i ^ bit) for bit in (2, 6, 4)]
    other = exchange(half, "gy", twin)
    half_x, half = lax.optimization_barrier((half_x, half))
    half_x = half_x + got[0] + got[1] + got[2]
    away_x = exchange(half_x, "gx", twin)

    table_x, base = prepare(lane, volume, beside, count_x)
    own = back_own(column_y, table_y, half, cells_x, count_y, count_x, pad_y, scale_y)
    gradient, residual_x, partial = back_x(
        column_x, table_x, base, half_x, away_x, own, count_x, count_y, pad_x, scale_x
    )
    gradient, residual_y = back_last(
        column_y, table_y, partial, half, other, gradient, count_y, count_x, pad_y, scale_y
    )
    return (gradient, residual_x, residual_y)


def solution(mesh):
    return jax.shard_map(
        steps,
        mesh=mesh,
        in_specs=(P("pa", "gx", "gy"), P(), P(None, "pa", "gy"), P(None, "pa", "gx")),
        out_specs=(P("pa", "gx", "gy"), P(None, "pa", "gy"), P(None, "pa", "gx")),
        check_vma=False,
    )
```

```python
import jax
import jax.numpy as jnp
from jax import lax
from jax.experimental import pallas as pl
from jax.experimental.pallas import tpu as pltpu
from jax.sharding import PartitionSpec as P


LEVELS = 16
RING = 8
CHUNKS = 2
PIECES = 4
LIMIT = pltpu.CompilerParams(vmem_limit_bytes=8 * 1024 * 1024)
SMEM = pltpu.SMEM
VMEM = pltpu.VMEM
F32 = jnp.float32
BF16 = jnp.bfloat16


def interpreted():
    return False


def fill(slopes_ref, family, shape, dim):
    views = slopes_ref.shape[1]
    view = lax.broadcasted_iota(jnp.int32, shape, dim) % views
    slopes = jnp.zeros(shape, jnp.int32)
    for v in range(views):
        slopes = jnp.where(view == v, slopes_ref[family, v], slopes)
    return slopes


def tiled(value, width):
    return jnp.concatenate([value] * (width // value.shape[1]), axis=1)


def lowest_shift(slopes, block, blocks):
    return slopes * (block - blocks // 2) + jnp.minimum(slopes, 0)


def tiles_of(value):
    return [value[:, k : k + 128] for k in range(0, value.shape[1], 128)]


def shifted(tiles, amount, count):
    if amount == 0:
        return tiles[:count]
    lane = lax.broadcasted_iota(jnp.int32, tiles[0].shape, 1)
    rolled = [None if tile is None else pltpu.roll(tile, amount, 1) for tile in tiles]
    out = []
    for k in range(count):
        here, before = rolled[k], rolled[k - 1]
        if here is None and before is None:
            out.append(None)
        elif here is None:
            out.append(jnp.where(lane < amount, before, 0.0))
        elif before is None:
            out.append(jnp.where(lane < amount, 0.0, here))
        else:
            out.append(jnp.where(lane < amount, before, here))
    return out


def barrel(tiles, amounts):
    lane = lax.broadcasted_iota(jnp.int32, amounts.shape, 1)
    low = amounts & 127
    source = (lane - amounts) & 127
    zero = jnp.zeros(amounts.shape, F32)
    turned = [zero if tile is None else jnp.take_along_axis(tile, source, axis=1) for tile in tiles]
    near = [jnp.where(lane < low, turned[k - 1], turned[k]) for k in range(len(tiles))]
    return [jnp.where(amounts >= 128, near[k - 1], near[k]) for k in range(len(tiles))]


def offsets(slopes, block, blocks, cells):
    views = slopes.shape[0]
    lowest = tiled(lowest_shift(slopes, block, blocks).astype(F32), cells)
    cell = lax.broadcasted_iota(jnp.int32, (views, cells), 1) + (block * cells - blocks * cells // 2)
    return tiled(slopes.astype(F32), cells) * (cell.astype(F32) * (1.0 / cells)) - lowest


def hat(offset, level):
    return jnp.maximum(1.0 - jnp.abs(offset - level), 0.0)


def in_vmem(value):
    if interpreted():
        return value
    return pltpu.with_memory_space_constraint(value, VMEM)


def in_hbm(value):
    if interpreted():
        return value
    return pltpu.with_memory_space_constraint(value, pltpu.HBM)


def out_vmem(shape, dtype):
    if interpreted():
        return jax.ShapeDtypeStruct(shape, dtype)
    return VMEM(shape, dtype)


def anywhere():
    return pl.BlockSpec(memory_space=pltpu.HBM)


def vmem():
    return pl.BlockSpec(memory_space=VMEM)


def in_roles(value, odd):
    edge = value.shape[1] // 3
    lead, mid, trail = value[:, :edge], value[:, edge : 2 * edge], value[:, 2 * edge :]
    return jnp.concatenate([jnp.where(odd, lead, trail), mid, jnp.where(odd, trail, lead)], axis=1)


def from_roles(value, odd):
    edge = value.shape[1] // 3
    a, mid, b = value[:, :edge], value[:, edge : 2 * edge], value[:, 2 * edge :]
    return jnp.concatenate([jnp.where(odd, a, b), mid, jnp.where(odd, b, a)], axis=1)


def on_grid(value):
    return jnp.round(value * 32768.0) * (1.0 / 32768.0)


def project(table_ref, volume_ref, rows_ref, slopes, out_ref, plane, family, block, blocks, odd, pad, scale):
    views = slopes.shape[0]
    bins = volume_ref.shape[2 - family]
    width = out_ref.shape[1]
    first = (block == 0).astype(F32)
    amounts = pad - LEVELS + 1 - lowest_shift(slopes, block, blocks)
    count = width // 128
    data = bins // 128
    dims = (((1,), (family,)), ((), ()))
    summands = lax.dot_general(table_ref[...], volume_ref[plane], dims, preferred_element_type=F32)
    total = [None] * count
    for level in range(LEVELS):
        piece = tiles_of(summands[level * views : (level + 1) * views, :]) + [None] * (count - data)
        piece = shifted(piece, LEVELS - 1 - level, count)
        total = [p if t is None else t if p is None else t + p for t, p in zip(total, piece)]
    total = jnp.concatenate(barrel(total, amounts), axis=1) * scale
    known = tiles_of(rows_ref[plane * views : (plane + 1) * views, :] * first) + [None] * (count - data)
    known = [None] * (pad // 128) + shifted(known, pad % 128, count - pad // 128)
    known = jnp.concatenate([jnp.zeros((views, 128), F32) if k is None else k for k in known], axis=1)
    total = on_grid(total - known)
    out_ref[plane * views : (plane + 1) * views, :] = in_roles(total, odd)


def build_table(slopes, block, blocks, cells, table_ref):
    views = slopes.shape[0]
    offset = offsets(slopes, block, blocks, cells)
    for level in range(LEVELS):
        table_ref[level * views : (level + 1) * views, :] = hat(offset, float(level)).astype(BF16)


def gather_rows(measured_ref, rows_ref):
    views, planes, _ = measured_ref.shape
    for plane in range(planes):
        for v in range(views):
            rows_ref[plane * views + v : plane * views + v + 1, :] = measured_ref[v, plane : plane + 1, :]


def forward_kernel(
    slopes_hbm, volume_hbm, mx_hbm, my_hbm,
    x_ref, y_ref, table_y_ref, near_ref, volume_ref, column_x_ref, column_y_ref, lane_ref,
    table_x_ref, slopes_ref, mx_ref, my_ref, rows_x_ref, rows_y_ref, sems,
    *, count_x, count_y, pad_x, pad_y, scale_x, scale_y,
):
    planes, cells_x, cells_y = volume_ref.shape
    fetches = [
        pltpu.make_async_copy(slopes_hbm, slopes_ref, sems.at[0]),
        pltpu.make_async_copy(volume_hbm, volume_ref, sems.at[1]),
        pltpu.make_async_copy(mx_hbm, mx_ref, sems.at[2]),
        pltpu.make_async_copy(my_hbm, my_ref, sems.at[3]),
        pltpu.make_async_copy(volume_hbm.at[pl.ds(1 - lax.axis_index("pa"), 1)], near_ref, sems.at[4]),
    ]
    for fetch in fetches:
        fetch.start()
    here_x, here_y = lax.axis_index("gx"), lax.axis_index("gy")
    fetches[0].wait()
    column_x = fill(slopes_ref, 0, column_x_ref.shape, 0)
    column_y = fill(slopes_ref, 1, column_y_ref.shape, 0)
    column_x_ref[...] = column_x
    column_y_ref[...] = column_y
    lane_ref[...] = fill(slopes_ref, 0, lane_ref.shape, 1)
    build_table(column_y, here_y, count_y, cells_y, table_y_ref)
    build_table(column_x, here_x, count_x, cells_x, table_x_ref)
    fetches[2].wait()
    fetches[3].wait()
    gather_rows(mx_ref, rows_x_ref)
    gather_rows(my_ref, rows_y_ref)
    fetches[1].wait()
    for plane in range(planes):
        project(
            table_y_ref, volume_ref, rows_y_ref, column_y, y_ref, plane, 1, here_y, count_y, here_x % 2 == 1, pad_y, scale_y
        )
    for plane in range(planes):
        project(
            table_x_ref, volume_ref, rows_x_ref, column_x, x_ref, plane, 0, here_x, count_x, here_y % 2 == 1, pad_x, scale_x
        )
    fetches[4].wait()


def forward(slopes, volume, measured_x, measured_y, count_x, count_y, pad_x, pad_y, scale_x, scale_y):
    views = slopes.shape[1]
    planes, cells_x, cells_y = volume.shape

    def body(*refs):
        forward_kernel(
            *refs, count_x=count_x, count_y=count_y, pad_x=pad_x, pad_y=pad_y, scale_x=scale_x, scale_y=scale_y
        )

    return pl.pallas_call(
        body,
        out_shape=(
            out_vmem((planes * views, cells_y + 2 * pad_x), F32),
            out_vmem((planes * views, cells_x + 2 * pad_y), F32),
            out_vmem((LEVELS * views, cells_y), BF16),
            out_vmem((1,) + volume.shape[1:], BF16),
            out_vmem(volume.shape, BF16),
            out_vmem((views, 128), jnp.int32),
            out_vmem((views, 128), jnp.int32),
            out_vmem((8, LEVELS * views), jnp.int32),
        ),
        in_specs=[anywhere()] * 4,
        out_specs=(vmem(),) * 8,
        scratch_shapes=[
            VMEM((LEVELS * views, cells_x), BF16),
            SMEM(slopes.shape, jnp.int32),
            VMEM(measured_x.shape, F32),
            VMEM(measured_y.shape, F32),
            VMEM((planes * views, cells_y), F32),
            VMEM((planes * views, cells_x), F32),
            pltpu.SemaphoreType.DMA((5,)),
        ],
        compiler_params=LIMIT,
        interpret=interpreted(),
        name="forward",
    )(*(in_hbm(value) for value in (slopes, volume, measured_x, measured_y)))


def half_of(index):
    return ((index + 1) // 2) % 2


def spread_into(value, slopes, block, blocks, other, others, pad, scale, spread_ref):
    views, width = value.shape
    bins = width - 2 * pad
    place = lax.broadcasted_iota(jnp.int32, (views, width), 1)
    inside = (place >= jnp.where(other == 0, pad, 0)) & (place < jnp.where(other == others - 1, pad + bins, width))
    value = jnp.where(inside, value * scale, 0.0).astype(BF16).astype(F32)
    tiles = barrel(tiles_of(value), lowest_shift(slopes, block, blocks) + pad)
    skip = 2 * pad // 128
    tiles = tiles[skip:] + tiles[:skip]
    for level in range(LEVELS):
        piece = jnp.concatenate(shifted(tiles, level, bins // 128), axis=1)
        spread_ref[level * views : (level + 1) * views, :] = piece.astype(BF16)


def middle(value, pad):
    tiles = tiles_of(value)
    skip = pad // 128
    tiles = tiles[skip:] + tiles[:skip]
    count = (value.shape[1] - 2 * pad) // 128
    if pad % 128 == 0:
        return jnp.concatenate(tiles[:count], axis=1)
    tiles = tiles[1:] + tiles[:1]
    return jnp.concatenate(shifted(tiles, 128 - pad % 128, count), axis=1)


def prepare_kernel(lane_ref, volume_ref, beside_ref, table_ref, base_ref, *, blocks):
    planes, cells, _ = volume_ref.shape
    block, band = lax.axis_index("gx"), lax.axis_index("pa")
    slopes = lane_ref[...]
    views = slopes.shape[1] // LEVELS
    level = lax.broadcasted_iota(jnp.int32, slopes.shape, 1) // views
    base = (lowest_shift(slopes, block, blocks) + level).astype(F32)[:1]
    slopes = slopes.astype(F32)[:1]
    shape = (cells, LEVELS * views)
    cell = lax.broadcasted_iota(jnp.int32, shape, 0).astype(F32) * (1.0 / cells) + (block - blocks // 2).astype(F32)
    table_ref[...] = jnp.maximum(1.0 - jnp.abs(cell * slopes - base), 0.0).astype(BF16)
    for plane in range(planes):
        here = volume_ref[plane].astype(F32)
        beside = beside_ref[0].astype(F32) * (band == 1 - plane).astype(F32)
        within = volume_ref[1 - plane].astype(F32)
        base_ref[plane] = 0.02 * (2.0 * here - beside - within)


def prepare(lane, volume, beside, blocks):
    def body(*refs):
        prepare_kernel(*refs, blocks=blocks)

    return pl.pallas_call(
        body,
        out_shape=(out_vmem((volume.shape[1], lane.shape[1]), BF16), out_vmem(volume.shape, F32)),
        in_specs=[vmem()] * 3,
        out_specs=(vmem(), vmem()),
        compiler_params=LIMIT,
        interpret=interpreted(),
        name="prepare",
    )(*(in_vmem(value) for value in (lane, volume, beside)))


def store_rows(values, rest_ref, rows_ref):
    planes, views = len(values), rest_ref.shape[0]
    for plane in range(planes):
        rows_ref[plane * views : (plane + 1) * views, :] = values[plane]
    for plane in range(planes):
        for v in range(views):
            rest_ref[v, plane : plane + 1, :] = rows_ref[plane * views + v : plane * views + v + 1, :]


def back_own_kernel(column_ref, table_ref, half_ref, out_ref, spread_ref, *, blocks, others, pad, scale):
    block, other = lax.axis_index("gy"), lax.axis_index("gx")
    value = from_roles(half_ref[...], other % 2 == 1)
    spread_into(value, column_ref[...], block, blocks, other, others, pad, scale, spread_ref)
    dims = (((0,), (0,)), ((), ()))
    out_ref[...] = lax.dot_general(spread_ref[...], table_ref[...], dims, preferred_element_type=F32)


def back_own(column, table, half, bins, blocks, others, pad, scale):
    def body(*refs):
        back_own_kernel(*refs, blocks=blocks, others=others, pad=pad, scale=scale)

    return pl.pallas_call(
        body,
        out_shape=out_vmem((bins, table.shape[1]), F32),
        in_specs=[vmem()] * 3,
        out_specs=vmem(),
        scratch_shapes=[VMEM((table.shape[0], bins), BF16)],
        compiler_params=LIMIT,
        interpret=interpreted(),
        name="back_own",
    )(*(in_vmem(value) for value in (column, table, half)))


def back_x_kernel(
    column_ref, table_ref, base_ref, half_ref, away_ref, own_ref, out_hbm, rest_hbm, partial_ref,
    spread_ref, sum_ref, rows_ref, rest_ref, sems, *, blocks, others, pad, scale,
):
    planes, cells, _ = base_ref.shape
    block, other = lax.axis_index("gx"), lax.axis_index("gy")
    column = column_ref[...]
    flip = other % 2 == 1
    mine = half_of(other)
    held = block % 2
    size = cells // CHUNKS
    copies = []

    def residual_of(plane):
        return from_roles(jnp.where(plane == held, half_ref[...], away_ref[...]), flip)

    for last in range(planes):
        plane = 1 - mine if last else mine
        spread_into(residual_of(plane), column, block, blocks, other, others, pad, scale, spread_ref)
        for c in range(CHUNKS):
            part = pl.ds(c * size, size)
            value = jnp.dot(table_ref[part, :], spread_ref[...], preferred_element_type=F32)
            value = base_ref[pl.ds(plane, 1), part, :] + value[None]
            if last:
                partial_ref[part, :] = value[0]
            else:
                sum_ref[:, part, :] = value + own_ref[part, :][None]
                copies.append(
                    pltpu.make_async_copy(sum_ref.at[:, part], out_hbm.at[pl.ds(plane, 1), part], sems.at[1 + c])
                )
                copies[-1].start()
    store_rows([middle(residual_of(p), pad) for p in range(planes)], rest_ref, rows_ref)
    copies.append(pltpu.make_async_copy(rest_ref, rest_hbm, sems.at[0]))
    copies[-1].start()
    for copy in copies:
        copy.wait()


def back_x(column, table, base, half, away, own, blocks, others, pad, scale):
    planes, cells, bins = base.shape
    views = column.shape[0]

    def body(*refs):
        back_x_kernel(*refs, blocks=blocks, others=others, pad=pad, scale=scale)

    return pl.pallas_call(
        body,
        out_shape=(
            jax.ShapeDtypeStruct(base.shape, F32),
            jax.ShapeDtypeStruct((views, planes, bins), F32),
            out_vmem((cells, bins), F32),
        ),
        in_specs=[vmem()] * 6,
        out_specs=(anywhere(), anywhere(), vmem()),
        scratch_shapes=[
            VMEM((LEVELS * views, bins), BF16),
            VMEM((1, cells, bins), F32),
            VMEM((planes * views, bins), F32),
            VMEM((views, planes, bins), F32),
            pltpu.SemaphoreType.DMA((1 + CHUNKS,)),
        ],
        compiler_params=LIMIT,
        interpret=interpreted(),
        name="back_x",
    )(*(in_vmem(value) for value in (column, table, base, half, away, own)))


def back_last_kernel(
    column_ref, table_ref, partial_ref, half_ref, other_ref, gradient_hbm, out_hbm, rest_hbm,
    spread_ref, sum_ref, rows_ref, rest_ref, sems, *, blocks, others, pad, scale,
):
    bins, _ = partial_ref.shape
    block, other = lax.axis_index("gy"), lax.axis_index("gx")
    flip = other % 2 == 1
    mine = half_of(block)
    value = from_roles(other_ref[...], flip)
    spread_into(value, column_ref[...], block, blocks, other, others, pad, scale, spread_ref)
    dims = (((0,), (0,)), ((), ()))
    size = bins // PIECES
    copies = []
    for c in range(PIECES):
        part = pl.ds(c * size, size)
        back = lax.dot_general(spread_ref[:, c * size : (c + 1) * size], table_ref[...], dims, preferred_element_type=F32)
        sum_ref[:, part, :] = (partial_ref[part, :] + back)[None]
        copies.append(pltpu.make_async_copy(sum_ref.at[:, part], out_hbm.at[pl.ds(1 - mine, 1), part], sems.at[1 + c]))
        copies[-1].start()
    odd = mine == 1
    low = from_roles(jnp.where(odd, other_ref[...], half_ref[...]), flip)
    high = from_roles(jnp.where(odd, half_ref[...], other_ref[...]), flip)
    store_rows([middle(low, pad), middle(high, pad)], rest_ref, rows_ref)
    copies.append(pltpu.make_async_copy(rest_ref, rest_hbm, sems.at[0]))
    copies[-1].start()
    for copy in copies:
        copy.wait()


def back_last(column, table, partial, half, other, gradient, blocks, others, pad, scale):
    bins, cells = partial.shape
    planes = gradient.shape[0]
    views = column.shape[0]

    def body(*refs):
        back_last_kernel(*refs, blocks=blocks, others=others, pad=pad, scale=scale)

    return pl.pallas_call(
        body,
        out_shape=(
            jax.ShapeDtypeStruct(gradient.shape, F32),
            jax.ShapeDtypeStruct((views, planes, bins), F32),
        ),
        in_specs=[vmem()] * 5 + [anywhere()],
        out_specs=(anywhere(), anywhere()),
        scratch_shapes=[
            VMEM((LEVELS * views, bins), BF16),
            VMEM((1, bins, cells), F32),
            VMEM((planes * views, bins), F32),
            VMEM((views, planes, bins), F32),
            pltpu.SemaphoreType.DMA((1 + PIECES,)),
        ],
        input_output_aliases={5: 0},
        compiler_params=LIMIT,
        interpret=interpreted(),
        name="back_last",
    )(*(in_vmem(value) for value in (column, table, partial, half, other)), gradient)


def exchange(value, axis, partner):
    return lax.ppermute(value, axis, [(i, partner(i)) for i in range(lax.axis_size(axis)) if partner(i) != i])


def twin(i):
    return i ^ 1


def odd_twin(i):
    return i - i % RING + (i + (1 if i % 2 else -1)) % RING


def next_twin(i):
    return odd_twin(i) if abs(odd_twin(i) - i) == 1 else i


def across(i):
    return i - i % RING + (i + (-3 if i % 2 else 3)) % RING


def seam(value, axis):
    ends = range(RING, lax.axis_size(axis), RING)
    pairs = [(i - 1, i) for i in ends] + [(i, i - 1) for i in ends]
    return lax.ppermute(value, axis, pairs)


def at_end(size, axis):
    index = lax.axis_index(axis) % size
    return (index == 0) | (index == size - 1)


def steps(volume, view_slopes, measured_x, measured_y):
    _, cells_x, cells_y = volume.shape
    count_x = lax.axis_size("gx")
    count_y = lax.axis_size("gy")
    scale_x = float(cells_x * count_x) ** (-0.5)
    scale_y = float(cells_y * count_y) ** (-0.5)
    pad_x, pad_y = 64, 128

    sum_x, sum_y, table_y, near, volume, column_x, column_y, lane = forward(
        view_slopes, volume, measured_x, measured_y, count_x, count_y, pad_x, pad_y, scale_x, scale_y
    )
    wide, long = sum_x.shape[1], sum_y.shape[1]
    edge_x, edge_y = wide // 3, long // 3
    rows = sum_x.shape[0] // 2

    def side_by_side(value):
        return jnp.concatenate([value[:rows], value[rows:]], axis=1)

    def one_above(value):
        return jnp.concatenate([value[:, : value.shape[1] // 2], value[:, value.shape[1] // 2 :]], axis=0)

    def split(value, held):
        owns = held == 0
        low, high = value[:rows], value[rows:]
        return jnp.where(owns, low, high), jnp.where(owns, high, low)

    y_a, y_mid, y_b = sum_y[:, :edge_y], sum_y[:, edge_y : 2 * edge_y], sum_y[:, 2 * edge_y :]
    half_x, sent = split(sum_x, lax.axis_index("gx") % 2)
    got = exchange(jnp.concatenate([sent, side_by_side(y_a)], axis=1), "gx", twin)
    got_b = exchange(y_b, "gx", next_twin)
    beside = lax.ppermute(near, "pa", [(0, 1), (1, 0)])
    half_x, y_a = half_x + got[:, :wide], y_a + one_above(got[:, wide:])
    y_b = y_b + got_b
    sum_y = jnp.concatenate([y_a, y_mid, y_b], axis=1)
    half, sent = split(sum_y, half_of(lax.axis_index("gy")))
    got_y = exchange(sent, "gy", twin)
    got_x = exchange(half_x, "gx", lambda i: i ^ 2)
    half = half + got_y
    half_x, half = lax.optimization_barrier((half_x, half))
    half_x = half_x + got_x
    got_y = exchange(half, "gy", lambda i: i ^ RING)
    got_x = exchange(half_x, "gx", lambda i: i ^ 6)
    half, half_x = half + got_y, half_x + got_x
    x_a, x_mid, x_b = half_x[:, :edge_x], half_x[:, edge_x : 2 * edge_x], half_x[:, 2 * edge_x :]

    got = exchange(jnp.concatenate([half, x_b], axis=1), "gy", odd_twin)
    got_b = seam(x_b, "gy")
    half = half + got[:, :long]
    x_a, half = lax.optimization_barrier((x_a, half))
    got_y = exchange(half, "gy", across)
    got_a = exchange(x_a, "gy", twin)
    half = half + got_y
    other = exchange(half, "gy", twin)
    x_a, half, got = lax.optimization_barrier((x_a, half, got))
    x_b = x_b + jnp.where(at_end(RING, "gy"), 0.0, got[:, long:]) + got_b
    half_x = jnp.concatenate([x_a + got_a, x_mid, x_b], axis=1)
    away_x = exchange(half_x, "gx", twin)

    table_x, base = prepare(lane, volume, beside, count_x)
    own = back_own(column_y, table_y, half, cells_x, count_y, count_x, pad_y, scale_y)
    gradient, residual_x, partial = back_x(
        column_x, table_x, base, half_x, away_x, own, count_x, count_y, pad_x, scale_x
    )
    gradient, residual_y = back_last(
        column_y, table_y, partial, half, other, gradient, count_y, count_x, pad_y, scale_y
    )
    return (gradient, residual_x, residual_y)


def solution(mesh):
    return jax.shard_map(
        steps,
        mesh=mesh,
        in_specs=(P("pa", "gx", "gy"), P(), P(None, "pa", "gy"), P(None, "pa", "gx")),
        out_specs=(P("pa", "gx", "gy"), P(None, "pa", "gy"), P(None, "pa", "gx")),
        check_vma=False,
    )
```

```python
import jax
import jax.numpy as jnp
from jax import lax
from jax.experimental import pallas as pl
from jax.experimental.pallas import tpu as pltpu
from jax.sharding import PartitionSpec as P


LEVELS = 16
RING = 8
CHUNKS = 2
PIECES = 4
LIMIT = pltpu.CompilerParams(vmem_limit_bytes=8 * 1024 * 1024)
SMEM = pltpu.SMEM
VMEM = pltpu.VMEM
F32 = jnp.float32
BF16 = jnp.bfloat16


def interpreted():
    return False


def fill(slopes_ref, family, shape, dim):
    views = slopes_ref.shape[1]
    view = lax.broadcasted_iota(jnp.int32, shape, dim) % views
    slopes = jnp.zeros(shape, jnp.int32)
    for v in range(views):
        slopes = jnp.where(view == v, slopes_ref[family, v], slopes)
    return slopes


def tiled(value, width):
    return jnp.concatenate([value] * (width // value.shape[1]), axis=1)


def lowest_shift(slopes, block, blocks):
    return slopes * (block - blocks // 2) + jnp.minimum(slopes, 0)


def tiles_of(value):
    return [value[:, k : k + 128] for k in range(0, value.shape[1], 128)]


def shifted(tiles, amount, count):
    if amount == 0:
        return tiles[:count]
    lane = lax.broadcasted_iota(jnp.int32, tiles[0].shape, 1)
    rolled = [None if tile is None else pltpu.roll(tile, amount, 1) for tile in tiles]
    out = []
    for k in range(count):
        here, before = rolled[k], rolled[k - 1]
        if here is None and before is None:
            out.append(None)
        elif here is None:
            out.append(jnp.where(lane < amount, before, 0.0))
        elif before is None:
            out.append(jnp.where(lane < amount, 0.0, here))
        else:
            out.append(jnp.where(lane < amount, before, here))
    return out


def barrel(tiles, amounts):
    lane = lax.broadcasted_iota(jnp.int32, amounts.shape, 1)
    low = amounts & 127
    source = (lane - amounts) & 127
    zero = jnp.zeros(amounts.shape, F32)
    turned = [zero if tile is None else jnp.take_along_axis(tile, source, axis=1) for tile in tiles]
    near = [jnp.where(lane < low, turned[k - 1], turned[k]) for k in range(len(tiles))]
    return [jnp.where(amounts >= 128, near[k - 1], near[k]) for k in range(len(tiles))]


def offsets(slopes, block, blocks, cells):
    views = slopes.shape[0]
    lowest = tiled(lowest_shift(slopes, block, blocks).astype(F32), cells)
    cell = lax.broadcasted_iota(jnp.int32, (views, cells), 1) + (block * cells - blocks * cells // 2)
    return tiled(slopes.astype(F32), cells) * (cell.astype(F32) * (1.0 / cells)) - lowest


def hat(offset, level):
    return jnp.maximum(1.0 - jnp.abs(offset - level), 0.0)


def in_vmem(value):
    if interpreted():
        return value
    return pltpu.with_memory_space_constraint(value, VMEM)


def in_hbm(value):
    if interpreted():
        return value
    return pltpu.with_memory_space_constraint(value, pltpu.HBM)


def out_vmem(shape, dtype):
    if interpreted():
        return jax.ShapeDtypeStruct(shape, dtype)
    return VMEM(shape, dtype)


def anywhere():
    return pl.BlockSpec(memory_space=pltpu.HBM)


def vmem():
    return pl.BlockSpec(memory_space=VMEM)


def in_roles(value, odd):
    edge = value.shape[1] // 3
    lead, mid, trail = value[:, :edge], value[:, edge : 2 * edge], value[:, 2 * edge :]
    return jnp.concatenate([jnp.where(odd, lead, trail), mid, jnp.where(odd, trail, lead)], axis=1)


def from_roles(value, odd):
    edge = value.shape[1] // 3
    a, mid, b = value[:, :edge], value[:, edge : 2 * edge], value[:, 2 * edge :]
    return jnp.concatenate([jnp.where(odd, a, b), mid, jnp.where(odd, b, a)], axis=1)


def on_grid(value):
    return jnp.round(value * 32768.0) * (1.0 / 32768.0)


def project(table_ref, volume_ref, rows_ref, slopes, out_ref, plane, family, block, blocks, odd, pad, scale):
    views = slopes.shape[0]
    bins = volume_ref.shape[2 - family]
    width = out_ref.shape[1]
    first = (block == 0).astype(F32)
    amounts = pad - LEVELS + 1 - lowest_shift(slopes, block, blocks)
    count = width // 128
    data = bins // 128
    dims = (((1,), (family,)), ((), ()))
    summands = lax.dot_general(table_ref[...], volume_ref[plane], dims, preferred_element_type=F32)
    total = [None] * count
    for level in range(LEVELS):
        piece = tiles_of(summands[level * views : (level + 1) * views, :]) + [None] * (count - data)
        piece = shifted(piece, LEVELS - 1 - level, count)
        total = [p if t is None else t if p is None else t + p for t, p in zip(total, piece)]
    total = jnp.concatenate(barrel(total, amounts), axis=1) * scale
    known = tiles_of(rows_ref[plane * views : (plane + 1) * views, :] * first) + [None] * (count - data)
    known = [None] * (pad // 128) + shifted(known, pad % 128, count - pad // 128)
    known = jnp.concatenate([jnp.zeros((views, 128), F32) if k is None else k for k in known], axis=1)
    total = on_grid(total - known)
    out_ref[plane * views : (plane + 1) * views, :] = in_roles(total, odd)


def build_table(slopes, block, blocks, cells, table_ref):
    views = slopes.shape[0]
    offset = offsets(slopes, block, blocks, cells)
    for level in range(LEVELS):
        table_ref[level * views : (level + 1) * views, :] = hat(offset, float(level)).astype(BF16)


def gather_rows(measured_ref, rows_ref):
    views, planes, _ = measured_ref.shape
    for plane in range(planes):
        for v in range(views):
            rows_ref[plane * views + v : plane * views + v + 1, :] = measured_ref[v, plane : plane + 1, :]


def forward_kernel(
    slopes_hbm, volume_hbm, mx_hbm, my_hbm,
    x_ref, y_ref, table_y_ref, near_ref, volume_ref, column_x_ref, column_y_ref, lane_ref,
    table_x_ref, slopes_ref, mx_ref, my_ref, rows_x_ref, rows_y_ref, sems,
    *, count_x, count_y, pad_x, pad_y, scale_x, scale_y,
):
    planes, cells_x, cells_y = volume_ref.shape
    fetches = [
        pltpu.make_async_copy(slopes_hbm, slopes_ref, sems.at[0]),
        pltpu.make_async_copy(volume_hbm, volume_ref, sems.at[1]),
        pltpu.make_async_copy(mx_hbm, mx_ref, sems.at[2]),
        pltpu.make_async_copy(my_hbm, my_ref, sems.at[3]),
        pltpu.make_async_copy(volume_hbm.at[pl.ds(1 - lax.axis_index("pa"), 1)], near_ref, sems.at[4]),
    ]
    for fetch in fetches:
        fetch.start()
    here_x, here_y = lax.axis_index("gx"), lax.axis_index("gy")
    fetches[0].wait()
    column_x = fill(slopes_ref, 0, column_x_ref.shape, 0)
    column_y = fill(slopes_ref, 1, column_y_ref.shape, 0)
    column_x_ref[...] = column_x
    column_y_ref[...] = column_y
    lane_ref[...] = fill(slopes_ref, 0, lane_ref.shape, 1)
    build_table(column_y, here_y, count_y, cells_y, table_y_ref)
    build_table(column_x, here_x, count_x, cells_x, table_x_ref)
    fetches[2].wait()
    fetches[3].wait()
    gather_rows(mx_ref, rows_x_ref)
    gather_rows(my_ref, rows_y_ref)
    fetches[1].wait()
    for plane in range(planes):
        project(
            table_y_ref, volume_ref, rows_y_ref, column_y, y_ref, plane, 1, here_y, count_y, here_x % 2 == 1, pad_y, scale_y
        )
    for plane in range(planes):
        project(
            table_x_ref, volume_ref, rows_x_ref, column_x, x_ref, plane, 0, here_x, count_x, here_y % 2 == 1, pad_x, scale_x
        )
    fetches[4].wait()


def forward(slopes, volume, measured_x, measured_y, count_x, count_y, pad_x, pad_y, scale_x, scale_y):
    views = slopes.shape[1]
    planes, cells_x, cells_y = volume.shape

    def body(*refs):
        forward_kernel(
            *refs, count_x=count_x, count_y=count_y, pad_x=pad_x, pad_y=pad_y, scale_x=scale_x, scale_y=scale_y
        )

    return pl.pallas_call(
        body,
        out_shape=(
            out_vmem((planes * views, cells_y + 2 * pad_x), F32),
            out_vmem((planes * views, cells_x + 2 * pad_y), F32),
            out_vmem((LEVELS * views, cells_y), BF16),
            out_vmem((1,) + volume.shape[1:], BF16),
            out_vmem(volume.shape, BF16),
            out_vmem((views, 128), jnp.int32),
            out_vmem((views, 128), jnp.int32),
            out_vmem((8, LEVELS * views), jnp.int32),
        ),
        in_specs=[anywhere()] * 4,
        out_specs=(vmem(),) * 8,
        scratch_shapes=[
            VMEM((LEVELS * views, cells_x), BF16),
            SMEM(slopes.shape, jnp.int32),
            VMEM(measured_x.shape, F32),
            VMEM(measured_y.shape, F32),
            VMEM((planes * views, cells_y), F32),
            VMEM((planes * views, cells_x), F32),
            pltpu.SemaphoreType.DMA((5,)),
        ],
        compiler_params=LIMIT,
        interpret=interpreted(),
        name="forward",
    )(*(in_hbm(value) for value in (slopes, volume, measured_x, measured_y)))


def half_of(index):
    return ((index + 1) // 2) % 2


def spread_into(value, slopes, block, blocks, other, others, pad, scale, spread_ref):
    views, width = value.shape
    bins = width - 2 * pad
    place = lax.broadcasted_iota(jnp.int32, (views, width), 1)
    inside = (place >= jnp.where(other == 0, pad, 0)) & (place < jnp.where(other == others - 1, pad + bins, width))
    value = jnp.where(inside, value * scale, 0.0).astype(BF16).astype(F32)
    tiles = barrel(tiles_of(value), lowest_shift(slopes, block, blocks) + pad)
    skip = 2 * pad // 128
    tiles = tiles[skip:] + tiles[:skip]
    for level in range(LEVELS):
        piece = jnp.concatenate(shifted(tiles, level, bins // 128), axis=1)
        spread_ref[level * views : (level + 1) * views, :] = piece.astype(BF16)


def middle(value, pad):
    tiles = tiles_of(value)
    skip = pad // 128
    tiles = tiles[skip:] + tiles[:skip]
    count = (value.shape[1] - 2 * pad) // 128
    if pad % 128 == 0:
        return jnp.concatenate(tiles[:count], axis=1)
    tiles = tiles[1:] + tiles[:1]
    return jnp.concatenate(shifted(tiles, 128 - pad % 128, count), axis=1)


def prepare_kernel(lane_ref, volume_ref, beside_ref, table_ref, base_ref, *, blocks):
    planes, cells, _ = volume_ref.shape
    block, band = lax.axis_index("gx"), lax.axis_index("pa")
    slopes = lane_ref[...]
    views = slopes.shape[1] // LEVELS
    level = lax.broadcasted_iota(jnp.int32, slopes.shape, 1) // views
    base = (lowest_shift(slopes, block, blocks) + level).astype(F32)[:1]
    slopes = slopes.astype(F32)[:1]
    shape = (cells, LEVELS * views)
    cell = lax.broadcasted_iota(jnp.int32, shape, 0).astype(F32) * (1.0 / cells) + (block - blocks // 2).astype(F32)
    table_ref[...] = jnp.maximum(1.0 - jnp.abs(cell * slopes - base), 0.0).astype(BF16)
    for plane in range(planes):
        here = volume_ref[plane].astype(F32)
        beside = beside_ref[0].astype(F32) * (band == 1 - plane).astype(F32)
        within = volume_ref[1 - plane].astype(F32)
        base_ref[plane] = 0.02 * (2.0 * here - beside - within)


def prepare(lane, volume, beside, blocks):
    def body(*refs):
        prepare_kernel(*refs, blocks=blocks)

    return pl.pallas_call(
        body,
        out_shape=(out_vmem((volume.shape[1], lane.shape[1]), BF16), out_vmem(volume.shape, F32)),
        in_specs=[vmem()] * 3,
        out_specs=(vmem(), vmem()),
        compiler_params=LIMIT,
        interpret=interpreted(),
        name="prepare",
    )(*(in_vmem(value) for value in (lane, volume, beside)))


def store_rows(values, rest_ref, rows_ref):
    planes, views = len(values), rest_ref.shape[0]
    for plane in range(planes):
        rows_ref[plane * views : (plane + 1) * views, :] = values[plane]
    for plane in range(planes):
        for v in range(views):
            rest_ref[v, plane : plane + 1, :] = rows_ref[plane * views + v : plane * views + v + 1, :]


def back_own_kernel(column_ref, table_ref, half_ref, out_ref, spread_ref, *, blocks, others, pad, scale):
    block, other = lax.axis_index("gy"), lax.axis_index("gx")
    value = from_roles(half_ref[...], other % 2 == 1)
    spread_into(value, column_ref[...], block, blocks, other, others, pad, scale, spread_ref)
    dims = (((0,), (0,)), ((), ()))
    out_ref[...] = lax.dot_general(spread_ref[...], table_ref[...], dims, preferred_element_type=F32)


def back_own(column, table, half, bins, blocks, others, pad, scale):
    def body(*refs):
        back_own_kernel(*refs, blocks=blocks, others=others, pad=pad, scale=scale)

    return pl.pallas_call(
        body,
        out_shape=out_vmem((bins, table.shape[1]), F32),
        in_specs=[vmem()] * 3,
        out_specs=vmem(),
        scratch_shapes=[VMEM((table.shape[0], bins), BF16)],
        compiler_params=LIMIT,
        interpret=interpreted(),
        name="back_own",
    )(*(in_vmem(value) for value in (column, table, half)))


def back_x_kernel(
    column_ref, table_ref, base_ref, half_ref, away_ref, own_ref, out_hbm, rest_hbm, partial_ref,
    spread_ref, sum_ref, rows_ref, rest_ref, sems, *, blocks, others, pad, scale,
):
    planes, cells, _ = base_ref.shape
    block, other = lax.axis_index("gx"), lax.axis_index("gy")
    column = column_ref[...]
    flip = other % 2 == 1
    mine = half_of(other)
    held = half_of(block)
    size = cells // CHUNKS
    copies = []

    def residual_of(plane):
        return from_roles(jnp.where(plane == held, half_ref[...], away_ref[...]), flip)

    for last in range(planes):
        plane = 1 - mine if last else mine
        spread_into(residual_of(plane), column, block, blocks, other, others, pad, scale, spread_ref)
        for c in range(CHUNKS):
            part = pl.ds(c * size, size)
            value = jnp.dot(table_ref[part, :], spread_ref[...], preferred_element_type=F32)
            value = base_ref[pl.ds(plane, 1), part, :] + value[None]
            if last:
                partial_ref[part, :] = value[0]
            else:
                sum_ref[:, part, :] = value + own_ref[part, :][None]
                copies.append(
                    pltpu.make_async_copy(sum_ref.at[:, part], out_hbm.at[pl.ds(plane, 1), part], sems.at[1 + c])
                )
                copies[-1].start()
    store_rows([middle(residual_of(p), pad) for p in range(planes)], rest_ref, rows_ref)
    copies.append(pltpu.make_async_copy(rest_ref, rest_hbm, sems.at[0]))
    copies[-1].start()
    for copy in copies:
        copy.wait()


def back_x(column, table, base, half, away, own, blocks, others, pad, scale):
    planes, cells, bins = base.shape
    views = column.shape[0]

    def body(*refs):
        back_x_kernel(*refs, blocks=blocks, others=others, pad=pad, scale=scale)

    return pl.pallas_call(
        body,
        out_shape=(
            jax.ShapeDtypeStruct(base.shape, F32),
            jax.ShapeDtypeStruct((views, planes, bins), F32),
            out_vmem((cells, bins), F32),
        ),
        in_specs=[vmem()] * 6,
        out_specs=(anywhere(), anywhere(), vmem()),
        scratch_shapes=[
            VMEM((LEVELS * views, bins), BF16),
            VMEM((1, cells, bins), F32),
            VMEM((planes * views, bins), F32),
            VMEM((views, planes, bins), F32),
            pltpu.SemaphoreType.DMA((1 + CHUNKS,)),
        ],
        compiler_params=LIMIT,
        interpret=interpreted(),
        name="back_x",
    )(*(in_vmem(value) for value in (column, table, base, half, away, own)))


def back_last_kernel(
    column_ref, table_ref, partial_ref, half_ref, other_ref, gradient_hbm, out_hbm, rest_hbm,
    spread_ref, sum_ref, rows_ref, rest_ref, sems, *, blocks, others, pad, scale,
):
    bins, _ = partial_ref.shape
    block, other = lax.axis_index("gy"), lax.axis_index("gx")
    flip = other % 2 == 1
    mine = half_of(block)
    value = from_roles(other_ref[...], flip)
    spread_into(value, column_ref[...], block, blocks, other, others, pad, scale, spread_ref)
    dims = (((0,), (0,)), ((), ()))
    size = bins // PIECES
    copies = []
    for c in range(PIECES):
        part = pl.ds(c * size, size)
        back = lax.dot_general(spread_ref[:, c * size : (c + 1) * size], table_ref[...], dims, preferred_element_type=F32)
        sum_ref[:, part, :] = (partial_ref[part, :] + back)[None]
        copies.append(pltpu.make_async_copy(sum_ref.at[:, part], out_hbm.at[pl.ds(1 - mine, 1), part], sems.at[1 + c]))
        copies[-1].start()
    odd = mine == 1
    low = from_roles(jnp.where(odd, other_ref[...], half_ref[...]), flip)
    high = from_roles(jnp.where(odd, half_ref[...], other_ref[...]), flip)
    store_rows([middle(low, pad), middle(high, pad)], rest_ref, rows_ref)
    copies.append(pltpu.make_async_copy(rest_ref, rest_hbm, sems.at[0]))
    copies[-1].start()
    for copy in copies:
        copy.wait()


def back_last(column, table, partial, half, other, gradient, blocks, others, pad, scale):
    bins, cells = partial.shape
    planes = gradient.shape[0]
    views = column.shape[0]

    def body(*refs):
        back_last_kernel(*refs, blocks=blocks, others=others, pad=pad, scale=scale)

    return pl.pallas_call(
        body,
        out_shape=(
            jax.ShapeDtypeStruct(gradient.shape, F32),
            jax.ShapeDtypeStruct((views, planes, bins), F32),
        ),
        in_specs=[vmem()] * 5 + [anywhere()],
        out_specs=(anywhere(), anywhere()),
        scratch_shapes=[
            VMEM((LEVELS * views, bins), BF16),
            VMEM((1, bins, cells), F32),
            VMEM((planes * views, bins), F32),
            VMEM((views, planes, bins), F32),
            pltpu.SemaphoreType.DMA((1 + PIECES,)),
        ],
        input_output_aliases={5: 0},
        compiler_params=LIMIT,
        interpret=interpreted(),
        name="back_last",
    )(*(in_vmem(value) for value in (column, table, partial, half, other)), gradient)


def exchange(value, axis, partner):
    return lax.ppermute(value, axis, [(i, partner(i)) for i in range(lax.axis_size(axis))])


def twin(i):
    return i ^ 1


def odd_twin(i):
    return i - i % RING + (i + (1 if i % 2 else -1)) % RING


def across(i):
    return i - i % RING + (i + (-3 if i % 2 else 3)) % RING


def at_end(size, axis):
    index = lax.axis_index(axis) % size
    return (index == 0) | (index == size - 1)


def steps(volume, view_slopes, measured_x, measured_y):
    _, cells_x, cells_y = volume.shape
    count_x = lax.axis_size("gx")
    count_y = lax.axis_size("gy")
    scale_x = float(cells_x * count_x) ** (-0.5)
    scale_y = float(cells_y * count_y) ** (-0.5)
    pad_x, pad_y = 64, 128

    sum_x, sum_y, table_y, near, volume, column_x, column_y, lane = forward(
        view_slopes, volume, measured_x, measured_y, count_x, count_y, pad_x, pad_y, scale_x, scale_y
    )
    wide, long = sum_x.shape[1], sum_y.shape[1]
    edge_x, edge_y = wide // 3, long // 3
    rows = sum_x.shape[0] // 2

    def side_by_side(value):
        return jnp.concatenate([value[:rows], value[rows:]], axis=1)

    def one_above(value):
        return jnp.concatenate([value[:, : value.shape[1] // 2], value[:, value.shape[1] // 2 :]], axis=0)

    def split(value, axis):
        owns = half_of(lax.axis_index(axis)) == 0
        low, high = value[:rows], value[rows:]
        return jnp.where(owns, low, high), jnp.where(owns, high, low)

    y_a, y_mid, y_b = sum_y[:, :edge_y], sum_y[:, edge_y : 2 * edge_y], sum_y[:, 2 * edge_y :]
    half_x, sent = split(sum_x, "gx")
    got = exchange(jnp.concatenate([sent, side_by_side(y_a)], axis=1), "gx", twin)
    beside = lax.ppermute(near, "pa", [(0, 1), (1, 0)])
    half_x, y_a = half_x + got[:, :wide], y_a + one_above(got[:, wide:])
    got = exchange(jnp.concatenate([half_x, side_by_side(y_b)], axis=1), "gx", odd_twin)
    half_x = half_x + got[:, :wide]
    y_b = y_b + jnp.where(at_end(count_x, "gx"), 0.0, one_above(got[:, wide:]))
    sum_y = jnp.concatenate([y_a, y_mid, y_b], axis=1)
    x_a, x_mid, x_b = half_x[:, :edge_x], half_x[:, edge_x : 2 * edge_x], half_x[:, 2 * edge_x :]

    half, sent = split(sum_y, "gy")
    got = exchange(jnp.concatenate([sent, x_a], axis=1), "gy", twin)
    half, x_a = half + got[:, :long], x_a + got[:, long:]
    got = exchange(jnp.concatenate([half, x_b], axis=1), "gy", lambda i: i ^ RING)
    half = half + got[:, :long]
    sent_b = jnp.where(at_end(RING, "gy"), got[:, long:], x_b)
    got = exchange(jnp.concatenate([half, sent_b], axis=1), "gy", odd_twin)
    half = half + got[:, :long]
    got = jnp.where(at_end(count_y, "gy"), 0.0, got[:, long:])
    half, x_b, got = lax.optimization_barrier((half, x_b, got))
    half_x = jnp.concatenate([x_a, x_mid, x_b + got], axis=1)

    half = half + exchange(half, "gy", across)
    got = exchange(half_x, "gx", across)
    other = exchange(half, "gy", twin)
    half_x, half = lax.optimization_barrier((half_x, half))
    half_x = half_x + got
    away_x = exchange(half_x, "gx", twin)

    table_x, base = prepare(lane, volume, beside, count_x)
    own = back_own(column_y, table_y, half, cells_x, count_y, count_x, pad_y, scale_y)
    gradient, residual_x, partial = back_x(
        column_x, table_x, base, half_x, away_x, own, count_x, count_y, pad_x, scale_x
    )
    gradient, residual_y = back_last(
        column_y, table_y, partial, half, other, gradient, count_y, count_x, pad_y, scale_y
    )
    return (gradient, residual_x, residual_y)


def solution(mesh):
    return jax.shard_map(
        steps,
        mesh=mesh,
        in_specs=(P("pa", "gx", "gy"), P(), P(None, "pa", "gy"), P(None, "pa", "gx")),
        out_specs=(P("pa", "gx", "gy"), P(None, "pa", "gy"), P(None, "pa", "gx")),
        check_vma=False,
    )
```

```python
import jax
import jax.numpy as jnp
from jax import lax
from jax.experimental import pallas as pl
from jax.experimental.pallas import tpu as pltpu
from jax.sharding import PartitionSpec as P


LEVELS = 16
RING = 8
CHUNKS = 2
PIECES = 4
LIMIT = pltpu.CompilerParams(vmem_limit_bytes=8 * 1024 * 1024)
SMEM = pltpu.SMEM
VMEM = pltpu.VMEM
F32 = jnp.float32
BF16 = jnp.bfloat16


def interpreted():
    return False


def fill(slopes_ref, family, shape, dim):
    views = slopes_ref.shape[1]
    view = lax.broadcasted_iota(jnp.int32, shape, dim) % views
    slopes = jnp.zeros(shape, jnp.int32)
    for v in range(views):
        slopes = jnp.where(view == v, slopes_ref[family, v], slopes)
    return slopes


def tiled(value, width):
    return jnp.concatenate([value] * (width // value.shape[1]), axis=1)


def lowest_shift(slopes, block, blocks):
    return slopes * (block - blocks // 2) + jnp.minimum(slopes, 0)


def tiles_of(value):
    return [value[:, k : k + 128] for k in range(0, value.shape[1], 128)]


def shifted(tiles, amount, count):
    if amount == 0:
        return tiles[:count]
    lane = lax.broadcasted_iota(jnp.int32, tiles[0].shape, 1)
    rolled = [None if tile is None else pltpu.roll(tile, amount, 1) for tile in tiles]
    out = []
    for k in range(count):
        here, before = rolled[k], rolled[k - 1]
        if here is None and before is None:
            out.append(None)
        elif here is None:
            out.append(jnp.where(lane < amount, before, 0.0))
        elif before is None:
            out.append(jnp.where(lane < amount, 0.0, here))
        else:
            out.append(jnp.where(lane < amount, before, here))
    return out


def barrel(tiles, amounts):
    lane = lax.broadcasted_iota(jnp.int32, amounts.shape, 1)
    low = amounts & 127
    source = (lane - amounts) & 127
    zero = jnp.zeros(amounts.shape, F32)
    turned = [zero if tile is None else jnp.take_along_axis(tile, source, axis=1) for tile in tiles]
    near = [jnp.where(lane < low, turned[k - 1], turned[k]) for k in range(len(tiles))]
    return [jnp.where(amounts >= 128, near[k - 1], near[k]) for k in range(len(tiles))]


def offsets(slopes, block, blocks, cells):
    views = slopes.shape[0]
    lowest = tiled(lowest_shift(slopes, block, blocks).astype(F32), cells)
    cell = lax.broadcasted_iota(jnp.int32, (views, cells), 1) + (block * cells - blocks * cells // 2)
    return tiled(slopes.astype(F32), cells) * (cell.astype(F32) * (1.0 / cells)) - lowest


def hat(offset, level):
    return jnp.maximum(1.0 - jnp.abs(offset - level), 0.0)


def in_vmem(value):
    if interpreted():
        return value
    return pltpu.with_memory_space_constraint(value, VMEM)


def in_hbm(value):
    if interpreted():
        return value
    return pltpu.with_memory_space_constraint(value, pltpu.HBM)


def out_vmem(shape, dtype):
    if interpreted():
        return jax.ShapeDtypeStruct(shape, dtype)
    return VMEM(shape, dtype)


def anywhere():
    return pl.BlockSpec(memory_space=pltpu.HBM)


def vmem():
    return pl.BlockSpec(memory_space=VMEM)


def in_roles(value, odd):
    edge = value.shape[1] // 3
    lead, mid, trail = value[:, :edge], value[:, edge : 2 * edge], value[:, 2 * edge :]
    return jnp.concatenate([jnp.where(odd, lead, trail), mid, jnp.where(odd, trail, lead)], axis=1)


def from_roles(value, odd):
    edge = value.shape[1] // 3
    a, mid, b = value[:, :edge], value[:, edge : 2 * edge], value[:, 2 * edge :]
    return jnp.concatenate([jnp.where(odd, a, b), mid, jnp.where(odd, b, a)], axis=1)


def on_grid(value):
    return jnp.round(value * 32768.0) * (1.0 / 32768.0)


def project(table_ref, volume_ref, rows_ref, slopes, out_ref, plane, family, block, blocks, odd, pad, scale):
    views = slopes.shape[0]
    bins = volume_ref.shape[2 - family]
    width = out_ref.shape[1]
    first = (block == 0).astype(F32)
    amounts = pad - LEVELS + 1 - lowest_shift(slopes, block, blocks)
    count = width // 128
    data = bins // 128
    dims = (((1,), (family,)), ((), ()))
    summands = lax.dot_general(table_ref[...], volume_ref[plane], dims, preferred_element_type=F32)
    total = [None] * count
    for level in range(LEVELS):
        piece = tiles_of(summands[level * views : (level + 1) * views, :]) + [None] * (count - data)
        piece = shifted(piece, LEVELS - 1 - level, count)
        total = [p if t is None else t if p is None else t + p for t, p in zip(total, piece)]
    total = jnp.concatenate(barrel(total, amounts), axis=1) * scale
    known = tiles_of(rows_ref[plane * views : (plane + 1) * views, :] * first) + [None] * (count - data)
    known = [None] * (pad // 128) + shifted(known, pad % 128, count - pad // 128)
    known = jnp.concatenate([jnp.zeros((views, 128), F32) if k is None else k for k in known], axis=1)
    total = on_grid(total - known)
    out_ref[plane * views : (plane + 1) * views, :] = in_roles(total, odd)


def build_table(slopes, block, blocks, cells, table_ref):
    views = slopes.shape[0]
    offset = offsets(slopes, block, blocks, cells)
    for level in range(LEVELS):
        table_ref[level * views : (level + 1) * views, :] = hat(offset, float(level)).astype(BF16)


def gather_rows(measured_ref, rows_ref):
    views, planes, _ = measured_ref.shape
    for plane in range(planes):
        for v in range(views):
            rows_ref[plane * views + v : plane * views + v + 1, :] = measured_ref[v, plane : plane + 1, :]


def forward_kernel(
    slopes_hbm, volume_hbm, mx_hbm, my_hbm,
    x_ref, y_ref, table_y_ref, near_ref, volume_ref, column_x_ref, column_y_ref, lane_ref,
    table_x_ref, slopes_ref, mx_ref, my_ref, rows_x_ref, rows_y_ref, sems,
    *, count_x, count_y, pad_x, pad_y, scale_x, scale_y,
):
    planes, cells_x, cells_y = volume_ref.shape
    fetches = [
        pltpu.make_async_copy(slopes_hbm, slopes_ref, sems.at[0]),
        pltpu.make_async_copy(volume_hbm, volume_ref, sems.at[1]),
        pltpu.make_async_copy(mx_hbm, mx_ref, sems.at[2]),
        pltpu.make_async_copy(my_hbm, my_ref, sems.at[3]),
        pltpu.make_async_copy(volume_hbm.at[pl.ds(1 - lax.axis_index("pa"), 1)], near_ref, sems.at[4]),
    ]
    for fetch in fetches:
        fetch.start()
    here_x, here_y = lax.axis_index("gx"), lax.axis_index("gy")
    fetches[0].wait()
    column_x = fill(slopes_ref, 0, column_x_ref.shape, 0)
    column_y = fill(slopes_ref, 1, column_y_ref.shape, 0)
    column_x_ref[...] = column_x
    column_y_ref[...] = column_y
    lane_ref[...] = fill(slopes_ref, 0, lane_ref.shape, 1)
    build_table(column_y, here_y, count_y, cells_y, table_y_ref)
    build_table(column_x, here_x, count_x, cells_x, table_x_ref)
    fetches[2].wait()
    fetches[3].wait()
    gather_rows(mx_ref, rows_x_ref)
    gather_rows(my_ref, rows_y_ref)
    fetches[1].wait()
    for plane in range(planes):
        project(
            table_y_ref, volume_ref, rows_y_ref, column_y, y_ref, plane, 1, here_y, count_y, here_x % 2 == 1, pad_y, scale_y
        )
    for plane in range(planes):
        project(
            table_x_ref, volume_ref, rows_x_ref, column_x, x_ref, plane, 0, here_x, count_x, here_y % 2 == 1, pad_x, scale_x
        )
    fetches[4].wait()


def forward(slopes, volume, measured_x, measured_y, count_x, count_y, pad_x, pad_y, scale_x, scale_y):
    views = slopes.shape[1]
    planes, cells_x, cells_y = volume.shape

    def body(*refs):
        forward_kernel(
            *refs, count_x=count_x, count_y=count_y, pad_x=pad_x, pad_y=pad_y, scale_x=scale_x, scale_y=scale_y
        )

    return pl.pallas_call(
        body,
        out_shape=(
            out_vmem((planes * views, cells_y + 2 * pad_x), F32),
            out_vmem((planes * views, cells_x + 2 * pad_y), F32),
            out_vmem((LEVELS * views, cells_y), BF16),
            out_vmem((1,) + volume.shape[1:], BF16),
            out_vmem(volume.shape, BF16),
            out_vmem((views, 128), jnp.int32),
            out_vmem((views, 128), jnp.int32),
            out_vmem((8, LEVELS * views), jnp.int32),
        ),
        in_specs=[anywhere()] * 4,
        out_specs=(vmem(),) * 8,
        scratch_shapes=[
            VMEM((LEVELS * views, cells_x), BF16),
            SMEM(slopes.shape, jnp.int32),
            VMEM(measured_x.shape, F32),
            VMEM(measured_y.shape, F32),
            VMEM((planes * views, cells_y), F32),
            VMEM((planes * views, cells_x), F32),
            pltpu.SemaphoreType.DMA((5,)),
        ],
        compiler_params=LIMIT,
        interpret=interpreted(),
        name="forward",
    )(*(in_hbm(value) for value in (slopes, volume, measured_x, measured_y)))


def half_of(index):
    return ((index + 1) // 2) % 2


def spread_into(value, slopes, block, blocks, other, others, pad, scale, spread_ref):
    views, width = value.shape
    bins = width - 2 * pad
    place = lax.broadcasted_iota(jnp.int32, (views, width), 1)
    inside = (place >= jnp.where(other == 0, pad, 0)) & (place < jnp.where(other == others - 1, pad + bins, width))
    value = jnp.where(inside, value * scale, 0.0).astype(BF16).astype(F32)
    tiles = barrel(tiles_of(value), lowest_shift(slopes, block, blocks) + pad)
    skip = 2 * pad // 128
    tiles = tiles[skip:] + tiles[:skip]
    for level in range(LEVELS):
        piece = jnp.concatenate(shifted(tiles, level, bins // 128), axis=1)
        spread_ref[level * views : (level + 1) * views, :] = piece.astype(BF16)


def middle(value, pad):
    tiles = tiles_of(value)
    skip = pad // 128
    tiles = tiles[skip:] + tiles[:skip]
    count = (value.shape[1] - 2 * pad) // 128
    if pad % 128 == 0:
        return jnp.concatenate(tiles[:count], axis=1)
    tiles = tiles[1:] + tiles[:1]
    return jnp.concatenate(shifted(tiles, 128 - pad % 128, count), axis=1)


def prepare_kernel(lane_ref, volume_ref, beside_ref, table_ref, base_ref, *, blocks):
    planes, cells, _ = volume_ref.shape
    block, band = lax.axis_index("gx"), lax.axis_index("pa")
    slopes = lane_ref[...]
    views = slopes.shape[1] // LEVELS
    level = lax.broadcasted_iota(jnp.int32, slopes.shape, 1) // views
    base = (lowest_shift(slopes, block, blocks) + level).astype(F32)[:1]
    slopes = slopes.astype(F32)[:1]
    shape = (cells, LEVELS * views)
    cell = lax.broadcasted_iota(jnp.int32, shape, 0).astype(F32) * (1.0 / cells) + (block - blocks // 2).astype(F32)
    table_ref[...] = jnp.maximum(1.0 - jnp.abs(cell * slopes - base), 0.0).astype(BF16)
    for plane in range(planes):
        here = volume_ref[plane].astype(F32)
        beside = beside_ref[0].astype(F32) * (band == 1 - plane).astype(F32)
        within = volume_ref[1 - plane].astype(F32)
        base_ref[plane] = 0.02 * (2.0 * here - beside - within)


def prepare(lane, volume, beside, blocks):
    def body(*refs):
        prepare_kernel(*refs, blocks=blocks)

    return pl.pallas_call(
        body,
        out_shape=(out_vmem((volume.shape[1], lane.shape[1]), BF16), out_vmem(volume.shape, F32)),
        in_specs=[vmem()] * 3,
        out_specs=(vmem(), vmem()),
        compiler_params=LIMIT,
        interpret=interpreted(),
        name="prepare",
    )(*(in_vmem(value) for value in (lane, volume, beside)))


def store_rows(values, rest_ref, rows_ref):
    planes, views = len(values), rest_ref.shape[0]
    for plane in range(planes):
        rows_ref[plane * views : (plane + 1) * views, :] = values[plane]
    for plane in range(planes):
        for v in range(views):
            rest_ref[v, plane : plane + 1, :] = rows_ref[plane * views + v : plane * views + v + 1, :]


def back_own_kernel(column_ref, table_ref, half_ref, out_ref, spread_ref, *, blocks, others, pad, scale):
    block, other = lax.axis_index("gy"), lax.axis_index("gx")
    value = from_roles(half_ref[...], other % 2 == 1)
    spread_into(value, column_ref[...], block, blocks, other, others, pad, scale, spread_ref)
    dims = (((0,), (0,)), ((), ()))
    out_ref[...] = lax.dot_general(spread_ref[...], table_ref[...], dims, preferred_element_type=F32)


def back_own(column, table, half, bins, blocks, others, pad, scale):
    def body(*refs):
        back_own_kernel(*refs, blocks=blocks, others=others, pad=pad, scale=scale)

    return pl.pallas_call(
        body,
        out_shape=out_vmem((bins, table.shape[1]), F32),
        in_specs=[vmem()] * 3,
        out_specs=vmem(),
        scratch_shapes=[VMEM((table.shape[0], bins), BF16)],
        compiler_params=LIMIT,
        interpret=interpreted(),
        name="back_own",
    )(*(in_vmem(value) for value in (column, table, half)))


def back_x_kernel(
    column_ref, table_ref, base_ref, half_ref, away_ref, own_ref, out_hbm, rest_hbm, partial_ref,
    spread_ref, sum_ref, rows_ref, rest_ref, sems, *, blocks, others, pad, scale,
):
    planes, cells, _ = base_ref.shape
    block, other = lax.axis_index("gx"), lax.axis_index("gy")
    column = column_ref[...]
    flip = other % 2 == 1
    mine = half_of(other)
    held = block % 2
    size = cells // CHUNKS
    copies = []

    def residual_of(plane):
        return from_roles(jnp.where(plane == held, half_ref[...], away_ref[...]), flip)

    for last in range(planes):
        plane = 1 - mine if last else mine
        spread_into(residual_of(plane), column, block, blocks, other, others, pad, scale, spread_ref)
        for c in range(CHUNKS):
            part = pl.ds(c * size, size)
            value = jnp.dot(table_ref[part, :], spread_ref[...], preferred_element_type=F32)
            value = base_ref[pl.ds(plane, 1), part, :] + value[None]
            if last:
                partial_ref[part, :] = value[0]
            else:
                sum_ref[:, part, :] = value + own_ref[part, :][None]
                copies.append(
                    pltpu.make_async_copy(sum_ref.at[:, part], out_hbm.at[pl.ds(plane, 1), part], sems.at[1 + c])
                )
                copies[-1].start()
    store_rows([middle(residual_of(p), pad) for p in range(planes)], rest_ref, rows_ref)
    copies.append(pltpu.make_async_copy(rest_ref, rest_hbm, sems.at[0]))
    copies[-1].start()
    for copy in copies:
        copy.wait()


def back_x(column, table, base, half, away, own, blocks, others, pad, scale):
    planes, cells, bins = base.shape
    views = column.shape[0]

    def body(*refs):
        back_x_kernel(*refs, blocks=blocks, others=others, pad=pad, scale=scale)

    return pl.pallas_call(
        body,
        out_shape=(
            jax.ShapeDtypeStruct(base.shape, F32),
            jax.ShapeDtypeStruct((views, planes, bins), F32),
            out_vmem((cells, bins), F32),
        ),
        in_specs=[vmem()] * 6,
        out_specs=(anywhere(), anywhere(), vmem()),
        scratch_shapes=[
            VMEM((LEVELS * views, bins), BF16),
            VMEM((1, cells, bins), F32),
            VMEM((planes * views, bins), F32),
            VMEM((views, planes, bins), F32),
            pltpu.SemaphoreType.DMA((1 + CHUNKS,)),
        ],
        compiler_params=LIMIT,
        interpret=interpreted(),
        name="back_x",
    )(*(in_vmem(value) for value in (column, table, base, half, away, own)))


def back_last_kernel(
    column_ref, table_ref, partial_ref, half_ref, other_ref, gradient_hbm, out_hbm, rest_hbm,
    spread_ref, sum_ref, rows_ref, rest_ref, sems, *, blocks, others, pad, scale,
):
    bins, _ = partial_ref.shape
    block, other = lax.axis_index("gy"), lax.axis_index("gx")
    flip = other % 2 == 1
    mine = half_of(block)
    value = from_roles(other_ref[...], flip)
    spread_into(value, column_ref[...], block, blocks, other, others, pad, scale, spread_ref)
    dims = (((0,), (0,)), ((), ()))
    size = bins // PIECES
    copies = []
    for c in range(PIECES):
        part = pl.ds(c * size, size)
        back = lax.dot_general(spread_ref[:, c * size : (c + 1) * size], table_ref[...], dims, preferred_element_type=F32)
        sum_ref[:, part, :] = (partial_ref[part, :] + back)[None]
        copies.append(pltpu.make_async_copy(sum_ref.at[:, part], out_hbm.at[pl.ds(1 - mine, 1), part], sems.at[1 + c]))
        copies[-1].start()
    odd = mine == 1
    low = from_roles(jnp.where(odd, other_ref[...], half_ref[...]), flip)
    high = from_roles(jnp.where(odd, half_ref[...], other_ref[...]), flip)
    store_rows([middle(low, pad), middle(high, pad)], rest_ref, rows_ref)
    copies.append(pltpu.make_async_copy(rest_ref, rest_hbm, sems.at[0]))
    copies[-1].start()
    for copy in copies:
        copy.wait()


def back_last(column, table, partial, half, other, gradient, blocks, others, pad, scale):
    bins, cells = partial.shape
    planes = gradient.shape[0]
    views = column.shape[0]

    def body(*refs):
        back_last_kernel(*refs, blocks=blocks, others=others, pad=pad, scale=scale)

    return pl.pallas_call(
        body,
        out_shape=(
            jax.ShapeDtypeStruct(gradient.shape, F32),
            jax.ShapeDtypeStruct((views, planes, bins), F32),
        ),
        in_specs=[vmem()] * 5 + [anywhere()],
        out_specs=(anywhere(), anywhere()),
        scratch_shapes=[
            VMEM((LEVELS * views, bins), BF16),
            VMEM((1, bins, cells), F32),
            VMEM((planes * views, bins), F32),
            VMEM((views, planes, bins), F32),
            pltpu.SemaphoreType.DMA((1 + PIECES,)),
        ],
        input_output_aliases={5: 0},
        compiler_params=LIMIT,
        interpret=interpreted(),
        name="back_last",
    )(*(in_vmem(value) for value in (column, table, partial, half, other)), gradient)


def exchange(value, axis, partner):
    size = lax.axis_size(axis)
    pairs = [(i, partner(i)) for i in range(size) if partner(i) != i and 0 <= partner(i) < size]
    return lax.ppermute(value, axis, pairs)


def twin(i):
    return i ^ 1


def odd_twin(i):
    return i - i % RING + (i + (1 if i % 2 else -1)) % RING


def next_twin(i):
    return odd_twin(i) if abs(odd_twin(i) - i) == 1 else i


def across(i):
    return i - i % RING + (i + (-3 if i % 2 else 3)) % RING


def border(i):
    return i + (1 if i % 2 else -1)


def steps(volume, view_slopes, measured_x, measured_y):
    _, cells_x, cells_y = volume.shape
    count_x = lax.axis_size("gx")
    count_y = lax.axis_size("gy")
    scale_x = float(cells_x * count_x) ** (-0.5)
    scale_y = float(cells_y * count_y) ** (-0.5)
    pad_x, pad_y = 64, 128

    sum_x, sum_y, table_y, near, volume, column_x, column_y, lane = forward(
        view_slopes, volume, measured_x, measured_y, count_x, count_y, pad_x, pad_y, scale_x, scale_y
    )
    wide, long = sum_x.shape[1], sum_y.shape[1]
    edge_x, edge_y = wide // 3, long // 3
    rows = sum_x.shape[0] // 2

    def side_by_side(value):
        return jnp.concatenate([value[:rows], value[rows:]], axis=1)

    def one_above(value):
        return jnp.concatenate([value[:, : value.shape[1] // 2], value[:, value.shape[1] // 2 :]], axis=0)

    def split(value, held):
        owns = held == 0
        low, high = value[:rows], value[rows:]
        return jnp.where(owns, low, high), jnp.where(owns, high, low)

    y_a, y_mid, y_b = sum_y[:, :edge_y], sum_y[:, edge_y : 2 * edge_y], sum_y[:, 2 * edge_y :]
    half_x, sent = split(sum_x, lax.axis_index("gx") % 2)
    got = exchange(jnp.concatenate([sent, side_by_side(y_a)], axis=1), "gx", twin)
    got_b = exchange(y_b, "gx", next_twin)
    beside = lax.ppermute(near, "pa", [(0, 1), (1, 0)])
    half_x, y_a = half_x + got[:, :wide], y_a + one_above(got[:, wide:])
    y_b = y_b + got_b
    sum_y = jnp.concatenate([y_a, y_mid, y_b], axis=1)
    half, sent = split(sum_y, half_of(lax.axis_index("gy")))
    got_y = exchange(sent, "gy", twin)
    got_x = exchange(half_x, "gx", lambda i: i ^ 2)
    half = half + got_y
    half_x, half = lax.optimization_barrier((half_x, half))
    half_x = half_x + got_x
    got_y = exchange(half, "gy", lambda i: i ^ RING)
    got_x = exchange(half_x, "gx", lambda i: i ^ 6)
    half = half + got_y
    got_y = exchange(half, "gy", odd_twin)
    half = half + got_y
    half_x, half = lax.optimization_barrier((half_x, half))
    half_x = half_x + got_x
    x_a, x_mid, x_b = half_x[:, :edge_x], half_x[:, edge_x : 2 * edge_x], half_x[:, 2 * edge_x :]
    got_y = exchange(half, "gy", across)
    got_a = exchange(x_a, "gy", twin)
    got_b = exchange(x_b, "gy", border)
    half = half + got_y
    other = exchange(half, "gy", twin)
    x_a, x_b, half = lax.optimization_barrier((x_a, x_b, half))
    x_b = x_b + got_b
    half_x = jnp.concatenate([x_a + got_a, x_mid, x_b], axis=1)
    away_x = exchange(half_x, "gx", twin)

    table_x, base = prepare(lane, volume, beside, count_x)
    own = back_own(column_y, table_y, half, cells_x, count_y, count_x, pad_y, scale_y)
    gradient, residual_x, partial = back_x(
        column_x, table_x, base, half_x, away_x, own, count_x, count_y, pad_x, scale_x
    )
    gradient, residual_y = back_last(
        column_y, table_y, partial, half, other, gradient, count_y, count_x, pad_y, scale_y
    )
    return (gradient, residual_x, residual_y)


def solution(mesh):
    return jax.shard_map(
        steps,
        mesh=mesh,
        in_specs=(P("pa", "gx", "gy"), P(), P(None, "pa", "gy"), P(None, "pa", "gx")),
        out_specs=(P("pa", "gx", "gy"), P(None, "pa", "gy"), P(None, "pa", "gx")),
        check_vma=False,
    )
```

```python
import jax
import jax.numpy as jnp
from jax import lax
from jax.experimental import pallas as pl
from jax.experimental.pallas import tpu as pltpu
from jax.sharding import PartitionSpec as P


LEVELS = 16
RING = 8
CHUNKS = 2
PIECES = 4
LIMIT = pltpu.CompilerParams(vmem_limit_bytes=8 * 1024 * 1024)
SMEM = pltpu.SMEM
VMEM = pltpu.VMEM
F32 = jnp.float32
BF16 = jnp.bfloat16


def interpreted():
    return False


def fill(slopes_ref, family, shape, dim):
    views = slopes_ref.shape[1]
    view = lax.broadcasted_iota(jnp.int32, shape, dim) % views
    slopes = jnp.zeros(shape, jnp.int32)
    for v in range(views):
        slopes = jnp.where(view == v, slopes_ref[family, v], slopes)
    return slopes


def tiled(value, width):
    return jnp.concatenate([value] * (width // value.shape[1]), axis=1)


def lowest_shift(slopes, block, blocks):
    return slopes * (block - blocks // 2) + jnp.minimum(slopes, 0)


def tiles_of(value):
    return [value[:, k : k + 128] for k in range(0, value.shape[1], 128)]


def shifted(tiles, amount, count):
    if amount == 0:
        return tiles[:count]
    lane = lax.broadcasted_iota(jnp.int32, tiles[0].shape, 1)
    rolled = [None if tile is None else pltpu.roll(tile, amount, 1) for tile in tiles]
    out = []
    for k in range(count):
        here, before = rolled[k], rolled[k - 1]
        if here is None and before is None:
            out.append(None)
        elif here is None:
            out.append(jnp.where(lane < amount, before, 0.0))
        elif before is None:
            out.append(jnp.where(lane < amount, 0.0, here))
        else:
            out.append(jnp.where(lane < amount, before, here))
    return out


def barrel(tiles, amounts):
    lane = lax.broadcasted_iota(jnp.int32, amounts.shape, 1)
    low = amounts & 127
    source = (lane - amounts) & 127
    zero = jnp.zeros(amounts.shape, F32)
    turned = [zero if tile is None else jnp.take_along_axis(tile, source, axis=1) for tile in tiles]
    near = [jnp.where(lane < low, turned[k - 1], turned[k]) for k in range(len(tiles))]
    return [jnp.where(amounts >= 128, near[k - 1], near[k]) for k in range(len(tiles))]


def offsets(slopes, block, blocks, cells):
    views = slopes.shape[0]
    lowest = tiled(lowest_shift(slopes, block, blocks).astype(F32), cells)
    cell = lax.broadcasted_iota(jnp.int32, (views, cells), 1) + (block * cells - blocks * cells // 2)
    return tiled(slopes.astype(F32), cells) * (cell.astype(F32) * (1.0 / cells)) - lowest


def hat(offset, level):
    return jnp.maximum(1.0 - jnp.abs(offset - level), 0.0)


def in_vmem(value):
    if interpreted():
        return value
    return pltpu.with_memory_space_constraint(value, VMEM)


def in_hbm(value):
    if interpreted():
        return value
    return pltpu.with_memory_space_constraint(value, pltpu.HBM)


def out_vmem(shape, dtype):
    if interpreted():
        return jax.ShapeDtypeStruct(shape, dtype)
    return VMEM(shape, dtype)


def anywhere():
    return pl.BlockSpec(memory_space=pltpu.HBM)


def vmem():
    return pl.BlockSpec(memory_space=VMEM)


def in_roles(value, odd):
    edge = value.shape[1] // 3
    lead, mid, trail = value[:, :edge], value[:, edge : 2 * edge], value[:, 2 * edge :]
    return jnp.concatenate([jnp.where(odd, lead, trail), mid, jnp.where(odd, trail, lead)], axis=1)


def from_roles(value, odd):
    edge = value.shape[1] // 3
    a, mid, b = value[:, :edge], value[:, edge : 2 * edge], value[:, 2 * edge :]
    return jnp.concatenate([jnp.where(odd, a, b), mid, jnp.where(odd, b, a)], axis=1)


def on_grid(value):
    return jnp.round(value * 32768.0) * (1.0 / 32768.0)


def project(table_ref, volume_ref, rows_ref, slopes, out_ref, plane, family, block, blocks, odd, pad, scale):
    views = slopes.shape[0]
    bins = volume_ref.shape[2 - family]
    width = out_ref.shape[1]
    first = (block == 0).astype(F32)
    amounts = pad - LEVELS + 1 - lowest_shift(slopes, block, blocks)
    count = width // 128
    data = bins // 128
    dims = (((1,), (family,)), ((), ()))
    summands = lax.dot_general(table_ref[...], volume_ref[plane], dims, preferred_element_type=F32)
    total = [None] * count
    for level in range(LEVELS):
        piece = tiles_of(summands[level * views : (level + 1) * views, :]) + [None] * (count - data)
        piece = shifted(piece, LEVELS - 1 - level, count)
        total = [p if t is None else t if p is None else t + p for t, p in zip(total, piece)]
    total = jnp.concatenate(barrel(total, amounts), axis=1) * scale
    known = tiles_of(rows_ref[plane * views : (plane + 1) * views, :] * first) + [None] * (count - data)
    known = [None] * (pad // 128) + shifted(known, pad % 128, count - pad // 128)
    known = jnp.concatenate([jnp.zeros((views, 128), F32) if k is None else k for k in known], axis=1)
    total = on_grid(total - known)
    out_ref[plane * views : (plane + 1) * views, :] = in_roles(total, odd)


def build_table(slopes, block, blocks, cells, table_ref):
    views = slopes.shape[0]
    offset = offsets(slopes, block, blocks, cells)
    for level in range(LEVELS):
        table_ref[level * views : (level + 1) * views, :] = hat(offset, float(level)).astype(BF16)


def gather_rows(measured_ref, rows_ref):
    views, planes, _ = measured_ref.shape
    for plane in range(planes):
        for v in range(views):
            rows_ref[plane * views + v : plane * views + v + 1, :] = measured_ref[v, plane : plane + 1, :]


def forward_kernel(
    slopes_hbm, volume_hbm, mx_hbm, my_hbm,
    x_ref, y_ref, table_y_ref, near_ref, volume_ref, column_x_ref, column_y_ref, lane_ref,
    table_x_ref, slopes_ref, mx_ref, my_ref, rows_x_ref, rows_y_ref, sems,
    *, count_x, count_y, pad_x, pad_y, scale_x, scale_y,
):
    planes, cells_x, cells_y = volume_ref.shape
    fetches = [
        pltpu.make_async_copy(slopes_hbm, slopes_ref, sems.at[0]),
        pltpu.make_async_copy(volume_hbm, volume_ref, sems.at[1]),
        pltpu.make_async_copy(mx_hbm, mx_ref, sems.at[2]),
        pltpu.make_async_copy(my_hbm, my_ref, sems.at[3]),
        pltpu.make_async_copy(volume_hbm.at[pl.ds(1 - lax.axis_index("pa"), 1)], near_ref, sems.at[4]),
    ]
    for fetch in fetches:
        fetch.start()
    here_x, here_y = lax.axis_index("gx"), lax.axis_index("gy")
    fetches[0].wait()
    column_x = fill(slopes_ref, 0, column_x_ref.shape, 0)
    column_y = fill(slopes_ref, 1, column_y_ref.shape, 0)
    column_x_ref[...] = column_x
    column_y_ref[...] = column_y
    lane_ref[...] = fill(slopes_ref, 0, lane_ref.shape, 1)
    build_table(column_y, here_y, count_y, cells_y, table_y_ref)
    build_table(column_x, here_x, count_x, cells_x, table_x_ref)
    fetches[2].wait()
    fetches[3].wait()
    gather_rows(mx_ref, rows_x_ref)
    gather_rows(my_ref, rows_y_ref)
    fetches[1].wait()
    for plane in range(planes):
        project(
            table_y_ref, volume_ref, rows_y_ref, column_y, y_ref, plane, 1, here_y, count_y, here_x % 2 == 1, pad_y, scale_y
        )
    for plane in range(planes):
        project(
            table_x_ref, volume_ref, rows_x_ref, column_x, x_ref, plane, 0, here_x, count_x, here_y % 2 == 1, pad_x, scale_x
        )
    fetches[4].wait()


def forward(slopes, volume, measured_x, measured_y, count_x, count_y, pad_x, pad_y, scale_x, scale_y):
    views = slopes.shape[1]
    planes, cells_x, cells_y = volume.shape

    def body(*refs):
        forward_kernel(
            *refs, count_x=count_x, count_y=count_y, pad_x=pad_x, pad_y=pad_y, scale_x=scale_x, scale_y=scale_y
        )

    return pl.pallas_call(
        body,
        out_shape=(
            out_vmem((planes * views, cells_y + 2 * pad_x), F32),
            out_vmem((planes * views, cells_x + 2 * pad_y), F32),
            out_vmem((LEVELS * views, cells_y), BF16),
            out_vmem((1,) + volume.shape[1:], BF16),
            out_vmem(volume.shape, BF16),
            out_vmem((views, 128), jnp.int32),
            out_vmem((views, 128), jnp.int32),
            out_vmem((8, LEVELS * views), jnp.int32),
        ),
        in_specs=[anywhere()] * 4,
        out_specs=(vmem(),) * 8,
        scratch_shapes=[
            VMEM((LEVELS * views, cells_x), BF16),
            SMEM(slopes.shape, jnp.int32),
            VMEM(measured_x.shape, F32),
            VMEM(measured_y.shape, F32),
            VMEM((planes * views, cells_y), F32),
            VMEM((planes * views, cells_x), F32),
            pltpu.SemaphoreType.DMA((5,)),
        ],
        compiler_params=LIMIT,
        interpret=interpreted(),
        name="forward",
    )(*(in_hbm(value) for value in (slopes, volume, measured_x, measured_y)))


def half_of(index):
    return ((index + 1) // 2) % 2


def spread_into(value, slopes, block, blocks, other, others, pad, scale, spread_ref):
    views, width = value.shape
    bins = width - 2 * pad
    place = lax.broadcasted_iota(jnp.int32, (views, width), 1)
    inside = (place >= jnp.where(other == 0, pad, 0)) & (place < jnp.where(other == others - 1, pad + bins, width))
    value = jnp.where(inside, value * scale, 0.0).astype(BF16).astype(F32)
    tiles = barrel(tiles_of(value), lowest_shift(slopes, block, blocks) + pad)
    skip = 2 * pad // 128
    tiles = tiles[skip:] + tiles[:skip]
    for level in range(LEVELS):
        piece = jnp.concatenate(shifted(tiles, level, bins // 128), axis=1)
        spread_ref[level * views : (level + 1) * views, :] = piece.astype(BF16)


def middle(value, pad):
    tiles = tiles_of(value)
    skip = pad // 128
    tiles = tiles[skip:] + tiles[:skip]
    count = (value.shape[1] - 2 * pad) // 128
    if pad % 128 == 0:
        return jnp.concatenate(tiles[:count], axis=1)
    tiles = tiles[1:] + tiles[:1]
    return jnp.concatenate(shifted(tiles, 128 - pad % 128, count), axis=1)


def prepare_kernel(lane_ref, volume_ref, beside_ref, table_ref, base_ref, *, blocks):
    planes, cells, _ = volume_ref.shape
    block, band = lax.axis_index("gx"), lax.axis_index("pa")
    slopes = lane_ref[...]
    views = slopes.shape[1] // LEVELS
    level = lax.broadcasted_iota(jnp.int32, slopes.shape, 1) // views
    base = (lowest_shift(slopes, block, blocks) + level).astype(F32)[:1]
    slopes = slopes.astype(F32)[:1]
    shape = (cells, LEVELS * views)
    cell = lax.broadcasted_iota(jnp.int32, shape, 0).astype(F32) * (1.0 / cells) + (block - blocks // 2).astype(F32)
    table_ref[...] = jnp.maximum(1.0 - jnp.abs(cell * slopes - base), 0.0).astype(BF16)
    for plane in range(planes):
        here = volume_ref[plane].astype(F32)
        beside = beside_ref[0].astype(F32) * (band == 1 - plane).astype(F32)
        within = volume_ref[1 - plane].astype(F32)
        base_ref[plane] = 0.02 * (2.0 * here - beside - within)


def prepare(lane, volume, beside, blocks):
    def body(*refs):
        prepare_kernel(*refs, blocks=blocks)

    return pl.pallas_call(
        body,
        out_shape=(out_vmem((volume.shape[1], lane.shape[1]), BF16), out_vmem(volume.shape, F32)),
        in_specs=[vmem()] * 3,
        out_specs=(vmem(), vmem()),
        compiler_params=LIMIT,
        interpret=interpreted(),
        name="prepare",
    )(*(in_vmem(value) for value in (lane, volume, beside)))


def store_rows(values, rest_ref, rows_ref):
    planes, views = len(values), rest_ref.shape[0]
    for plane in range(planes):
        rows_ref[plane * views : (plane + 1) * views, :] = values[plane]
    for plane in range(planes):
        for v in range(views):
            rest_ref[v, plane : plane + 1, :] = rows_ref[plane * views + v : plane * views + v + 1, :]


def back_own_kernel(column_ref, table_ref, half_ref, out_ref, spread_ref, *, blocks, others, pad, scale):
    block, other = lax.axis_index("gy"), lax.axis_index("gx")
    value = from_roles(half_ref[...], other % 2 == 1)
    spread_into(value, column_ref[...], block, blocks, other, others, pad, scale, spread_ref)
    dims = (((0,), (0,)), ((), ()))
    out_ref[...] = lax.dot_general(spread_ref[...], table_ref[...], dims, preferred_element_type=F32)


def back_own(column, table, half, bins, blocks, others, pad, scale):
    def body(*refs):
        back_own_kernel(*refs, blocks=blocks, others=others, pad=pad, scale=scale)

    return pl.pallas_call(
        body,
        out_shape=out_vmem((bins, table.shape[1]), F32),
        in_specs=[vmem()] * 3,
        out_specs=vmem(),
        scratch_shapes=[VMEM((table.shape[0], bins), BF16)],
        compiler_params=LIMIT,
        interpret=interpreted(),
        name="back_own",
    )(*(in_vmem(value) for value in (column, table, half)))


def back_x_kernel(
    column_ref, table_ref, base_ref, half_ref, away_ref, own_ref, out_hbm, rest_hbm, partial_ref,
    spread_ref, sum_ref, rows_ref, rest_ref, sems, *, blocks, others, pad, scale,
):
    planes, cells, _ = base_ref.shape
    block, other = lax.axis_index("gx"), lax.axis_index("gy")
    column = column_ref[...]
    flip = other % 2 == 1
    mine = half_of(other)
    held = half_of(block)
    size = cells // CHUNKS
    copies = []

    def residual_of(plane):
        return from_roles(jnp.where(plane == held, half_ref[...], away_ref[...]), flip)

    for last in range(planes):
        plane = 1 - mine if last else mine
        spread_into(residual_of(plane), column, block, blocks, other, others, pad, scale, spread_ref)
        for c in range(CHUNKS):
            part = pl.ds(c * size, size)
            value = jnp.dot(table_ref[part, :], spread_ref[...], preferred_element_type=F32)
            value = base_ref[pl.ds(plane, 1), part, :] + value[None]
            if last:
                partial_ref[part, :] = value[0]
            else:
                sum_ref[:, part, :] = value + own_ref[part, :][None]
                copies.append(
                    pltpu.make_async_copy(sum_ref.at[:, part], out_hbm.at[pl.ds(plane, 1), part], sems.at[1 + c])
                )
                copies[-1].start()
    store_rows([middle(residual_of(p), pad) for p in range(planes)], rest_ref, rows_ref)
    copies.append(pltpu.make_async_copy(rest_ref, rest_hbm, sems.at[0]))
    copies[-1].start()
    for copy in copies:
        copy.wait()


def back_x(column, table, base, half, away, own, blocks, others, pad, scale):
    planes, cells, bins = base.shape
    views = column.shape[0]

    def body(*refs):
        back_x_kernel(*refs, blocks=blocks, others=others, pad=pad, scale=scale)

    return pl.pallas_call(
        body,
        out_shape=(
            jax.ShapeDtypeStruct(base.shape, F32),
            jax.ShapeDtypeStruct((views, planes, bins), F32),
            out_vmem((cells, bins), F32),
        ),
        in_specs=[vmem()] * 6,
        out_specs=(anywhere(), anywhere(), vmem()),
        scratch_shapes=[
            VMEM((LEVELS * views, bins), BF16),
            VMEM((1, cells, bins), F32),
            VMEM((planes * views, bins), F32),
            VMEM((views, planes, bins), F32),
            pltpu.SemaphoreType.DMA((1 + CHUNKS,)),
        ],
        compiler_params=LIMIT,
        interpret=interpreted(),
        name="back_x",
    )(*(in_vmem(value) for value in (column, table, base, half, away, own)))


def back_last_kernel(
    column_ref, table_ref, partial_ref, half_ref, other_ref, gradient_hbm, out_hbm, rest_hbm,
    spread_ref, sum_ref, rows_ref, rest_ref, sems, *, blocks, others, pad, scale,
):
    bins, _ = partial_ref.shape
    block, other = lax.axis_index("gy"), lax.axis_index("gx")
    flip = other % 2 == 1
    mine = half_of(block)
    value = from_roles(other_ref[...], flip)
    spread_into(value, column_ref[...], block, blocks, other, others, pad, scale, spread_ref)
    dims = (((0,), (0,)), ((), ()))
    size = bins // PIECES
    copies = []
    for c in range(PIECES):
        part = pl.ds(c * size, size)
        back = lax.dot_general(spread_ref[:, c * size : (c + 1) * size], table_ref[...], dims, preferred_element_type=F32)
        sum_ref[:, part, :] = (partial_ref[part, :] + back)[None]
        copies.append(pltpu.make_async_copy(sum_ref.at[:, part], out_hbm.at[pl.ds(1 - mine, 1), part], sems.at[1 + c]))
        copies[-1].start()
    odd = mine == 1
    low = from_roles(jnp.where(odd, other_ref[...], half_ref[...]), flip)
    high = from_roles(jnp.where(odd, half_ref[...], other_ref[...]), flip)
    store_rows([middle(low, pad), middle(high, pad)], rest_ref, rows_ref)
    copies.append(pltpu.make_async_copy(rest_ref, rest_hbm, sems.at[0]))
    copies[-1].start()
    for copy in copies:
        copy.wait()


def back_last(column, table, partial, half, other, gradient, blocks, others, pad, scale):
    bins, cells = partial.shape
    planes = gradient.shape[0]
    views = column.shape[0]

    def body(*refs):
        back_last_kernel(*refs, blocks=blocks, others=others, pad=pad, scale=scale)

    return pl.pallas_call(
        body,
        out_shape=(
            jax.ShapeDtypeStruct(gradient.shape, F32),
            jax.ShapeDtypeStruct((views, planes, bins), F32),
        ),
        in_specs=[vmem()] * 5 + [anywhere()],
        out_specs=(anywhere(), anywhere()),
        scratch_shapes=[
            VMEM((LEVELS * views, bins), BF16),
            VMEM((1, bins, cells), F32),
            VMEM((planes * views, bins), F32),
            VMEM((views, planes, bins), F32),
            pltpu.SemaphoreType.DMA((1 + PIECES,)),
        ],
        input_output_aliases={5: 0},
        compiler_params=LIMIT,
        interpret=interpreted(),
        name="back_last",
    )(*(in_vmem(value) for value in (column, table, partial, half, other)), gradient)


def exchange(value, axis, partner):
    return lax.ppermute(value, axis, [(i, partner(i)) for i in range(lax.axis_size(axis)) if partner(i) != i])


def twin(i):
    return i ^ 1


def odd_twin(i):
    return i - i % RING + (i + (1 if i % 2 else -1)) % RING


def next_twin(i):
    return odd_twin(i) if abs(odd_twin(i) - i) == 1 else i


def across(i):
    return i - i % RING + (i + (-3 if i % 2 else 3)) % RING


def at_end(size, axis):
    index = lax.axis_index(axis) % size
    return (index == 0) | (index == size - 1)


def steps(volume, view_slopes, measured_x, measured_y):
    _, cells_x, cells_y = volume.shape
    count_x = lax.axis_size("gx")
    count_y = lax.axis_size("gy")
    scale_x = float(cells_x * count_x) ** (-0.5)
    scale_y = float(cells_y * count_y) ** (-0.5)
    pad_x, pad_y = 64, 128

    sum_x, sum_y, table_y, near, volume, column_x, column_y, lane = forward(
        view_slopes, volume, measured_x, measured_y, count_x, count_y, pad_x, pad_y, scale_x, scale_y
    )
    wide, long = sum_x.shape[1], sum_y.shape[1]
    edge_x, edge_y = wide // 3, long // 3
    rows = sum_x.shape[0] // 2

    def side_by_side(value):
        return jnp.concatenate([value[:rows], value[rows:]], axis=1)

    def one_above(value):
        return jnp.concatenate([value[:, : value.shape[1] // 2], value[:, value.shape[1] // 2 :]], axis=0)

    def split(value, axis):
        owns = half_of(lax.axis_index(axis)) == 0
        low, high = value[:rows], value[rows:]
        return jnp.where(owns, low, high), jnp.where(owns, high, low)

    y_a, y_mid, y_b = sum_y[:, :edge_y], sum_y[:, edge_y : 2 * edge_y], sum_y[:, 2 * edge_y :]
    half_x, sent = split(sum_x, "gx")
    got = exchange(jnp.concatenate([sent, side_by_side(y_a)], axis=1), "gx", twin)
    got_b = exchange(y_b, "gx", next_twin)
    beside = lax.ppermute(near, "pa", [(0, 1), (1, 0)])
    half_x, y_a = half_x + got[:, :wide], y_a + one_above(got[:, wide:])
    half_x = half_x + exchange(half_x, "gx", odd_twin)
    y_b = y_b + got_b
    sum_y = jnp.concatenate([y_a, y_mid, y_b], axis=1)
    x_a, x_mid, x_b = half_x[:, :edge_x], half_x[:, edge_x : 2 * edge_x], half_x[:, 2 * edge_x :]

    half, sent = split(sum_y, "gy")
    got = exchange(jnp.concatenate([sent, x_a], axis=1), "gy", twin)
    half, x_a = half + got[:, :long], x_a + got[:, long:]
    got = exchange(jnp.concatenate([half, x_b], axis=1), "gy", lambda i: i ^ RING)
    half = half + got[:, :long]
    sent_b = jnp.where(at_end(RING, "gy"), got[:, long:], x_b)
    got = exchange(jnp.concatenate([half, sent_b], axis=1), "gy", odd_twin)
    half = half + got[:, :long]
    got = jnp.where(at_end(count_y, "gy"), 0.0, got[:, long:])
    half, x_b, got = lax.optimization_barrier((half, x_b, got))
    half_x = jnp.concatenate([x_a, x_mid, x_b + got], axis=1)

    half = half + exchange(half, "gy", across)
    got = exchange(half_x, "gx", across)
    other = exchange(half, "gy", twin)
    half_x, half = lax.optimization_barrier((half_x, half))
    half_x = half_x + got
    away_x = exchange(half_x, "gx", twin)

    table_x, base = prepare(lane, volume, beside, count_x)
    own = back_own(column_y, table_y, half, cells_x, count_y, count_x, pad_y, scale_y)
    gradient, residual_x, partial = back_x(
        column_x, table_x, base, half_x, away_x, own, count_x, count_y, pad_x, scale_x
    )
    gradient, residual_y = back_last(
        column_y, table_y, partial, half, other, gradient, count_y, count_x, pad_y, scale_y
    )
    return (gradient, residual_x, residual_y)


def solution(mesh):
    return jax.shard_map(
        steps,
        mesh=mesh,
        in_specs=(P("pa", "gx", "gy"), P(), P(None, "pa", "gy"), P(None, "pa", "gx")),
        out_specs=(P("pa", "gx", "gy"), P(None, "pa", "gy"), P(None, "pa", "gx")),
        check_vma=False,
    )
```
